32 devices in a mesh: row: 4 (over y, x), col: 8 (over z, core).
Axes of the slice: x: 2, y: 2, z: 4, core: 2. Of those that a mesh axis runs over, the one named last changes fastest.
Arguments:
- pixels: float32 [3, 192, 256], P(None, 'row', 'col'), may hold values from -6 to 6
- stem_weight: bfloat16 [64, 3, 4, 4], replicated, may hold values from -0.875 to 0.875
- first_weight: bfloat16 [64, 64, 3, 3], replicated, may hold values from -0.25 to 0.25
- second_weight: bfloat16 [64, 64, 3, 3], replicated, may hold values from -0.25 to 0.25
- entry_weight: bfloat16 [256, 64, 3, 3], P('col'), may hold values from -0.25 to 0.25
- final_weight: bfloat16 [256, 256, 3, 3], P('col'), may hold values from -0.125 to 0.125
- upstream: bfloat16 [256, 96, 128], P('col', 'row'), may hold values from -6 to 6
Outputs:
- stem_grad: float32 [64, 3, 4, 4], replicated
- first_grad: float32 [64, 64, 3, 3], replicated
- second_grad: float32 [64, 64, 3, 3], replicated
- entry_grad: float32 [256, 64, 3, 3], P('col')
- final_grad: float32 [256, 256, 3, 3], P('col')
The draws below stay inside these ranges and needn't reach their ends.
All inputs are finite; a program needn't handle non-finite values.
Results may differ from the reference program's by a relative error of at most 0.023.
Values may be sent and summed in bfloat16 or wider, within the bound.
A program may use at most 64 MiB of HBM per device.

```python
import math
import jax
import jax.numpy as jnp
from jax import lax

C_IN = 3
F = 64
G = 256
HH = 96
WW = 128
H = 192
W = 256
G_DEV = 32
N_COL = 8


def block_levels(key, dims, pieces, low, high):
    def one(axis_at, shards_of):
        draws = jax.random.uniform(jax.random.fold_in(jax.random.fold_in(key, 6), axis_at), (shards_of,), jnp.float32, low / len(pieces), high / len(pieces))
        return jnp.repeat(jnp.exp(draws), dims[axis_at] // shards_of).reshape((-1,) + (1,) * (len(dims) - axis_at - 1))

    level = one(*pieces[0])
    for cut in pieces[1:]:
        level = level * one(*cut)
    return level


def scatter_about(own_key, extent, scale, reach, shards=(), kind=jnp.bfloat16):
    array = scale * jax.random.normal(own_key, extent, jnp.float32)
    if shards:
        array = array * block_levels(own_key, extent, shards, -0.22, 0.18)
    return jnp.clip(array, -reach, reach).astype(kind)


def setup_inputs(seed: int = 0) -> dict:
    streams_of = jax.random.split(jax.random.key(seed), 8)
    return {
        "pixels": scatter_about(streams_of[0], (C_IN, H, W), 1.0, 6.0, ((1, 4), (2, 8)), jnp.float32),
        "stem_weight": scatter_about(streams_of[1], (F, C_IN, 4, 4), (C_IN * 16) ** -0.5, 0.875),
        "first_weight": scatter_about(streams_of[2], (F, F, 3, 3), (F * 9) ** -0.5, 0.25),
        "second_weight": scatter_about(streams_of[3], (F, F, 3, 3), (F * 9) ** -0.5, 0.25),
        "entry_weight": scatter_about(streams_of[4], (G, F, 3, 3), (F * 9) ** -0.5, 0.25, ((0, 8),)),
        "final_weight": scatter_about(streams_of[5], (G, G, 3, 3), (G * 9) ** -0.5, 0.125, ((0, 8),)),
        "upstream": scatter_about(streams_of[6], (G, HH, WW), 1.0, 6.0, ((0, 8), (1, 4))),
    }


def conv_valid(field, kernel, stride):
    return lax.conv_general_dilated(field[None], kernel, (stride, stride), 'VALID', dimension_numbers=('NCHW', 'OIHW', 'NCHW'), preferred_element_type=jnp.float32)[0]

def weight_grad(padded, upstream, stride):
    result = lax.conv_general_dilated(padded[:, None], upstream[:, None], (1, 1), 'VALID', rhs_dilation=(stride, stride), dimension_numbers=('NCHW', 'OIHW', 'NCHW'), preferred_element_type=jnp.float32)
    return result.transpose(1, 0, 2, 3)

def back_kernel(kernel):
    return jnp.flip(kernel, (2, 3)).transpose(1, 0, 2, 3)

def silu_slope(values):
    logistic = jax.nn.sigmoid(values)
    return logistic * (1.0 + values * (1.0 - logistic))

def border(field):
    return jnp.pad(field, ((0, 0), (1, 1), (1, 1)))

def reference(pixels, stem_weight, first_weight, second_weight, entry_weight, final_weight, upstream):
    norm_scale = 1.0 / math.sqrt(HH * WW)
    inputs = pixels.astype(jnp.bfloat16)
    padded_in = border(inputs)
    stem_pre = conv_valid(padded_in, stem_weight, 2)
    stem_act = border(jax.nn.silu(stem_pre).astype(jnp.bfloat16))
    first_pre = conv_valid(stem_act, first_weight, 1)
    first_act = border(jax.nn.silu(first_pre).astype(jnp.bfloat16))
    second_pre = conv_valid(first_act, second_weight, 1)
    second_act = border(jax.nn.silu(second_pre).astype(jnp.bfloat16))
    entry_pre = conv_valid(second_act, entry_weight, 1)
    entry_act = border(jax.nn.silu(entry_pre).astype(jnp.bfloat16))
    final_grad = weight_grad(entry_act, upstream, 1)
    groups_kernel = final_weight.reshape(N_COL, G_DEV, G, 3, 3)
    groups_up = border(upstream).reshape(N_COL, G_DEV, HH + 2, WW + 2)

    def add_group(running, member):
        partial_value = conv_valid(member[1], back_kernel(member[0]), 1).astype(jnp.bfloat16)
        partial_value = lax.optimization_barrier(partial_value)
        return (running + partial_value.astype(jnp.float32), None)
    entry_back, ignored = lax.scan(add_group, jnp.zeros((G, HH, WW), jnp.float32), (groups_kernel, groups_up))
    entry_delta = (entry_back * silu_slope(entry_pre)).astype(jnp.bfloat16)
    entry_grad = weight_grad(second_act, entry_delta, 1)
    second_back = conv_valid(border(entry_delta), back_kernel(entry_weight), 1)
    second_delta = (second_back * silu_slope(second_pre)).astype(jnp.bfloat16)
    second_grad = weight_grad(first_act, second_delta, 1)
    first_back = conv_valid(border(second_delta), back_kernel(second_weight), 1)
    first_delta = (first_back * silu_slope(first_pre)).astype(jnp.bfloat16)
    first_grad = weight_grad(stem_act, first_delta, 1)
    stem_back = conv_valid(border(first_delta), back_kernel(first_weight), 1)
    stem_delta = (stem_back * silu_slope(stem_pre)).astype(jnp.bfloat16)
    stem_grad = weight_grad(padded_in, stem_delta, 2)
    return (stem_grad * norm_scale, first_grad * norm_scale, second_grad * norm_scale, entry_grad * norm_scale, final_grad * norm_scale)
```

```python
import functools
import math

import jax
import jax.numpy as jnp
from jax import lax
from jax.experimental import pallas as pl
from jax.experimental.pallas import tpu as pltpu
from jax.sharding import PartitionSpec as P

BF = jnp.bfloat16
F32 = jnp.float32
MESH = pl.DeviceIdType.MESH
VMEM = pl.BlockSpec(memory_space=pltpu.VMEM)
EDGE = 4
SLABS = 12


def silu(v):
    h = 0.5 * v
    return h + h * jnp.tanh(h)


def slope(v):
    h = 0.5 * v
    t = jnp.tanh(h)
    return (0.5 + 0.5 * t) * (1.0 + h * (1.0 - t))


def slab_table(rows_of):
    slots = -(-SLABS // rows_of)
    table, free = {}, [(i, r) for i in range(slots) for r in range(rows_of)]
    for n in range(3):
        table["e", n] = free.pop(0)
    free.sort(key=lambda at: (at[1], at[0]))
    for n in range(9):
        table["f", n] = free.pop(0)
    return slots, table


def shift_up(v, axis):
    return pltpu.roll(v, 1, axis)


def shift_down(v, axis):
    return pltpu.roll(v, v.shape[axis] - 1, axis)


def step_kernel(dims, *refs):
    rows_of, cols_of, rows, cols, tile, group, feats, tail, scale = dims
    (pix_ref, stem_ref, first_ref, second_ref, entry_ref, final_ref, up_ref) = refs[:7]
    fg_out, eg_out, sg_out = refs[7:10]
    (qsend, pixbuf, quads, padf, padz, stem_mat, onehot, fwd1, fwd2, bwd1, bwd2, entry_mat,
     back_mat, act0, act1, act2, pre0, pre1, pre2, entry_act, entry_pre, upq, facc,
     zsend, zbuf, up3, ed3, sd3, fd3, td3, wall,
     egs, egr, egm, sgs, sgr, sgm, sga, sgf,
     pix_s, pix_r, prim_s, prim_r, up_s, up_r, urim_s, urim_r,
     wa_s, wa_r, wb_s, wb_r, wc_s, wc_r, fg_s, fg_r,
     e1_s, e1_r, e2_s, e2_r, s1_s, s1_r, s2_s, s2_r, s3_s, s3_r) = refs[10:]

    row, col = lax.axis_index("row"), lax.axis_index("col")
    core, chip = lax.rem(col, 2), lax.div(col, 2)
    chips = cols_of // 2
    groups = rows // 8
    wide, win = cols + 16, tile + 16
    span = rows * rows_of
    pairs = rows // 2
    wfrom = pl.multiple_of(col * tile, tile)
    not_first, not_last = row > 0, row < rows_of - 1
    slots, table = slab_table(rows_of)

    def remote(src, dst, send, recv, peer):
        return pltpu.make_async_remote_copy(
            src_ref=src, dst_ref=dst, send_sem=send, recv_sem=recv,
            device_id=peer, device_id_type=MESH)

    barrier = pltpu.get_barrier_semaphore()
    for k in range(1, cols_of):
        pl.semaphore_signal(barrier, inc=1, device_id=(row, lax.rem(col + k, cols_of)), device_id_type=MESH)
    for k in range(1, rows_of):
        pl.semaphore_signal(barrier, inc=1, device_id=(lax.rem(row + k, rows_of), col), device_id_type=MESH)
    for side, there in ((-1, not_first), (1, not_last)):

        @pl.when(there)
        def _():
            for k in range(1, cols_of):
                pl.semaphore_signal(
                    barrier, inc=1, device_id=(row + side, lax.rem(col + k, cols_of)), device_id_type=MESH)

    lane_q = lax.broadcasted_iota(jnp.int32, (4 * group, 128), 1)
    for g in range(groups):
        pieces = []
        for a in range(2):
            for c in range(3):
                pieces.append(pix_ref[c, pl.ds(a, tile, stride=2), :][:, 16 * g : 16 * g + 16])
            pieces.append(jnp.zeros((tile, 16), F32))
        qsend[g] = jnp.concatenate(pieces, axis=1).astype(BF)

    own = pl.ds(pl.multiple_of(group * col, group), group)
    for t in range(9):
        i, r = table["f", t]
        wall[i, r, own, :] = final_ref[t]
    for n in range(3):
        i, r = table["e", n]
        taps = [entry_ref[4 * n + u] if 4 * n + u < 9 else jnp.zeros((group, feats), BF) for u in range(4)]
        wall[i, r, own, :] = jnp.concatenate(taps, axis=1)

    padz[...] = jnp.zeros_like(padz)
    padf[...] = jnp.zeros_like(padf)

    def spread_up(m, carry):
        x = up_ref[pl.ds(4 * m, 4)].reshape(4 * group, cols).astype(F32)
        padz[EDGE : EDGE + cols, :] = x.T
        zsend[m] = padz[...].astype(BF)
        return carry

    lax.fori_loop(0, rows // 4, spread_up, 0)

    adj = not_first.astype(jnp.int32) + not_last.astype(jnp.int32)
    pl.semaphore_wait(barrier, (cols_of - 1) * (1 + adj) + rows_of - 1)

    sides = ((-1, not_first), (1, not_last))

    def pix_copy(k):
        return remote(qsend, pixbuf.at[pl.ds(1, groups), col], pix_s.at[k], pix_r.at[k],
                      (row, lax.rem(col + k, cols_of)))

    def pix_rim(side, k):
        at = 0 if side < 0 else 1
        return remote(qsend.at[0 if side < 0 else groups - 1],
                      pixbuf.at[groups + 1 if side < 0 else 0, col],
                      prim_s.at[at, k], prim_r.at[at, k], (row + side, lax.rem(col + k, cols_of)))

    fours = rows // 4

    def up_window(k):
        peer = lax.rem(col + k, cols_of)
        return peer, pl.ds(pl.multiple_of(peer * tile, tile), tile + 8)

    def up_copy(k):
        peer, window = up_window(k)
        return remote(zsend.at[:, window], zbuf.at[col, pl.ds(1, fours), pl.ds(0, tile + 8)],
                      up_s.at[k], up_r.at[k], (row, peer))

    def up_rim(side, k):
        at = 0 if side < 0 else 1
        peer, window = up_window(k)
        return remote(zsend.at[0 if side < 0 else fours - 1, window],
                      zbuf.at[col, fours + 1 if side < 0 else 0, pl.ds(0, tile + 8)],
                      urim_s.at[at, k], urim_r.at[at, k], (row + side, peer))

    def shard(z, c):
        return pl.ds(pl.multiple_of(group * (2 * z + c), group), group)

    def gather_a(part, k):
        at = wall.at[0, row, shard(chip, core)] if part == 0 else wall.at[pl.ds(1, slots - 1), row, shard(chip, core)]
        return remote(at, at, wa_s.at[part, k], wa_r.at[part, k],
                      (row, 2 * lax.rem(chip + k, chips) + core))

    def gather_b(part, k, z):
        here = shard(lax.rem(chip + z, chips), core)
        at = wall.at[0, row, here] if part == 0 else wall.at[pl.ds(1, slots - 1), row, here]
        return remote(at, at, wb_s.at[part, k, z], wb_r.at[part, k, z], (lax.rem(row + k, rows_of), col))

    def gather_c(part, z):
        here = shard(z, core)
        at = wall.at[0, :, here] if part == 0 else wall.at[pl.ds(1, slots - 1), :, here]
        return remote(at, at, wc_s.at[part, z], wc_r.at[part, z], (row, 2 * chip + 1 - core))

    for k in range(1, cols_of):
        pix_copy(k).start()
    for side, there in sides:

        @pl.when(there)
        def _():
            for k in range(cols_of):
                pix_rim(side, k).start()

    for part in range(2):
        for k in range(1, chips):
            gather_a(part, k).start()
    for k in range(1, cols_of):
        up_copy(k).start()
    for side, there in sides:

        @pl.when(there)
        def _():
            for k in range(cols_of):
                up_rim(side, k).start()

    pixbuf[pl.ds(1, groups), col] = qsend[...]
    zbuf[:, :, tile + 8 :, :] = jnp.zeros((cols_of, fours + 2, win - tile - 8, 4 * group), BF)
    zbuf[col, pl.ds(1, fours), 0 : tile + 8] = zsend[:, pl.ds(wfrom, tile + 8)]

    @pl.when(row == 0)
    def _():
        pixbuf[0] = jnp.zeros(pixbuf.shape[1:], BF)
        zbuf[:, 0] = jnp.zeros((cols_of,) + zbuf.shape[2:], BF)

    @pl.when(row == rows_of - 1)
    def _():
        pixbuf[groups + 1] = jnp.zeros(pixbuf.shape[1:], BF)
        zbuf[:, fours + 1] = jnp.zeros((cols_of,) + zbuf.shape[2:], BF)

    spot = lax.broadcasted_iota(jnp.int32, (128, 48), 0)
    want = lax.broadcasted_iota(jnp.int32, (128, 48), 1)
    la, lc, lr, lb = spot // 64, (spot // 16) % 4, (spot // 4) % 4, spot % 4
    for v in range(4):
        d = (lr + (5 - v)) % 4 - 1
        for s in range(3):
            q = 2 * (s - 1) + la + 1
            parts = []
            for e in range(2):
                p = 4 * d + lb - 2 * e + 1
                fits = (lc < 3) & (p >= 0) & (p < 4) & (q >= 0) & (q < 4)
                hot = (fits & (want == lc * 16 + p * 4 + q)).astype(F32).astype(BF)
                onehot[2 * s + e, 128 * v : 128 * v + 128, :] = hot
                parts.append(jnp.dot(hot, stem_ref[...], preferred_element_type=F32))
            stem_mat[v, :, 2 * feats * s : 2 * feats * (s + 1)] = jnp.concatenate(parts, axis=1).astype(BF)

    zero = jnp.zeros((feats, feats), F32)
    for w_ref, fwd, bwd in ((first_ref, fwd1, bwd1), (second_ref, fwd2, bwd2)):
        for q in range(3):
            w = [w_ref[3 * p + q].astype(F32) for p in range(3)]
            even = jnp.concatenate([w[1], w[2], zero, w[0]], axis=1)
            odd = jnp.concatenate([w[0], w[1], w[2], zero], axis=1)
            both = jnp.concatenate([even, odd], axis=0)
            fwd[4 * feats * q : 4 * feats * (q + 1)] = both.T.astype(BF)
            lines = [[w[1], w[2]], [w[0], w[1]], [zero, w[0]], [w[2], zero]]
            back = jnp.concatenate([jnp.concatenate(line, axis=1) for line in lines], axis=0)
            bwd[4 * feats * q : 4 * feats * (q + 1)] = back.astype(BF)

    for at in (act0, act1, act2):
        for q in range(3):
            at[q, 0] = jnp.zeros((wide, 128), BF)
            at[q, pairs + 7] = jnp.zeros((wide, 128), BF)

    for k in range(1, cols_of):
        pix_copy(k).wait_recv()
    for side, there in sides:
        other = not_last if side < 0 else not_first

        @pl.when(other)
        def _():
            for k in range(cols_of):
                pix_rim(side, k).wait_recv()

    for g in range(groups + 2):
        padf[EDGE : EDGE + cols, :] = pixbuf[g].reshape(cols, 128).astype(F32)
        quads[g] = padf[...].astype(BF)

    for k in range(1, chips):
        gather_a(0, k).wait_recv()
    for k in range(1, rows_of):
        for z in range(1, chips):
            gather_b(0, k, z).start()

    lane = lax.broadcasted_iota(jnp.int32, (1, 128), 1)
    upper = (lane >= feats).astype(jnp.int32)
    sub = lax.broadcasted_iota(jnp.int32, (wide, 1), 0) - EDGE
    in_cols = (sub >= 0) & (sub < cols)
    base = row * rows

    def in_rows(r):
        line = base + 2 * r + upper
        return (line >= 0) & (line < span)

    def put(dst, at, value):
        dst[0, at] = shift_up(value, 0).astype(BF)
        dst[1, at] = value.astype(BF)
        dst[2, at] = shift_down(value, 0).astype(BF)

    def stem_lhs(g, v, window):
        if v == 0:
            return jnp.where(lr_lane == 3, quads[g - 1, window, :], quads[g, window, :])
        if v == 3:
            return jnp.where(lr_lane == 0, quads[g + 1, window, :], quads[g, window, :])
        return quads[g, window, :]

    lr_lane = (lax.broadcasted_iota(jnp.int32, (1, 128), 1) // 4) % 4

    def stem_one(g, v):
        r = 4 * (g - 1) + v
        out = jnp.dot(stem_lhs(g, v, pl.ds(0, wide)), stem_mat[v], preferred_element_type=F32)
        n = 2 * feats
        pre = shift_up(out[:, :n], 0) + out[:, n : 2 * n] + shift_down(out[:, 2 * n :], 0)
        pre0[r + 3] = pre
        put(act0, r + 4, jnp.where(in_rows(r) & in_cols, silu(pre), 0.0))

    for v in (1, 2, 3):
        stem_one(0, v)

    def stem_group(g, carry):
        for v in range(4):
            stem_one(g, v)
        return carry

    lax.fori_loop(1, groups + 1, stem_group, 0)
    for v in (0, 1, 2):
        stem_one(groups + 1, v)

    low = lax.broadcasted_iota(jnp.int32, (1, 1, 128), 2) < feats

    def conv_lhs(src, at, n, window):
        size = window.size
        out = []
        for q in range(3):
            x = src[q, pl.ds(at, n), window, :]
            mix = jnp.where(low, src[q, pl.ds(at + 1, n), window, :], src[q, pl.ds(at - 1, n), window, :])
            out += [x.reshape(n * size, 128), mix.reshape(n * size, 128)]
        return out

    everything = pl.ds(0, wide)

    def conv(src, at, n, window, mat):
        parts = conv_lhs(src, at, n, window)
        lhs = jnp.concatenate(parts, axis=1)
        out = jnp.dot(lhs, mat, preferred_element_type=F32)
        return out.reshape(n, window.size, out.shape[1])

    def forward(src, mat, pre_ref, dst, first, count):
        def one(m, carry):
            r = first + 2 * m
            out = conv(src, r + 4, 2, everything, mat[...])
            for n in range(2):
                pre_ref[r + n + 3] = out[n]
                put(dst, r + n + 4, jnp.where(in_rows(r + n) & in_cols, silu(out[n]), 0.0))
            return carry

        lax.fori_loop(0, count // 2, one, 0)

    for k in range(1, chips):
        gather_a(1, k).wait_recv()
    for k in range(1, rows_of):
        for z in range(1, chips):
            gather_b(1, k, z).start()
    forward(act0, fwd1, pre1, act1, -3, pairs + 6)
    for k in range(1, rows_of):
        for z in range(1, chips):
            gather_b(0, k, z).wait_recv()
    for z in range(chips):
        gather_c(0, z).start()
    forward(act1, fwd2, pre2, act2, -2, pairs + 4)

    def spread_final(i, carry):
        x = up_ref[i].astype(F32)
        at = lax.broadcasted_iota(jnp.int32, x.shape, 1)
        left = jnp.where(at == cols - 1, 0.0, shift_down(x, 1))
        right = jnp.where(at == 0, 0.0, shift_up(x, 1))
        upq[i + 2] = jnp.concatenate([left, x, right], axis=0).astype(BF)
        return carry

    for i in (0, 1, rows + 2, rows + 3):
        upq[i] = jnp.zeros(upq.shape[1:], BF)
    lax.fori_loop(0, rows, spread_final, 0)

    for z in range(chips):
        gather_c(0, z).wait_recv()

    def entry_tap(t):
        i, r = table["e", t // 4]
        u = t % 4
        return wall[i, r, :, feats * u : feats * (u + 1)]

    none = jnp.zeros((tail, feats), F32)
    for q in range(3):
        w = [entry_tap(3 * p + q) for p in range(3)]
        wf = [x.astype(F32) for x in w]
        for e, line in enumerate(([wf[1], wf[2], none, wf[0]], [wf[0], wf[1], wf[2], none])):
            for h in range(2):
                block = jnp.concatenate(line[2 * h : 2 * h + 2], axis=1).T.astype(BF)
                entry_mat[e, 4 * feats * q + 2 * feats * h : 4 * feats * q + 2 * feats * (h + 1), :] = block
        nil = jnp.zeros((tail, feats), BF)
        for a, pair in enumerate(([w[2], nil], [w[1], w[2]], [w[0], w[1]], [nil, w[0]])):
            back_mat[tail * (4 * q + a) : tail * (4 * q + a + 1), :] = jnp.concatenate(pair, axis=1)

    def entry_step(m, carry):
        r = 2 * m - 2
        lhs = jnp.concatenate(conv_lhs(act2, r + 4, 2, everything), axis=1)
        for e in range(2):
            out = jnp.dot(lhs, entry_mat[e], preferred_element_type=F32).reshape(2, wide, tail)
            for n in range(2):
                line = base + 2 * (r + n) + e
                inside = (line >= 0) & (line < span)
                at = 2 * (r + n + 2) + e
                entry_pre[at] = out[n]
                moved = pltpu.roll(silu(out[n]), wide - EDGE, 0)[:cols]
                entry_act[at] = jnp.where(inside, moved, 0.0).astype(BF)
        return carry

    lax.fori_loop(0, pairs // 2 + 2, entry_step, 0)

    for k in range(1, rows_of):
        for z in range(1, chips):
            gather_b(1, k, z).wait_recv()
    for z in range(chips):
        gather_c(1, z).start()

    facc[...] = jnp.zeros_like(facc)
    three = 9 * group

    def final_step(m, carry):
        one = upq[pl.ds(2 * m, 3)].reshape(three, cols)
        two = upq[pl.ds(2 * m + 1, 3)].reshape(three, cols)
        rhs = entry_act[pl.ds(2 * m + 3, 2)].reshape(2 * cols, tail)
        facc[...] += jnp.dot(jnp.concatenate([one, two], axis=1), rhs, preferred_element_type=F32)
        return carry

    lax.fori_loop(0, rows // 2 + 1, final_step, 0)
    fg_out[row] = (facc[...] * scale).astype(BF)

    def fg_copy(k):
        return remote(fg_out.at[row], fg_out.at[row], fg_s.at[k], fg_r.at[k], (lax.rem(row + k, rows_of), col))

    for k in range(1, rows_of):
        fg_copy(k).start()

    for k in range(1, cols_of):
        up_copy(k).wait_recv()
    for side, there in sides:
        other = not_last if side < 0 else not_first

        @pl.when(other)
        def _():
            for k in range(cols_of):
                up_rim(side, k).wait_recv()

    def unpack_up(m, carry):
        got = [zbuf[s, m].astype(F32) for s in range(cols_of)]
        for r in range(4):
            x = jnp.concatenate([z[:, group * r : group * (r + 1)] for z in got], axis=1)
            at = 4 * m + r
            up3[0, at] = shift_down(x, 0).astype(BF)
            up3[1, at] = x.astype(BF)
            up3[2, at] = shift_up(x, 0).astype(BF)
        return carry

    lax.fori_loop(0, fours + 2, unpack_up, 0)
    for z in range(chips):
        gather_c(1, z).wait_recv()

    wsub = lax.broadcasted_iota(jnp.int32, (win, 1), 0) - EDGE
    wcol = wsub + wfrom
    win_cols = (wcol >= 0) & (wcol < cols)
    mine = (wsub >= 0) & (wsub < tile)
    window = pl.ds(wfrom, win)

    def put_back(dst, at, value):
        lead = at if isinstance(at, tuple) else (at,)
        dst[(0,) + lead] = shift_down(value, 0).astype(BF)
        dst[(1,) + lead] = value.astype(BF)
        dst[(2,) + lead] = shift_up(value, 0).astype(BF)

    lot = 10 if (rows + 6) % 10 == 0 else 2

    def entry_back(m, carry):
        k0 = m * lot
        total = jnp.zeros((lot * win, tail), F32)
        for p in range(3):
            for q in range(3):
                i, r = table["f", 3 * p + q]
                lhs = up3[q, pl.ds(k0 + 2 - p, lot)].reshape(lot * win, tail)
                total = total + jnp.dot(lhs, wall[i, r], preferred_element_type=F32)
        total = total.reshape(lot, win, tail)
        for n in range(lot):
            k = k0 + n
            line = base + k - 3
            inside = (line >= 0) & (line < span) & win_cols
            delta = jnp.where(inside, total[n] * slope(entry_pre[k + 1, window, :]), 0.0)
            put_back(ed3, (lax.div(k, 2), lax.rem(k, 2)), delta)
        return carry

    lax.fori_loop(0, (rows + 6) // lot, entry_back, 0)

    def grad_lhs(src, at):
        x = src[1, pl.ds(at, pairs)]
        return jnp.where(mine, x, jnp.zeros_like(x)).reshape(pairs * win, 2 * feats)

    def grad_taps(src, q):
        x = src[q, pl.ds(4, pairs), window, :]
        mix = jnp.where(low, src[q, pl.ds(5, pairs), window, :], src[q, pl.ds(3, pairs), window, :])
        return jnp.concatenate([x.reshape(pairs * win, 128), mix.reshape(pairs * win, 128)], axis=1)

    def outer(lhs, rhs):
        return lax.dot_general(lhs, rhs, (((0,), (0,)), ((), ())), preferred_element_type=F32) * scale

    def entry_own(e):
        x = ed3[1, pl.ds(1 + e, pairs), 1 - e]
        return jnp.where(mine, x, jnp.zeros_like(x)).reshape(pairs * win, tail)

    own_even, own_odd = entry_own(0), entry_own(1)
    grads = {}
    f = feats
    for q in range(3):
        taps = grad_taps(act2, q)
        ge, go = outer(own_even, taps), outer(own_odd, taps)
        grads[0, q] = ge[:, 3 * f :] + go[:, :f]
        grads[1, q] = ge[:, :f] + go[:, f : 2 * f]
        grads[2, q] = ge[:, f : 2 * f] + go[:, 2 * f : 3 * f]
    for t in range(0, 9, 2):
        two = [grads[(t + u) // 3, (t + u) % 3] if t + u < 9 else jnp.zeros((tail, f), F32) for u in range(2)]
        egs[:, t // 2] = jnp.concatenate(two, axis=1).astype(BF).reshape(cols_of, group, 2 * f)

    def e1_copy(k):
        peer = lax.rem(col + k, cols_of)
        return remote(egs.at[peer], egr.at[k], e1_s.at[k], e1_r.at[k], (row, peer))

    for k in range(1, cols_of):
        e1_copy(k).start()

    some = 7 if (pairs + 2) % 7 == 0 else 2

    def second_back(m, carry):
        r0 = m * some
        total = jnp.zeros((some * win, 2 * feats), F32)
        for q in range(3):
            for a in range(4):
                lhs = ed3[q, pl.ds(r0 + a // 2, some), a % 2].reshape(some * win, tail)
                at = tail * (4 * q + a)
                total = total + jnp.dot(lhs, back_mat[at : at + tail, :], preferred_element_type=F32)
        total = total.reshape(some, win, 2 * feats)
        for n in range(some):
            r = r0 + n - 1
            inside = in_rows(r) & win_cols
            put_back(sd3, r + 2, jnp.where(inside, total[n] * slope(pre2[r + 3, window, :]), 0.0))
        return carry

    for q in range(3):
        sd3[q, 0] = jnp.zeros((win, 128), BF)
        sd3[q, pairs + 3] = jnp.zeros((win, 128), BF)
    lax.fori_loop(0, (pairs + 2) // some, second_back, 0)

    def pair_grads(src, delta):
        out = {}
        for q in range(3):
            g = outer(delta, grad_taps(src, q))
            out[0, q] = g[:f, 3 * f :] + g[f:, :f]
            out[1, q] = g[:f, :f] + g[f:, f : 2 * f]
            out[2, q] = g[:f, f : 2 * f] + g[f:, 2 * f : 3 * f]
        return out

    whole = pl.ds(0, win)
    second_grads = pair_grads(act1, grad_lhs(sd3, 2))

    def first_back(m, carry):
        r0 = m * some
        out = conv(sd3, r0 + 1, some, whole, bwd2[...])
        for n in range(some):
            r = r0 + n - 1
            inside = in_rows(r) & win_cols
            put_back(fd3, r + 1, jnp.where(inside, out[n] * slope(pre1[r + 3, window, :]), 0.0))
        return carry

    lax.fori_loop(0, (pairs + 2) // some, first_back, 0)
    first_grads = pair_grads(act0, grad_lhs(fd3, 1))
    for t in range(9):
        both = jnp.concatenate([second_grads[t // 3, t % 3], first_grads[t // 3, t % 3]], axis=1)
        sgs[:, t] = both.reshape(cols_of, feats // cols_of, 2 * f).astype(BF)

    few = 6 if pairs % 6 == 0 else 2

    def stem_back(m, carry):
        r0 = m * few
        out = conv(fd3, r0 + 1, few, whole, bwd1[...])
        for n in range(few):
            r = r0 + n
            delta = jnp.where(mine, out[n] * slope(pre0[r + 3, window, :]), 0.0)
            td3[r] = jnp.concatenate(
                [shift_down(delta, 0), delta, shift_up(delta, 0)], axis=1).astype(BF)
        return carry

    lax.fori_loop(0, pairs // few, stem_back, 0)
    moments = []
    for v in range(4):
        lhs = jnp.concatenate([stem_lhs(g, v, window) for g in range(1, groups + 1)], axis=0)
        rhs = jnp.concatenate([td3[4 * g + v] for g in range(groups)], axis=0)
        moments.append(outer(lhs, rhs))
    moment = jnp.concatenate(moments, axis=0)
    total = jnp.zeros((feats, 48), F32)
    for s in range(3):
        for e in range(2):
            part = moment[:, 2 * f * s + f * e : 2 * f * s + f * (e + 1)].astype(BF)
            total = total + lax.dot_general(
                part, onehot[2 * s + e], (((0,), (0,)), ((), ())), preferred_element_type=F32)
    total = jnp.concatenate([total, jnp.zeros((feats, 2 * f - 48), F32)], axis=1)
    sgs[:, 9] = total.reshape(cols_of, feats // cols_of, 2 * f).astype(BF)

    def s1_copy(k):
        peer = lax.rem(col + k, cols_of)
        return remote(sgs.at[peer], sgr.at[k], s1_s.at[k], s1_r.at[k], (row, peer))

    def e2_copy(k):
        return remote(egm, eg_out.at[row], e2_s.at[k], e2_r.at[k], (lax.rem(row + k, rows_of), col))

    def s2_copy(k):
        return remote(sgm, sga.at[row], s2_s.at[k], s2_r.at[k], (lax.rem(row + k, rows_of), col))

    def s3_copy(k):
        return remote(sgf, sg_out.at[col], s3_s.at[k], s3_r.at[k], (row, lax.rem(col + k, cols_of)))

    for k in range(1, cols_of):
        s1_copy(k).start()

    def col_sum(sent, got, copy):
        acc = sent[col].astype(F32)
        for k in range(1, cols_of):
            copy(k).wait_recv()
            acc = acc + got[k].astype(F32)
        return acc.astype(BF)

    esum = col_sum(egs, egr, e1_copy)
    egm[...] = esum
    eg_out[row] = esum
    for k in range(1, rows_of):
        e2_copy(k).start()
    ssum = col_sum(sgs, sgr, s1_copy)
    sgm[...] = ssum
    for k in range(1, rows_of):
        s2_copy(k).start()
    sga[row] = ssum
    for k in range(1, rows_of):
        s2_copy(k).wait_recv()
    acc = sga[0].astype(F32)
    for r in range(1, rows_of):
        acc = acc + sga[r].astype(F32)
    sgf[...] = acc.astype(BF)
    for k in range(1, cols_of):
        s3_copy(k).start()
    sg_out[col] = acc.astype(BF)

    for part in range(2):
        for k in range(1, chips):
            gather_a(part, k).wait_send()
        for k in range(1, rows_of):
            for z in range(1, chips):
                gather_b(part, k, z).wait_send()
        for z in range(chips):
            gather_c(part, z).wait_send()
    for k in range(1, cols_of):
        pix_copy(k).wait_send()
        up_copy(k).wait_send()
        e1_copy(k).wait_send()
        s1_copy(k).wait_send()
    for side, there in sides:

        @pl.when(there)
        def _():
            for k in range(cols_of):
                pix_rim(side, k).wait_send()
                up_rim(side, k).wait_send()

    for k in range(1, rows_of):
        fg_copy(k).wait()
        e2_copy(k).wait()
        s2_copy(k).wait_send()
    for k in range(1, cols_of):
        s3_copy(k).wait()


def step(pix, stem, first, second, entry, final, up, tile, scale):
    rows_of, cols_of = lax.axis_size("row"), lax.axis_size("col")
    rows, group, cols = up.shape
    feats, tail = first.shape[1], final.shape[2]
    dims = (rows_of, cols_of, rows, cols, tile, group, feats, tail, scale)
    groups, wide, win, pairs, fours = rows // 8, cols + 16, tile + 16, rows // 2, rows // 4
    slots, _ = slab_table(rows_of)
    chips, share = cols_of // 2, feats // cols_of
    act = pltpu.VMEM((3, pairs + 8, wide, 128), BF)
    pre = pltpu.VMEM((pairs + 6, wide, 128), F32)
    dma = pltpu.SemaphoreType.DMA
    mat = pltpu.VMEM((12 * feats, 2 * feats), BF)

    def vm(*shape, kind=BF):
        return pltpu.VMEM(shape, kind)

    scratch = [
        vm(groups, tile, 128), vm(groups + 2, cols_of, tile, 128), vm(groups + 2, wide, 128),
        vm(wide, 128, kind=F32), vm(wide, 4 * group, kind=F32), vm(4, 128, 6 * feats), vm(6, 512, 48),
        mat, mat, mat, mat, vm(2, 12 * feats, tail),
        vm(12 * tail, 2 * feats), act, act, act, pre, pre, pre,
        vm(rows + 8, cols, tail), vm(rows + 8, wide, tail, kind=F32),
        vm(rows + 4, 3 * group, cols), vm(9 * group, tail, kind=F32),
        vm(fours, wide, 4 * group), vm(cols_of, fours + 2, win, 4 * group),
        vm(3, rows + 8, win, tail), vm(3, pairs + 3, 2, win, tail),
        vm(3, pairs + 4, win, 128), vm(3, pairs + 2, win, 128), vm(pairs, win, 384),
        vm(slots, rows_of, tail, tail),
        vm(cols_of, 5, group, 128), vm(cols_of, 5, group, 128), vm(5, group, 128),
        vm(cols_of, 10, share, 128), vm(cols_of, 10, share, 128), vm(10, share, 128),
        vm(rows_of, 10, share, 128), vm(10, share, 128),
    ]
    for shape in (
        (cols_of,), (2, cols_of), (cols_of,), (2, cols_of), (2, chips), (2, rows_of, chips), (2, chips), (rows_of,),
        (cols_of,), (rows_of,), (cols_of,), (rows_of,), (cols_of,),
    ):
        scratch += [dma(shape), dma(shape)]
    return pl.pallas_call(
        functools.partial(step_kernel, dims),
        out_shape=(
            jax.ShapeDtypeStruct((rows_of, 9 * group, tail), BF),
            jax.ShapeDtypeStruct((rows_of, 5, group, 128), BF),
            jax.ShapeDtypeStruct((cols_of, 10, share, 128), BF),
        ),
        in_specs=[VMEM] * 7,
        out_specs=(VMEM,) * 3,
        scratch_shapes=scratch,
        compiler_params=pltpu.CompilerParams(
            collective_id=0, has_side_effects=True, vmem_limit_bytes=58 * 1024 * 1024),
    )(pix, stem, first, second, entry, final, up)


def finish_kernel(fg_ref, eg_ref, sg_ref, stem_out, first_out, second_out, entry_out, final_out):
    rows_of, _, tail = fg_ref.shape
    group, feats = entry_out.shape[1:]

    def total(ref, at):
        acc = ref[(0,) + at].astype(F32)
        for r in range(1, rows_of):
            acc = acc + ref[(r,) + at].astype(F32)
        return acc

    for p in range(3):
        for q in range(3):
            at = ((2 - p) * 3 + q) * group
            final_out[3 * p + q] = total(fg_ref, (slice(at, at + group),))
    for t in range(9):
        if t % 2 == 0:
            both = total(eg_ref, (t // 2,))
        entry_out[t] = both[:, (t % 2) * feats : (t % 2 + 1) * feats]
        pair = sg_ref[:, t].astype(F32).reshape(feats, 2 * feats)
        second_out[t] = pair[:, :feats]
        first_out[t] = pair[:, feats:]
    stem = sg_ref[:, 9].astype(F32).reshape(feats, 2 * feats)
    stem_out[...] = stem.T[: stem_out.shape[0]]


def finish(fg, eg, sg, feats):
    group, tail = eg.shape[2], fg.shape[2]
    return pl.pallas_call(
        finish_kernel,
        out_shape=(
            jax.ShapeDtypeStruct((48, feats), F32),
            jax.ShapeDtypeStruct((9, feats, feats), F32),
            jax.ShapeDtypeStruct((9, feats, feats), F32),
            jax.ShapeDtypeStruct((9, group, feats), F32),
            jax.ShapeDtypeStruct((9, group, tail), F32),
        ),
        in_specs=[VMEM] * 3,
        out_specs=(VMEM,) * 5,
    )(fg, eg, sg)


def per_device(pixels, stem_weight, first_weight, second_weight, entry_weight, final_weight, upstream):
    chans, pix_rows, pix_cols = pixels.shape
    rows, tile = pix_rows // 2, pix_cols // 2
    cols = tile * lax.axis_size("col")
    scale = 1.0 / math.sqrt(rows * lax.axis_size("row") * cols)

    def flat(kernel):
        return kernel.transpose(2, 3, 0, 1).reshape(9, kernel.shape[0], kernel.shape[1])

    stem = stem_weight.transpose(1, 2, 3, 0).reshape(chans * 16, stem_weight.shape[0])
    fg, eg, sg = step(
        pixels.transpose(0, 2, 1), stem, flat(first_weight), flat(second_weight), flat(entry_weight),
        flat(final_weight), upstream.transpose(1, 0, 2), tile, scale)
    stem_grad, first_grad, second_grad, entry_grad, final_grad = finish(fg, eg, sg, stem_weight.shape[0])

    def taps_last(grad):
        return grad.reshape(3, 3, grad.shape[1], grad.shape[2]).transpose(2, 3, 0, 1)

    return (
        stem_grad.reshape(chans, 4, 4, -1).transpose(3, 0, 1, 2),
        taps_last(first_grad),
        taps_last(second_grad),
        taps_last(entry_grad),
        taps_last(final_grad),
    )


def solution(mesh):
    return jax.shard_map(
        per_device,
        mesh=mesh,
        in_specs=(
            P(None, "row", "col"),
            P(),
            P(),
            P(),
            P("col", None, None, None),
            P("col", None, None, None),
            P("col", "row", None),
        ),
        out_specs=(P(), P(), P(), P("col", None, None, None), P("col", None, None, None)),
        check_vma=False,
    )
```

```python
import functools
import math

import jax
import jax.numpy as jnp
from jax import lax
from jax.experimental import pallas as pl
from jax.experimental.pallas import tpu as pltpu
from jax.sharding import PartitionSpec as P

BF = jnp.bfloat16
F32 = jnp.float32
MESH = pl.DeviceIdType.MESH
VMEM = pl.BlockSpec(memory_space=pltpu.VMEM)
EDGE = 4
SLABS = 12


def silu(v):
    h = 0.5 * v
    return h + h * jnp.tanh(h)


def slope(v):
    h = 0.5 * v
    t = jnp.tanh(h)
    return (0.5 + 0.5 * t) * (1.0 + h * (1.0 - t))


def slab_table(rows_of):
    slots = -(-SLABS // rows_of)
    table, free = {}, [(i, r) for i in range(slots) for r in range(rows_of)]
    for n in range(3):
        table["e", n] = free.pop(0)
    free.sort(key=lambda at: (at[1], at[0]))
    for n in range(9):
        table["f", n] = free.pop(0)
    return slots, table


def shift_up(v, axis):
    return pltpu.roll(v, 1, axis)


def shift_down(v, axis):
    return pltpu.roll(v, v.shape[axis] - 1, axis)


def step_kernel(dims, *refs):
    rows_of, cols_of, rows, cols, tile, group, feats, tail, scale = dims
    (pix_ref, stem_ref, first_ref, second_ref, entry_ref, final_ref, up_ref) = refs[:7]
    fg_out, eg_out, sa_out, sb_out = refs[7:11]
    (qsend, pixbuf, quads, padf, padz, stem_mat, onehot, fwd1, fwd2, bwd1, bwd2, entry_mat,
     back_mat, act0, act1, act2, pre0, pre1, pre2, entry_act, entry_pre, upq, facc,
     up_rows, zsend, zbuf, up3, ed3, sd3, fd3, td3, wall, fgbuf,
     egs, egr, egm, egq, egn, sas, sar, sam, saa, saf, sbs, sbr, sbm, sba, sbf,
     pix_s, pix_r, prim_s, prim_r, up_s, up_r, urim_s, urim_r,
     wa_s, wa_r, wb_s, wb_r, wc_s, wc_r, fg_s, fg_r,
     e1_s, e1_r, e2_s, e2_r, e3_s, e3_r,
     a1_s, a1_r, a2_s, a2_r, a3_s, a3_r, b1_s, b1_r, b2_s, b2_r, b3_s, b3_r) = refs[11:]

    row, col = lax.axis_index("row"), lax.axis_index("col")
    core, chip = lax.rem(col, 2), lax.div(col, 2)
    chips = cols_of // 2
    groups = rows // 8
    wide, win = cols + 16, tile + 16
    span = rows * rows_of
    pairs = rows // 2
    wfrom = pl.multiple_of(col * tile, tile)
    not_first, not_last = row > 0, row < rows_of - 1
    slots, table = slab_table(rows_of)

    def remote(src, dst, send, recv, peer):
        return pltpu.make_async_remote_copy(
            src_ref=src, dst_ref=dst, send_sem=send, recv_sem=recv,
            device_id=peer, device_id_type=MESH)

    barrier = pltpu.get_barrier_semaphore()
    for k in range(1, cols_of):
        pl.semaphore_signal(barrier, inc=1, device_id=(row, lax.rem(col + k, cols_of)), device_id_type=MESH)
    for k in range(1, rows_of):
        pl.semaphore_signal(barrier, inc=1, device_id=(lax.rem(row + k, rows_of), col), device_id_type=MESH)
    for side, there in ((-1, not_first), (1, not_last)):

        @pl.when(there)
        def _():
            for k in range(1, cols_of):
                pl.semaphore_signal(
                    barrier, inc=1, device_id=(row + side, lax.rem(col + k, cols_of)), device_id_type=MESH)

    for g in range(groups):
        pieces = []
        for a in range(2):
            for c in range(3):
                pieces.append(pix_ref[c, pl.ds(a, tile, stride=2), :][:, 16 * g : 16 * g + 16])
            pieces.append(jnp.zeros((tile, 16), F32))
        qsend[g] = jnp.concatenate(pieces, axis=1).astype(BF)

    own = pl.ds(pl.multiple_of(group * col, group), group)
    for t in range(9):
        i, r = table["f", t]
        wall[i, r, own, :] = final_ref[t]
    for n in range(3):
        i, r = table["e", n]
        taps = [entry_ref[4 * n + u] if 4 * n + u < 9 else jnp.zeros((group, feats), BF) for u in range(4)]
        wall[i, r, own, :] = jnp.concatenate(taps, axis=1)

    up_rows[...] = up_ref[...].astype(F32).transpose(1, 0, 2)
    padz[...] = jnp.zeros_like(padz)
    padf[...] = jnp.zeros_like(padf)

    def spread_up(m, carry):
        x = up_rows[pl.ds(4 * m, 4)].reshape(4 * group, cols)
        padz[EDGE : EDGE + cols, :] = x.T
        zsend[m] = padz[...].astype(BF)
        return carry

    lax.fori_loop(0, rows // 4, spread_up, 0)

    adj = not_first.astype(jnp.int32) + not_last.astype(jnp.int32)
    pl.semaphore_wait(barrier, (cols_of - 1) * (1 + adj) + rows_of - 1)

    sides = ((-1, not_first), (1, not_last))

    def pix_copy(k):
        return remote(qsend, pixbuf.at[pl.ds(1, groups), col], pix_s.at[k], pix_r.at[k],
                      (row, lax.rem(col + k, cols_of)))

    def pix_rim(side, k):
        at = 0 if side < 0 else 1
        return remote(qsend.at[0 if side < 0 else groups - 1],
                      pixbuf.at[groups + 1 if side < 0 else 0, col],
                      prim_s.at[at, k], prim_r.at[at, k], (row + side, lax.rem(col + k, cols_of)))

    fours = rows // 4

    def up_window(k):
        peer = lax.rem(col + k, cols_of)
        return peer, pl.ds(pl.multiple_of(peer * tile, tile), tile + 8)

    def up_copy(k):
        peer, window = up_window(k)
        return remote(zsend.at[:, window], zbuf.at[col, pl.ds(1, fours), pl.ds(0, tile + 8)],
                      up_s.at[k], up_r.at[k], (row, peer))

    def up_rim(side, k):
        at = 0 if side < 0 else 1
        peer, window = up_window(k)
        return remote(zsend.at[0 if side < 0 else fours - 1, window],
                      zbuf.at[col, fours + 1 if side < 0 else 0, pl.ds(0, tile + 8)],
                      urim_s.at[at, k], urim_r.at[at, k], (row + side, peer))

    def shard(z, c):
        return pl.ds(pl.multiple_of(group * (2 * z + c), group), group)

    def gather_a(part, k):
        at = wall.at[0, row, shard(chip, core)] if part == 0 else wall.at[pl.ds(1, slots - 1), row, shard(chip, core)]
        return remote(at, at, wa_s.at[part, k], wa_r.at[part, k],
                      (row, 2 * lax.rem(chip + k, chips) + core))

    def gather_b(part, k, z):
        here = shard(lax.rem(chip + z, chips), core)
        at = wall.at[0, row, here] if part == 0 else wall.at[pl.ds(1, slots - 1), row, here]
        return remote(at, at, wb_s.at[part, k, z], wb_r.at[part, k, z], (lax.rem(row + k, rows_of), col))

    def gather_c(part, z):
        here = shard(z, core)
        at = wall.at[0, :, here] if part == 0 else wall.at[pl.ds(1, slots - 1), :, here]
        return remote(at, at, wc_s.at[part, z], wc_r.at[part, z], (row, 2 * chip + 1 - core))

    for k in range(1, cols_of):
        pix_copy(k).start()
    for side, there in sides:

        @pl.when(there)
        def _():
            for k in range(cols_of):
                pix_rim(side, k).start()

    for part in range(2):
        for k in range(1, chips):
            gather_a(part, k).start()
    pixbuf[pl.ds(1, groups), col] = qsend[...]
    zbuf[:, :, tile + 8 :, :] = jnp.zeros((cols_of, fours + 2, win - tile - 8, 4 * group), BF)
    zbuf[col, pl.ds(1, fours), 0 : tile + 8] = zsend[:, pl.ds(wfrom, tile + 8)]

    @pl.when(row == 0)
    def _():
        pixbuf[0] = jnp.zeros(pixbuf.shape[1:], BF)
        zbuf[:, 0] = jnp.zeros((cols_of,) + zbuf.shape[2:], BF)

    @pl.when(row == rows_of - 1)
    def _():
        pixbuf[groups + 1] = jnp.zeros(pixbuf.shape[1:], BF)
        zbuf[:, fours + 1] = jnp.zeros((cols_of,) + zbuf.shape[2:], BF)

    spot = lax.broadcasted_iota(jnp.int32, (128, 48), 0)
    want = lax.broadcasted_iota(jnp.int32, (128, 48), 1)
    la, lc, lr, lb = spot // 64, (spot // 16) % 4, (spot // 4) % 4, spot % 4
    for v in range(4):
        d = (lr + (5 - v)) % 4 - 1
        for s in range(3):
            q = 2 * (s - 1) + la + 1
            parts = []
            for e in range(2):
                p = 4 * d + lb - 2 * e + 1
                fits = (lc < 3) & (p >= 0) & (p < 4) & (q >= 0) & (q < 4)
                hot = (fits & (want == lc * 16 + p * 4 + q)).astype(F32).astype(BF)
                onehot[2 * s + e, 128 * v : 128 * v + 128, :] = hot
                parts.append(jnp.dot(hot, stem_ref[...], preferred_element_type=F32))
            stem_mat[v, :, 2 * feats * s : 2 * feats * (s + 1)] = jnp.concatenate(parts, axis=1).astype(BF)

    zero = jnp.zeros((feats, feats), F32)
    for w_ref, fwd, bwd in ((first_ref, fwd1, bwd1), (second_ref, fwd2, bwd2)):
        for q in range(3):
            w = [w_ref[3 * p + q].astype(F32) for p in range(3)]
            even = jnp.concatenate([w[1], w[2], zero, w[0]], axis=1)
            odd = jnp.concatenate([w[0], w[1], w[2], zero], axis=1)
            both = jnp.concatenate([even, odd], axis=0)
            fwd[4 * feats * q : 4 * feats * (q + 1)] = both.T.astype(BF)
            lines = [[w[1], w[2]], [w[0], w[1]], [zero, w[0]], [w[2], zero]]
            back = jnp.concatenate([jnp.concatenate(line, axis=1) for line in lines], axis=0)
            bwd[4 * feats * q : 4 * feats * (q + 1)] = back.astype(BF)

    for at in (act0, act1, act2):
        for q in range(3):
            at[q, 0] = jnp.zeros((wide, 128), BF)
            at[q, pairs + 7] = jnp.zeros((wide, 128), BF)

    for k in range(1, cols_of):
        pix_copy(k).wait_recv()
    for side, there in sides:
        other = not_last if side < 0 else not_first

        @pl.when(other)
        def _():
            for k in range(cols_of):
                pix_rim(side, k).wait_recv()

    for g in range(groups + 2):
        padf[EDGE : EDGE + cols, :] = pixbuf[g].reshape(cols, 128).astype(F32)
        quads[g] = padf[...].astype(BF)

    for k in range(1, chips):
        gather_a(0, k).wait_recv()
    for k in range(1, rows_of):
        for z in range(1, chips):
            gather_b(0, k, z).start()
    for k in range(1, cols_of):
        up_copy(k).start()
    for side, there in sides:

        @pl.when(there)
        def _():
            for k in range(cols_of):
                up_rim(side, k).start()

    lane = lax.broadcasted_iota(jnp.int32, (1, 128), 1)
    upper = (lane >= feats).astype(jnp.int32)
    sub = lax.broadcasted_iota(jnp.int32, (wide, 1), 0) - EDGE
    in_cols = (sub >= 0) & (sub < cols)
    base = row * rows

    def in_rows(r):
        line = base + 2 * r + upper
        return (line >= 0) & (line < span)

    def put(dst, at, value):
        dst[0, at] = shift_up(value, 0).astype(BF)
        dst[1, at] = value.astype(BF)
        dst[2, at] = shift_down(value, 0).astype(BF)

    def stem_lhs(g, v, window):
        if v == 0:
            return jnp.where(lr_lane == 3, quads[g - 1, window, :], quads[g, window, :])
        if v == 3:
            return jnp.where(lr_lane == 0, quads[g + 1, window, :], quads[g, window, :])
        return quads[g, window, :]

    lr_lane = (lax.broadcasted_iota(jnp.int32, (1, 128), 1) // 4) % 4

    def stem_one(g, v):
        r = 4 * (g - 1) + v
        out = jnp.dot(stem_lhs(g, v, pl.ds(0, wide)), stem_mat[v], preferred_element_type=F32)
        n = 2 * feats
        pre = shift_up(out[:, :n], 0) + out[:, n : 2 * n] + shift_down(out[:, 2 * n :], 0)
        pre0[r + 3] = pre
        put(act0, r + 4, jnp.where(in_rows(r) & in_cols, silu(pre), 0.0))

    for v in (1, 2, 3):
        stem_one(0, v)

    def stem_group(g, carry):
        for v in range(4):
            stem_one(g, v)
        return carry

    lax.fori_loop(1, groups + 1, stem_group, 0)
    for v in (0, 1, 2):
        stem_one(groups + 1, v)

    low = lax.broadcasted_iota(jnp.int32, (1, 1, 128), 2) < feats

    def conv_lhs(src, at, n, window):
        size = window.size
        out = []
        for q in range(3):
            x = src[q, pl.ds(at, n), window, :]
            mix = jnp.where(low, src[q, pl.ds(at + 1, n), window, :], src[q, pl.ds(at - 1, n), window, :])
            out += [x.reshape(n * size, 128), mix.reshape(n * size, 128)]
        return out

    everything = pl.ds(0, wide)

    def conv(src, at, n, window, mat):
        parts = conv_lhs(src, at, n, window)
        lhs = jnp.concatenate(parts, axis=1)
        out = jnp.dot(lhs, mat, preferred_element_type=F32)
        return out.reshape(n, window.size, out.shape[1])

    def forward(src, mat, pre_ref, dst, first, count):
        def one(m, carry):
            r = first + 2 * m
            out = conv(src, r + 4, 2, everything, mat[...])
            for n in range(2):
                pre_ref[r + n + 3] = out[n]
                put(dst, r + n + 4, jnp.where(in_rows(r + n) & in_cols, silu(out[n]), 0.0))
            return carry

        lax.fori_loop(0, count // 2, one, 0)

    for k in range(1, chips):
        gather_a(1, k).wait_recv()
    for k in range(1, rows_of):
        for z in range(1, chips):
            gather_b(1, k, z).start()
    forward(act0, fwd1, pre1, act1, -3, pairs + 6)
    for k in range(1, rows_of):
        for z in range(1, chips):
            gather_b(0, k, z).wait_recv()
    for z in range(chips):
        gather_c(0, z).start()
    forward(act1, fwd2, pre2, act2, -2, pairs + 4)

    def spread_final(i, carry):
        x = up_rows[i]
        at = lax.broadcasted_iota(jnp.int32, x.shape, 1)
        left = jnp.where(at == cols - 1, 0.0, shift_down(x, 1))
        right = jnp.where(at == 0, 0.0, shift_up(x, 1))
        upq[i + 2] = jnp.concatenate([left, x, right], axis=0).astype(BF)
        return carry

    for i in (0, 1, rows + 2, rows + 3):
        upq[i] = jnp.zeros(upq.shape[1:], BF)
    lax.fori_loop(0, rows, spread_final, 0)

    for z in range(chips):
        gather_c(0, z).wait_recv()

    def entry_tap(t):
        i, r = table["e", t // 4]
        u = t % 4
        return wall[i, r, :, feats * u : feats * (u + 1)]

    none = jnp.zeros((tail, feats), F32)
    for q in range(3):
        w = [entry_tap(3 * p + q) for p in range(3)]
        wf = [x.astype(F32) for x in w]
        for e, line in enumerate(([wf[1], wf[2], none, wf[0]], [wf[0], wf[1], wf[2], none])):
            for h in range(2):
                block = jnp.concatenate(line[2 * h : 2 * h + 2], axis=1).T.astype(BF)
                entry_mat[e, 4 * feats * q + 2 * feats * h : 4 * feats * q + 2 * feats * (h + 1), :] = block
        nil = jnp.zeros((tail, feats), BF)
        for a, pair in enumerate(([w[2], nil], [w[1], w[2]], [w[0], w[1]], [nil, w[0]])):
            back_mat[tail * (4 * q + a) : tail * (4 * q + a + 1), :] = jnp.concatenate(pair, axis=1)

    def entry_step(m, carry):
        r = 2 * m - 2
        lhs = jnp.concatenate(conv_lhs(act2, r + 4, 2, everything), axis=1)
        for e in range(2):
            out = jnp.dot(lhs, entry_mat[e], preferred_element_type=F32).reshape(2, wide, tail)
            for n in range(2):
                line = base + 2 * (r + n) + e
                inside = (line >= 0) & (line < span)
                at = 2 * (r + n + 2) + e
                entry_pre[at] = out[n]
                moved = pltpu.roll(silu(out[n]), wide - EDGE, 0)[:cols]
                entry_act[at] = jnp.where(inside, moved, 0.0).astype(BF)
        return carry

    lax.fori_loop(0, pairs // 2 + 2, entry_step, 0)

    for k in range(1, rows_of):
        for z in range(1, chips):
            gather_b(1, k, z).wait_recv()
    for z in range(chips):
        gather_c(1, z).start()

    facc[...] = jnp.zeros_like(facc)
    three = 9 * group

    def final_step(m, carry):
        one = upq[pl.ds(2 * m, 3)].reshape(three, cols)
        two = upq[pl.ds(2 * m + 1, 3)].reshape(three, cols)
        rhs = entry_act[pl.ds(2 * m + 3, 2)].reshape(2 * cols, tail)
        facc[...] += jnp.dot(jnp.concatenate([one, two], axis=1), rhs, preferred_element_type=F32)
        return carry

    lax.fori_loop(0, rows // 2 + 1, final_step, 0)
    fgbuf[row] = (facc[...] * scale).astype(BF)

    def fg_copy(k):
        return remote(fgbuf.at[row], fgbuf.at[row], fg_s.at[k], fg_r.at[k], (lax.rem(row + k, rows_of), col))

    for k in range(1, rows_of):
        fg_copy(k).start()

    for k in range(1, cols_of):
        up_copy(k).wait_recv()
    for side, there in sides:
        other = not_last if side < 0 else not_first

        @pl.when(other)
        def _():
            for k in range(cols_of):
                up_rim(side, k).wait_recv()

    def unpack_up(m, carry):
        got = [zbuf[s, m].astype(F32) for s in range(cols_of)]
        for r in range(4):
            x = jnp.concatenate([z[:, group * r : group * (r + 1)] for z in got], axis=1)
            at = 4 * m + r
            up3[0, at] = shift_down(x, 0).astype(BF)
            up3[1, at] = x.astype(BF)
            up3[2, at] = shift_up(x, 0).astype(BF)
        return carry

    lax.fori_loop(0, fours + 2, unpack_up, 0)
    for z in range(chips):
        gather_c(1, z).wait_recv()

    wsub = lax.broadcasted_iota(jnp.int32, (win, 1), 0) - EDGE
    wcol = wsub + wfrom
    win_cols = (wcol >= 0) & (wcol < cols)
    mine = (wsub >= 0) & (wsub < tile)
    window = pl.ds(wfrom, win)

    def put_back(dst, at, value):
        lead = at if isinstance(at, tuple) else (at,)
        dst[(0,) + lead] = shift_down(value, 0).astype(BF)
        dst[(1,) + lead] = value.astype(BF)
        dst[(2,) + lead] = shift_up(value, 0).astype(BF)

    lot = 10 if (rows + 6) % 10 == 0 else 2

    def entry_back(m, carry):
        k0 = m * lot
        total = jnp.zeros((lot * win, tail), F32)
        for p in range(3):
            for q in range(3):
                i, r = table["f", 3 * p + q]
                lhs = up3[q, pl.ds(k0 + 2 - p, lot)].reshape(lot * win, tail)
                total = total + jnp.dot(lhs, wall[i, r], preferred_element_type=F32)
        total = total.reshape(lot, win, tail)
        for n in range(lot):
            k = k0 + n
            line = base + k - 3
            inside = (line >= 0) & (line < span) & win_cols
            delta = jnp.where(inside, total[n] * slope(entry_pre[k + 1, window, :]), 0.0)
            put_back(ed3, (lax.div(k, 2), lax.rem(k, 2)), delta)
        return carry

    lax.fori_loop(0, (rows + 6) // lot, entry_back, 0)

    def grad_lhs(src, at):
        x = src[1, pl.ds(at, pairs)]
        return jnp.where(mine, x, jnp.zeros_like(x)).reshape(pairs * win, 2 * feats)

    def grad_taps(src, q):
        x = src[q, pl.ds(4, pairs), window, :]
        mix = jnp.where(low, src[q, pl.ds(5, pairs), window, :], src[q, pl.ds(3, pairs), window, :])
        return jnp.concatenate([x.reshape(pairs * win, 128), mix.reshape(pairs * win, 128)], axis=1)

    def outer(lhs, rhs):
        return lax.dot_general(lhs, rhs, (((0,), (0,)), ((), ())), preferred_element_type=F32) * scale

    f = feats

    some = 7 if (pairs + 2) % 7 == 0 else 2

    def second_back(m, carry):
        r0 = m * some
        total = jnp.zeros((some * win, 2 * feats), F32)
        for q in range(3):
            for a in range(4):
                lhs = ed3[q, pl.ds(r0 + a // 2, some), a % 2].reshape(some * win, tail)
                at = tail * (4 * q + a)
                total = total + jnp.dot(lhs, back_mat[at : at + tail, :], preferred_element_type=F32)
        total = total.reshape(some, win, 2 * feats)
        for n in range(some):
            r = r0 + n - 1
            inside = in_rows(r) & win_cols
            put_back(sd3, r + 2, jnp.where(inside, total[n] * slope(pre2[r + 3, window, :]), 0.0))
        return carry

    for q in range(3):
        sd3[q, 0] = jnp.zeros((win, 128), BF)
        sd3[q, pairs + 3] = jnp.zeros((win, 128), BF)
    lax.fori_loop(0, (pairs + 2) // some, second_back, 0)

    def pair_grads(src, delta):
        out = {}
        for q in range(3):
            g = outer(delta, grad_taps(src, q))
            out[0, q] = g[:f, 3 * f :] + g[f:, :f]
            out[1, q] = g[:f, :f] + g[f:, f : 2 * f]
            out[2, q] = g[:f, f : 2 * f] + g[f:, 2 * f : 3 * f]
        return out

    whole = pl.ds(0, win)

    def stage(dst, taps):
        for t in range(0, len(taps), 2):
            both = jnp.concatenate(taps[t : t + 2], axis=1)
            dst[:, t // 2] = both.reshape(cols_of, feats // cols_of, 2 * f).astype(BF)

    def chain(sent, got, mid, every, last, out, sems):
        s1, r1, s2, r2, s3, r3 = sems

        def first_copy(k):
            peer = lax.rem(col + k, cols_of)
            return remote(sent.at[peer], got.at[k], s1.at[k], r1.at[k], (row, peer))

        def second_copy(k):
            return remote(mid, every.at[row], s2.at[k], r2.at[k], (lax.rem(row + k, rows_of), col))

        def third_copy(k):
            return remote(last, out.at[col], s3.at[k], r3.at[k], (row, lax.rem(col + k, cols_of)))

        return first_copy, second_copy, third_copy

    a_copies = chain(sas, sar, sam, saa, saf, sa_out, (a1_s, a1_r, a2_s, a2_r, a3_s, a3_r))
    b_copies = chain(sbs, sbr, sbm, sba, sbf, sb_out, (b1_s, b1_r, b2_s, b2_r, b3_s, b3_r))
    blank = jnp.zeros((f, f), F32)
    second_grads = pair_grads(act1, grad_lhs(sd3, 2))
    stage(sas, [second_grads[t // 3, t % 3] for t in range(9)] + [blank])
    for k in range(1, cols_of):
        a_copies[0](k).start()

    def first_back(m, carry):
        r0 = m * some
        out = conv(sd3, r0 + 1, some, whole, bwd2[...])
        for n in range(some):
            r = r0 + n - 1
            inside = in_rows(r) & win_cols
            put_back(fd3, r + 1, jnp.where(inside, out[n] * slope(pre1[r + 3, window, :]), 0.0))
        return carry

    lax.fori_loop(0, (pairs + 2) // some, first_back, 0)
    first_grads = pair_grads(act0, grad_lhs(fd3, 1))

    few = 6 if pairs % 6 == 0 else 2

    def stem_back(m, carry):
        r0 = m * few
        out = conv(fd3, r0 + 1, few, whole, bwd1[...])
        for n in range(few):
            r = r0 + n
            delta = jnp.where(mine, out[n] * slope(pre0[r + 3, window, :]), 0.0)
            td3[r] = jnp.concatenate(
                [shift_down(delta, 0), delta, shift_up(delta, 0)], axis=1).astype(BF)
        return carry

    lax.fori_loop(0, pairs // few, stem_back, 0)
    moments = []
    for v in range(4):
        lhs = jnp.concatenate([stem_lhs(g, v, window) for g in range(1, groups + 1)], axis=0)
        rhs = jnp.concatenate([td3[4 * g + v] for g in range(groups)], axis=0)
        moments.append(outer(lhs, rhs))
    moment = jnp.concatenate(moments, axis=0)
    total = jnp.zeros((feats, 48), F32)
    for s in range(3):
        for e in range(2):
            part = moment[:, 2 * f * s + f * e : 2 * f * s + f * (e + 1)].astype(BF)
            total = total + lax.dot_general(
                part, onehot[2 * s + e], (((0,), (0,)), ((), ())), preferred_element_type=F32)
    total = jnp.concatenate([total, jnp.zeros((feats, f - 48), F32)], axis=1)
    stage(sbs, [first_grads[t // 3, t % 3] for t in range(9)] + [total])
    for k in range(1, cols_of):
        b_copies[0](k).start()

    def entry_own(e):
        x = ed3[1, pl.ds(1 + e, pairs), 1 - e]
        return jnp.where(mine, x, jnp.zeros_like(x)).reshape(pairs * win, tail)

    own_even, own_odd = entry_own(0), entry_own(1)
    grads = {}
    for q in range(3):
        taps = grad_taps(act2, q)
        ge, go = outer(own_even, taps), outer(own_odd, taps)
        grads[0, q] = ge[:, 3 * f :] + go[:, :f]
        grads[1, q] = ge[:, :f] + go[:, f : 2 * f]
        grads[2, q] = ge[:, f : 2 * f] + go[:, 2 * f : 3 * f]
    quarter = group // rows_of
    for t in range(0, 9, 2):
        two = [grads[(t + u) // 3, (t + u) % 3] if t + u < 9 else jnp.zeros((tail, f), F32) for u in range(2)]
        both = jnp.concatenate(two, axis=1).reshape(cols_of, rows_of, quarter, 2 * f)
        for r in range(rows_of):
            egs[r, :, t // 2] = both[:, r].astype(BF)

    def e1_copy(k):
        peer = lax.rem(row + k, rows_of)
        return remote(egs.at[peer], egr.at[k], e1_s.at[k], e1_r.at[k], (peer, col))

    def e2_copy(k):
        peer = lax.rem(col + k, cols_of)
        return remote(egm.at[peer], egq.at[k], e2_s.at[k], e2_r.at[k], (row, peer))

    def e3_copy(k):
        return remote(egn, eg_out.at[row], e3_s.at[k], e3_r.at[k], (lax.rem(row + k, rows_of), col))

    for k in range(1, rows_of):
        e1_copy(k).start()

    def summed(mine_value, got, copy, count):
        acc = mine_value.astype(F32)
        for k in range(1, count):
            copy(k).wait_recv()
            acc = acc + got[k].astype(F32)
        return acc.astype(BF)

    for (one_copy, two_copy, _), sent, got, mid, every in (
        (a_copies, sas, sar, sam, saa), (b_copies, sbs, sbr, sbm, sba)):
        value = summed(sent[col], got, one_copy, cols_of)
        mid[...] = value
        every[row] = value
        for k in range(1, rows_of):
            two_copy(k).start()
    egm[...] = summed(egs[row], egr, e1_copy, rows_of)
    for k in range(1, cols_of):
        e2_copy(k).start()
    for (_, two_copy, three_copy), every, last, out in (
        (a_copies, saa, saf, sa_out), (b_copies, sba, sbf, sb_out)):
        for k in range(1, rows_of):
            two_copy(k).wait_recv()
        acc = every[0].astype(F32)
        for r in range(1, rows_of):
            acc = acc + every[r].astype(F32)
        value = acc.astype(BF)
        last[...] = value
        out[col] = value
        for k in range(1, cols_of):
            three_copy(k).start()
    value = summed(egm[col], egq, e2_copy, cols_of)
    egn[...] = value
    eg_out[row] = value
    for k in range(1, rows_of):
        e3_copy(k).start()
    for k in range(1, rows_of):
        fg_copy(k).wait_recv()

    def final_sum(t, carry):
        at = pl.ds(t * group, group)
        acc = fgbuf[0, at].astype(F32)
        for r in range(1, rows_of):
            acc = acc + fgbuf[r, at].astype(F32)
        fg_out[at] = acc
        return carry

    lax.fori_loop(0, 9, final_sum, 0)

    for part in range(2):
        for k in range(1, chips):
            gather_a(part, k).wait_send()
        for k in range(1, rows_of):
            for z in range(1, chips):
                gather_b(part, k, z).wait_send()
        for z in range(chips):
            gather_c(part, z).wait_send()
    for k in range(1, cols_of):
        pix_copy(k).wait_send()
        up_copy(k).wait_send()
        a_copies[0](k).wait_send()
        b_copies[0](k).wait_send()
        e2_copy(k).wait_send()
    for side, there in sides:

        @pl.when(there)
        def _():
            for k in range(cols_of):
                pix_rim(side, k).wait_send()
                up_rim(side, k).wait_send()

    for k in range(1, rows_of):
        fg_copy(k).wait_send()
        e1_copy(k).wait_send()
        a_copies[1](k).wait_send()
        b_copies[1](k).wait_send()
        e3_copy(k).wait()
    for k in range(1, cols_of):
        a_copies[2](k).wait()
        b_copies[2](k).wait()


def step(pix, stem, first, second, entry, final, up, tile, scale):
    rows_of, cols_of = lax.axis_size("row"), lax.axis_size("col")
    group, rows, cols = up.shape
    feats, tail = first.shape[1], final.shape[2]
    dims = (rows_of, cols_of, rows, cols, tile, group, feats, tail, scale)
    groups, wide, win, pairs, fours = rows // 8, cols + 16, tile + 16, rows // 2, rows // 4
    slots, _ = slab_table(rows_of)
    chips, share, quarter = cols_of // 2, feats // cols_of, group // rows_of
    act = pltpu.VMEM((3, pairs + 8, wide, 128), BF)
    pre = pltpu.VMEM((pairs + 6, wide, 128), F32)
    dma = pltpu.SemaphoreType.DMA
    mat = pltpu.VMEM((12 * feats, 2 * feats), BF)

    def vm(*shape, kind=BF):
        return pltpu.VMEM(shape, kind)

    scratch = [
        vm(groups, tile, 128), vm(groups + 2, cols_of, tile, 128), vm(groups + 2, wide, 128),
        vm(wide, 128, kind=F32), vm(wide, 4 * group, kind=F32), vm(4, 128, 6 * feats), vm(6, 512, 48),
        mat, mat, mat, mat, vm(2, 12 * feats, tail),
        vm(12 * tail, 2 * feats), act, act, act, pre, pre, pre,
        vm(rows + 8, cols, tail), vm(rows + 8, wide, tail, kind=F32),
        vm(rows + 4, 3 * group, cols), vm(9 * group, tail, kind=F32),
        vm(rows, group, cols, kind=F32),
        vm(fours, wide, 4 * group), vm(cols_of, fours + 2, win, 4 * group),
        vm(3, rows + 8, win, tail), vm(3, pairs + 3, 2, win, tail),
        vm(3, pairs + 4, win, 128), vm(3, pairs + 2, win, 128), vm(pairs, win, 384),
        vm(slots, rows_of, tail, tail),
        vm(rows_of, 9 * group, tail),
        vm(rows_of, cols_of, 5, quarter, 128), vm(rows_of, cols_of, 5, quarter, 128), vm(cols_of, 5, quarter, 128),
        vm(cols_of, 5, quarter, 128), vm(5, quarter, 128),
        vm(cols_of, 5, share, 128), vm(cols_of, 5, share, 128), vm(5, share, 128),
        vm(rows_of, 5, share, 128), vm(5, share, 128),
        vm(cols_of, 5, share, 128), vm(cols_of, 5, share, 128), vm(5, share, 128),
        vm(rows_of, 5, share, 128), vm(5, share, 128),
    ]
    for shape in (
        (cols_of,), (2, cols_of), (cols_of,), (2, cols_of), (2, chips), (2, rows_of, chips), (2, chips), (rows_of,),
        (rows_of,), (cols_of,), (rows_of,),
        (cols_of,), (rows_of,), (cols_of,), (cols_of,), (rows_of,), (cols_of,),
    ):
        scratch += [dma(shape), dma(shape)]
    return pl.pallas_call(
        functools.partial(step_kernel, dims),
        out_shape=(
            jax.ShapeDtypeStruct((9 * group, tail), F32),
            jax.ShapeDtypeStruct((rows_of, 5, quarter, 128), BF),
            jax.ShapeDtypeStruct((cols_of, 5, share, 128), BF),
            jax.ShapeDtypeStruct((cols_of, 5, share, 128), BF),
        ),
        in_specs=[VMEM] * 7,
        out_specs=(VMEM,) * 4,
        scratch_shapes=scratch,
        compiler_params=pltpu.CompilerParams(
            collective_id=0, has_side_effects=True, vmem_limit_bytes=58 * 1024 * 1024),
    )(pix, stem, first, second, entry, final, up)


def finish_kernel(fg_ref, eg_ref, sa_ref, sb_ref, stem_out, first_out, second_out, entry_out, final_out):
    group, feats = entry_out.shape[1:]
    for p in range(3):
        for q in range(3):
            at = ((2 - p) * 3 + q) * group
            final_out[3 * p + q] = fg_ref[at : at + group]
    for t in range(5):
        entry = eg_ref[:, t].astype(F32).reshape(group, 2 * feats)
        second = sa_ref[:, t].astype(F32).reshape(feats, 2 * feats)
        first = sb_ref[:, t].astype(F32).reshape(feats, 2 * feats)
        for u in range(2):
            if 2 * t + u < 9:
                half = slice(u * feats, (u + 1) * feats)
                entry_out[2 * t + u] = entry[:, half]
                second_out[2 * t + u] = second[:, half]
                first_out[2 * t + u] = first[:, half]
    stem_out[...] = first.T[feats : feats + stem_out.shape[0]]


def finish(fg, eg, sa, sb, feats):
    group, tail = fg.shape[0] // 9, fg.shape[1]
    return pl.pallas_call(
        finish_kernel,
        out_shape=(
            jax.ShapeDtypeStruct((48, feats), F32),
            jax.ShapeDtypeStruct((9, feats, feats), F32),
            jax.ShapeDtypeStruct((9, feats, feats), F32),
            jax.ShapeDtypeStruct((9, group, feats), F32),
            jax.ShapeDtypeStruct((9, group, tail), F32),
        ),
        in_specs=[VMEM] * 4,
        out_specs=(VMEM,) * 5,
    )(fg, eg, sa, sb)


def per_device(pixels, stem_weight, first_weight, second_weight, entry_weight, final_weight, upstream):
    chans, pix_rows, pix_cols = pixels.shape
    rows, tile = pix_rows // 2, pix_cols // 2
    cols = tile * lax.axis_size("col")
    scale = 1.0 / math.sqrt(rows * lax.axis_size("row") * cols)

    def flat(kernel):
        return kernel.transpose(2, 3, 0, 1).reshape(9, kernel.shape[0], kernel.shape[1])

    stem = stem_weight.transpose(1, 2, 3, 0).reshape(chans * 16, stem_weight.shape[0])
    fg, eg, sa, sb = step(
        pixels.transpose(0, 2, 1), stem, flat(first_weight), flat(second_weight), flat(entry_weight),
        flat(final_weight), upstream, tile, scale)
    stem_grad, first_grad, second_grad, entry_grad, final_grad = finish(fg, eg, sa, sb, stem_weight.shape[0])

    def taps_last(grad):
        return grad.reshape(3, 3, grad.shape[1], grad.shape[2]).transpose(2, 3, 0, 1)

    return (
        stem_grad.reshape(chans, 4, 4, -1).transpose(3, 0, 1, 2),
        taps_last(first_grad),
        taps_last(second_grad),
        taps_last(entry_grad),
        taps_last(final_grad),
    )


def solution(mesh):
    return jax.shard_map(
        per_device,
        mesh=mesh,
        in_specs=(
            P(None, "row", "col"),
            P(),
            P(),
            P(),
            P("col", None, None, None),
            P("col", None, None, None),
            P("col", "row", None),
        ),
        out_specs=(P(), P(), P(), P("col", None, None, None), P("col", None, None, None)),
        check_vma=False,
    )
```

```python
import functools
import math

import jax
import jax.numpy as jnp
from jax import lax
from jax.experimental import pallas as pl
from jax.experimental.pallas import tpu as pltpu
from jax.sharding import PartitionSpec as P

BF = jnp.bfloat16
F32 = jnp.float32
MESH = pl.DeviceIdType.MESH
VMEM = pl.BlockSpec(memory_space=pltpu.VMEM)
ANY = pl.BlockSpec(memory_space=pl.ANY)
EDGE = 4
SLABS = 12


def silu(v):
    h = 0.5 * v
    return h + h * jnp.tanh(h)


def slope(v):
    h = 0.5 * v
    t = jnp.tanh(h)
    return (0.5 + 0.5 * t) * (1.0 + h * (1.0 - t))


def slab_table(rows_of):
    slots = -(-SLABS // rows_of)
    table, free = {}, [(i, r) for i in range(slots) for r in range(rows_of)]
    for n in range(3):
        table["e", n] = free.pop(0)
    free.sort(key=lambda at: (at[1], at[0]))
    for n in range(9):
        table["f", n] = free.pop(0)
    return slots, table


def shift_up(v, axis):
    return pltpu.roll(v, 1, axis)


def shift_down(v, axis):
    return pltpu.roll(v, v.shape[axis] - 1, axis)


def step_kernel(dims, *refs):
    rows_of, cols_of, rows, cols, tile, group, feats, tail, scale = dims
    given = refs[:7]
    fg_out, eg_out, sa_out, sb_out = refs[7:11]
    (pix_ref, stem_ref, first_ref, second_ref, entry_ref, final_ref, up_ref, in_sem, out_sem,
     qsend, pixbuf, quads, padf, padz, stem_mat, onehot, fwd1, fwd2, bwd1, bwd2, entry_mat,
     back_mat, act0, act1, act2, pre0, pre1, pre2, entry_act, entry_pre, upq, facc,
     up_rows, zsend, zbuf, up3, ed3, sd3, fd3, td3, wall, fgbuf,
     egs, egr, egm, egq, egn, sas, sar, sam, saa, saf, sbs, sbr, sbm, sba, sbf,
     pix_s, pix_r, prim_s, prim_r, up_s, up_r, urim_s, urim_r,
     wa_s, wa_r, wb_s, wb_r, wc_s, wc_r, fg_s, fg_r,
     e1_s, e1_r, e2_s, e2_r, e3_s, e3_r,
     a1_s, a1_r, a2_s, a2_r, a3_s, a3_r, b1_s, b1_r, b2_s, b2_r, b3_s, b3_r) = refs[11:]

    row, col = lax.axis_index("row"), lax.axis_index("col")
    core, chip = lax.rem(col, 2), lax.div(col, 2)
    chips = cols_of // 2
    groups = rows // 8
    wide, win = cols + 16, tile + 16
    span = rows * rows_of
    pairs = rows // 2
    wfrom = pl.multiple_of(col * tile, tile)
    not_first, not_last = row > 0, row < rows_of - 1
    slots, table = slab_table(rows_of)

    def remote(src, dst, send, recv, peer):
        return pltpu.make_async_remote_copy(
            src_ref=src, dst_ref=dst, send_sem=send, recv_sem=recv,
            device_id=peer, device_id_type=MESH)

    loads = {}
    for n, (src, dst) in enumerate(zip(
        given, (pix_ref, stem_ref, first_ref, second_ref, entry_ref, final_ref, up_ref))):
        loads[n] = pltpu.make_async_copy(src, dst, in_sem.at[n])
    for n in (0, 6, 4, 5, 1, 2, 3):
        loads[n].start()

    barrier = pltpu.get_barrier_semaphore()
    for k in range(1, cols_of):
        pl.semaphore_signal(barrier, inc=1, device_id=(row, lax.rem(col + k, cols_of)), device_id_type=MESH)
    for k in range(1, rows_of):
        pl.semaphore_signal(barrier, inc=1, device_id=(lax.rem(row + k, rows_of), col), device_id_type=MESH)
    for side, there in ((-1, not_first), (1, not_last)):

        @pl.when(there)
        def _():
            for k in range(1, cols_of):
                pl.semaphore_signal(
                    barrier, inc=1, device_id=(row + side, lax.rem(col + k, cols_of)), device_id_type=MESH)

    loads[0].wait()
    for g in range(groups):
        pieces = []
        for a in range(2):
            for c in range(3):
                pieces.append(pix_ref[c, pl.ds(a, tile, stride=2), :][:, 16 * g : 16 * g + 16])
            pieces.append(jnp.zeros((tile, 16), F32))
        qsend[g] = jnp.concatenate(pieces, axis=1).astype(BF)

    loads[4].wait()
    loads[5].wait()
    own = pl.ds(pl.multiple_of(group * col, group), group)
    for t in range(9):
        i, r = table["f", t]
        wall[i, r, own, :] = final_ref[t]
    for n in range(3):
        i, r = table["e", n]
        taps = [entry_ref[4 * n + u] if 4 * n + u < 9 else jnp.zeros((group, feats), BF) for u in range(4)]
        wall[i, r, own, :] = jnp.concatenate(taps, axis=1)

    loads[6].wait()
    up_rows[...] = up_ref[...].astype(F32).transpose(1, 0, 2)
    padz[...] = jnp.zeros_like(padz)
    padf[...] = jnp.zeros_like(padf)

    def spread_up(m, carry):
        x = up_rows[pl.ds(4 * m, 4)].reshape(4 * group, cols)
        padz[EDGE : EDGE + cols, :] = x.T
        zsend[m] = padz[...].astype(BF)
        return carry

    lax.fori_loop(0, rows // 4, spread_up, 0)

    adj = not_first.astype(jnp.int32) + not_last.astype(jnp.int32)
    pl.semaphore_wait(barrier, (cols_of - 1) * (1 + adj) + rows_of - 1)

    sides = ((-1, not_first), (1, not_last))

    def pix_copy(k):
        return remote(qsend, pixbuf.at[pl.ds(1, groups), col], pix_s.at[k], pix_r.at[k],
                      (row, lax.rem(col + k, cols_of)))

    def pix_rim(side, k):
        at = 0 if side < 0 else 1
        return remote(qsend.at[0 if side < 0 else groups - 1],
                      pixbuf.at[groups + 1 if side < 0 else 0, col],
                      prim_s.at[at, k], prim_r.at[at, k], (row + side, lax.rem(col + k, cols_of)))

    fours = rows // 4

    def up_window(k):
        peer = lax.rem(col + k, cols_of)
        return peer, pl.ds(pl.multiple_of(peer * tile, tile), tile + 8)

    def up_copy(k):
        peer, window = up_window(k)
        return remote(zsend.at[:, window], zbuf.at[col, pl.ds(1, fours), pl.ds(0, tile + 8)],
                      up_s.at[k], up_r.at[k], (row, peer))

    def up_rim(side, k):
        at = 0 if side < 0 else 1
        peer, window = up_window(k)
        return remote(zsend.at[0 if side < 0 else fours - 1, window],
                      zbuf.at[col, fours + 1 if side < 0 else 0, pl.ds(0, tile + 8)],
                      urim_s.at[at, k], urim_r.at[at, k], (row + side, peer))

    def shard(z, c):
        return pl.ds(pl.multiple_of(group * (2 * z + c), group), group)

    def gather_a(part, k):
        at = wall.at[0, row, shard(chip, core)] if part == 0 else wall.at[pl.ds(1, slots - 1), row, shard(chip, core)]
        return remote(at, at, wa_s.at[part, k], wa_r.at[part, k],
                      (row, 2 * lax.rem(chip + k, chips) + core))

    def gather_b(part, k, z):
        here = shard(lax.rem(chip + z, chips), core)
        at = wall.at[0, row, here] if part == 0 else wall.at[pl.ds(1, slots - 1), row, here]
        return remote(at, at, wb_s.at[part, k, z], wb_r.at[part, k, z], (lax.rem(row + k, rows_of), col))

    def gather_c(part, z):
        here = shard(z, core)
        at = wall.at[0, :, here] if part == 0 else wall.at[pl.ds(1, slots - 1), :, here]
        return remote(at, at, wc_s.at[part, z], wc_r.at[part, z], (row, 2 * chip + 1 - core))

    for k in range(1, cols_of):
        pix_copy(k).start()
    for side, there in sides:

        @pl.when(there)
        def _():
            for k in range(cols_of):
                pix_rim(side, k).start()

    for part in range(2):
        for k in range(1, chips):
            gather_a(part, k).start()
    pixbuf[pl.ds(1, groups), col] = qsend[...]
    zbuf[:, :, tile + 8 :, :] = jnp.zeros((cols_of, fours + 2, win - tile - 8, 4 * group), BF)
    zbuf[col, pl.ds(1, fours), 0 : tile + 8] = zsend[:, pl.ds(wfrom, tile + 8)]

    @pl.when(row == 0)
    def _():
        pixbuf[0] = jnp.zeros(pixbuf.shape[1:], BF)
        zbuf[:, 0] = jnp.zeros((cols_of,) + zbuf.shape[2:], BF)

    @pl.when(row == rows_of - 1)
    def _():
        pixbuf[groups + 1] = jnp.zeros(pixbuf.shape[1:], BF)
        zbuf[:, fours + 1] = jnp.zeros((cols_of,) + zbuf.shape[2:], BF)

    for n in (1, 2, 3):
        loads[n].wait()
    spot = lax.broadcasted_iota(jnp.int32, (128, 48), 0)
    want = lax.broadcasted_iota(jnp.int32, (128, 48), 1)
    la, lc, lr, lb = spot // 64, (spot // 16) % 4, (spot // 4) % 4, spot % 4
    d = (lr + 1) % 4 - 1
    base_mat = []
    for s in range(3):
        q = 2 * (s - 1) + la + 1
        for e in range(2):
            p = 4 * d + lb - 2 * e + 1
            fits = (lc < 3) & (p >= 0) & (p < 4) & (q >= 0) & (q < 4)
            hot = (fits & (want == lc * 16 + p * 4 + q)).astype(F32).astype(BF)
            onehot[2 * s + e] = hot
            base_mat.append(jnp.dot(hot, stem_ref[...], preferred_element_type=F32))
    for s in range(3):
        pair = jnp.concatenate(base_mat[2 * s : 2 * s + 2], axis=1).reshape(8, 16, 2 * feats)
        for v in range(4):
            turned = pltpu.roll(pair, 4 * v, 1) if v else pair
            stem_mat[v, :, 2 * feats * s : 2 * feats * (s + 1)] = turned.reshape(128, 2 * feats).astype(BF)

    zero = jnp.zeros((feats, feats), F32)
    for w_ref, fwd, bwd in ((first_ref, fwd1, bwd1), (second_ref, fwd2, bwd2)):
        for q in range(3):
            w = [w_ref[3 * p + q].astype(F32) for p in range(3)]
            even = jnp.concatenate([w[1], w[2], zero, w[0]], axis=1)
            odd = jnp.concatenate([w[0], w[1], w[2], zero], axis=1)
            both = jnp.concatenate([even, odd], axis=0)
            fwd[4 * feats * q : 4 * feats * (q + 1)] = both.T.astype(BF)
            lines = [[w[1], w[2]], [w[0], w[1]], [zero, w[0]], [w[2], zero]]
            back = jnp.concatenate([jnp.concatenate(line, axis=1) for line in lines], axis=0)
            bwd[4 * feats * q : 4 * feats * (q + 1)] = back.astype(BF)

    for at in (act0, act1, act2):
        for q in range(3):
            at[q, 0] = jnp.zeros((wide, 128), BF)
            at[q, pairs + 7] = jnp.zeros((wide, 128), BF)

    for k in range(1, cols_of):
        pix_copy(k).wait_recv()
    for side, there in sides:
        other = not_last if side < 0 else not_first

        @pl.when(other)
        def _():
            for k in range(cols_of):
                pix_rim(side, k).wait_recv()

    for g in range(groups + 2):
        padf[EDGE : EDGE + cols, :] = pixbuf[g].reshape(cols, 128).astype(F32)
        quads[g] = padf[...].astype(BF)

    for k in range(1, chips):
        gather_a(0, k).wait_recv()
    for k in range(1, rows_of):
        for z in range(1, chips):
            gather_b(0, k, z).start()
    for k in range(1, cols_of):
        up_copy(k).start()
    for side, there in sides:

        @pl.when(there)
        def _():
            for k in range(cols_of):
                up_rim(side, k).start()

    lane = lax.broadcasted_iota(jnp.int32, (1, 128), 1)
    upper = (lane >= feats).astype(jnp.int32)
    sub = lax.broadcasted_iota(jnp.int32, (wide, 1), 0) - EDGE
    in_cols = (sub >= 0) & (sub < cols)
    base = row * rows

    def in_rows(r):
        line = base + 2 * r + upper
        return (line >= 0) & (line < span)

    def put(dst, at, value):
        dst[0, at] = shift_up(value, 0).astype(BF)
        dst[1, at] = value.astype(BF)
        dst[2, at] = shift_down(value, 0).astype(BF)

    def stem_lhs(g, v, window):
        if v == 0:
            return jnp.where(lr_lane == 3, quads[g - 1, window, :], quads[g, window, :])
        if v == 3:
            return jnp.where(lr_lane == 0, quads[g + 1, window, :], quads[g, window, :])
        return quads[g, window, :]

    lr_lane = (lax.broadcasted_iota(jnp.int32, (1, 128), 1) // 4) % 4

    def stem_one(g, v):
        r = 4 * (g - 1) + v
        out = jnp.dot(stem_lhs(g, v, pl.ds(0, wide)), stem_mat[v], preferred_element_type=F32)
        n = 2 * feats
        pre = shift_up(out[:, :n], 0) + out[:, n : 2 * n] + shift_down(out[:, 2 * n :], 0)
        pre0[r + 3] = pre
        put(act0, r + 4, jnp.where(in_rows(r) & in_cols, silu(pre), 0.0))

    for v in (1, 2, 3):
        stem_one(0, v)

    def stem_group(g, carry):
        for v in range(4):
            stem_one(g, v)
        return carry

    lax.fori_loop(1, groups + 1, stem_group, 0)
    for v in (0, 1, 2):
        stem_one(groups + 1, v)

    low = lax.broadcasted_iota(jnp.int32, (1, 1, 128), 2) < feats

    def conv_lhs(src, at, n, window):
        size = window.size
        out = []
        for q in range(3):
            x = src[q, pl.ds(at, n), window, :]
            mix = jnp.where(low, src[q, pl.ds(at + 1, n), window, :], src[q, pl.ds(at - 1, n), window, :])
            out += [x.reshape(n * size, 128), mix.reshape(n * size, 128)]
        return out

    everything = pl.ds(0, wide)

    def conv(src, at, n, window, mat):
        parts = conv_lhs(src, at, n, window)
        lhs = jnp.concatenate(parts, axis=1)
        out = jnp.dot(lhs, mat, preferred_element_type=F32)
        return out.reshape(n, window.size, out.shape[1])

    def forward(src, mat, pre_ref, dst, first, count):
        def one(m, carry):
            r = first + 2 * m
            out = conv(src, r + 4, 2, everything, mat[...])
            for n in range(2):
                pre_ref[r + n + 3] = out[n]
                put(dst, r + n + 4, jnp.where(in_rows(r + n) & in_cols, silu(out[n]), 0.0))
            return carry

        lax.fori_loop(0, count // 2, one, 0, unroll=2)

    for k in range(1, chips):
        gather_a(1, k).wait_recv()
    for k in range(1, rows_of):
        for z in range(1, chips):
            gather_b(1, k, z).start()
    forward(act0, fwd1, pre1, act1, -3, pairs + 6)
    for k in range(1, rows_of):
        for z in range(1, chips):
            gather_b(0, k, z).wait_recv()
    for z in range(chips):
        gather_c(0, z).start()
    forward(act1, fwd2, pre2, act2, -2, pairs + 4)

    def spread_final(i, carry):
        x = up_rows[i]
        at = lax.broadcasted_iota(jnp.int32, x.shape, 1)
        left = jnp.where(at == cols - 1, 0.0, shift_down(x, 1))
        right = jnp.where(at == 0, 0.0, shift_up(x, 1))
        upq[i + 2] = jnp.concatenate([left, x, right], axis=0).astype(BF)
        return carry

    for i in (0, 1, rows + 2, rows + 3):
        upq[i] = jnp.zeros(upq.shape[1:], BF)
    lax.fori_loop(0, rows, spread_final, 0)

    for z in range(chips):
        gather_c(0, z).wait_recv()

    def entry_tap(t):
        i, r = table["e", t // 4]
        u = t % 4
        return wall[i, r, :, feats * u : feats * (u + 1)]

    nil = jnp.zeros((tail, feats), BF)
    turned = []
    for t in range(0, 9, 2):
        i, r = table["e", t // 4]
        u = t % 4
        both = wall[i, r, :, feats * u : feats * (u + 2)].astype(F32).T.astype(BF)
        turned += [both[:feats], both[feats:]]
    empty = jnp.zeros((feats, tail), BF)
    for q in range(3):
        t = [turned[3 * p + q] for p in range(3)]
        for e, line in enumerate(([t[1], t[2], empty, t[0]], [t[0], t[1], t[2], empty])):
            for h in range(4):
                at = feats * (4 * q + h)
                entry_mat[e, at : at + feats, :] = line[h]

    def fill_back():
        for q in range(3):
            w = [entry_tap(3 * p + q) for p in range(3)]
            for a, pair in enumerate(([w[2], nil], [w[1], w[2]], [w[0], w[1]], [nil, w[0]])):
                back_mat[tail * (4 * q + a) : tail * (4 * q + a + 1), :] = jnp.concatenate(pair, axis=1)

    def entry_step(m, carry):
        r = 2 * m - 2
        lhs = jnp.concatenate(conv_lhs(act2, r + 4, 2, everything), axis=1)
        for e in range(2):
            out = jnp.dot(lhs, entry_mat[e], preferred_element_type=F32).reshape(2, wide, tail)
            for n in range(2):
                line = base + 2 * (r + n) + e
                inside = (line >= 0) & (line < span)
                at = 2 * (r + n + 2) + e
                entry_pre[at] = out[n]
                moved = pltpu.roll(silu(out[n]), wide - EDGE, 0)[:cols]
                entry_act[at] = jnp.where(inside, moved, 0.0).astype(BF)
        return carry

    lax.fori_loop(0, pairs // 2 + 2, entry_step, 0, unroll=2)

    for k in range(1, rows_of):
        for z in range(1, chips):
            gather_b(1, k, z).wait_recv()
    for z in range(chips):
        gather_c(1, z).start()

    facc[...] = jnp.zeros_like(facc)
    three = 9 * group

    def final_step(m, carry):
        one = upq[pl.ds(2 * m, 3)].reshape(three, cols)
        two = upq[pl.ds(2 * m + 1, 3)].reshape(three, cols)
        rhs = entry_act[pl.ds(2 * m + 3, 2)].reshape(2 * cols, tail)
        facc[...] += jnp.dot(jnp.concatenate([one, two], axis=1), rhs, preferred_element_type=F32)
        return carry

    lax.fori_loop(0, rows // 2 + 1, final_step, 0)
    fgbuf[row] = (facc[...] * scale).astype(BF)

    def fg_copy(k):
        return remote(fgbuf.at[row], fgbuf.at[row], fg_s.at[k], fg_r.at[k], (lax.rem(row + k, rows_of), col))

    for k in range(1, rows_of):
        fg_copy(k).start()

    fill_back()

    for k in range(1, cols_of):
        up_copy(k).wait_recv()
    for side, there in sides:
        other = not_last if side < 0 else not_first

        @pl.when(other)
        def _():
            for k in range(cols_of):
                up_rim(side, k).wait_recv()

    def unpack_up(m, carry):
        got = [zbuf[s, m].astype(F32) for s in range(cols_of)]
        for r in range(4):
            x = jnp.concatenate([z[:, group * r : group * (r + 1)] for z in got], axis=1)
            at = 4 * m + r
            up3[0, at] = shift_down(x, 0).astype(BF)
            up3[1, at] = x.astype(BF)
            up3[2, at] = shift_up(x, 0).astype(BF)
        return carry

    lax.fori_loop(0, fours + 2, unpack_up, 0)
    for z in range(chips):
        gather_c(1, z).wait_recv()

    wsub = lax.broadcasted_iota(jnp.int32, (win, 1), 0) - EDGE
    wcol = wsub + wfrom
    win_cols = (wcol >= 0) & (wcol < cols)
    mine = (wsub >= 0) & (wsub < tile)
    window = pl.ds(wfrom, win)

    def put_back(dst, at, value):
        lead = at if isinstance(at, tuple) else (at,)
        dst[(0,) + lead] = shift_down(value, 0).astype(BF)
        dst[(1,) + lead] = value.astype(BF)
        dst[(2,) + lead] = shift_up(value, 0).astype(BF)

    lot = 10 if (rows + 6) % 10 == 0 else 2

    def entry_back(m, carry):
        k0 = m * lot
        total = jnp.zeros((lot * win, tail), F32)
        for p in range(3):
            for q in range(3):
                i, r = table["f", 3 * p + q]
                lhs = up3[q, pl.ds(k0 + 2 - p, lot)].reshape(lot * win, tail)
                total = total + jnp.dot(lhs, wall[i, r], preferred_element_type=F32)
        total = total.reshape(lot, win, tail)
        for n in range(lot):
            k = k0 + n
            line = base + k - 3
            inside = (line >= 0) & (line < span) & win_cols
            delta = jnp.where(inside, total[n] * slope(entry_pre[k + 1, window, :]), 0.0)
            put_back(ed3, (lax.div(k, 2), lax.rem(k, 2)), delta)
        return carry

    lax.fori_loop(0, (rows + 6) // lot, entry_back, 0)

    def grad_lhs(src, at):
        x = src[1, pl.ds(at, pairs)]
        return jnp.where(mine, x, jnp.zeros_like(x)).reshape(pairs * win, 2 * feats)

    def grad_taps(src, q):
        x = src[q, pl.ds(4, pairs), window, :]
        mix = jnp.where(low, src[q, pl.ds(5, pairs), window, :], src[q, pl.ds(3, pairs), window, :])
        return jnp.concatenate([x.reshape(pairs * win, 128), mix.reshape(pairs * win, 128)], axis=1)

    def turn(lhs):
        return lhs.astype(F32).T.astype(BF)

    def product(lhs, rhs):
        return jnp.dot(lhs, rhs, preferred_element_type=F32) * scale

    def outer(lhs, rhs):
        return lax.dot_general(lhs, rhs, (((0,), (0,)), ((), ())), preferred_element_type=F32) * scale

    f = feats

    some = 7 if (pairs + 2) % 7 == 0 else 2

    def second_back(m, carry):
        r0 = m * some
        total = jnp.zeros((some * win, 2 * feats), F32)
        for q in range(3):
            for a in range(4):
                lhs = ed3[q, pl.ds(r0 + a // 2, some), a % 2].reshape(some * win, tail)
                at = tail * (4 * q + a)
                total = total + jnp.dot(lhs, back_mat[at : at + tail, :], preferred_element_type=F32)
        total = total.reshape(some, win, 2 * feats)
        for n in range(some):
            r = r0 + n - 1
            inside = in_rows(r) & win_cols
            put_back(sd3, r + 2, jnp.where(inside, total[n] * slope(pre2[r + 3, window, :]), 0.0))
        return carry

    for q in range(3):
        sd3[q, 0] = jnp.zeros((win, 128), BF)
        sd3[q, pairs + 3] = jnp.zeros((win, 128), BF)
    lax.fori_loop(0, (pairs + 2) // some, second_back, 0)

    def pair_grads(src, delta):
        out = {}
        delta = turn(delta)
        for q in range(3):
            g = product(delta, grad_taps(src, q))
            out[0, q] = g[:f, 3 * f :] + g[f:, :f]
            out[1, q] = g[:f, :f] + g[f:, f : 2 * f]
            out[2, q] = g[:f, f : 2 * f] + g[f:, 2 * f : 3 * f]
        return out

    whole = pl.ds(0, win)

    def stage(dst, taps):
        for t in range(0, len(taps), 2):
            both = jnp.concatenate(taps[t : t + 2], axis=1)
            dst[:, t // 2] = both.reshape(cols_of, feats // cols_of, 2 * f).astype(BF)

    def chain(sent, got, mid, every, last, out, sems):
        s1, r1, s2, r2, s3, r3 = sems

        def first_copy(k):
            peer = lax.rem(col + k, cols_of)
            return remote(sent.at[peer], got.at[k], s1.at[k], r1.at[k], (row, peer))

        def second_copy(k):
            return remote(mid, every.at[row], s2.at[k], r2.at[k], (lax.rem(row + k, rows_of), col))

        def third_copy(k):
            return remote(last, out.at[col], s3.at[k], r3.at[k], (row, lax.rem(col + k, cols_of)))

        return first_copy, second_copy, third_copy

    a_copies = chain(sas, sar, sam, saa, saf, sa_out, (a1_s, a1_r, a2_s, a2_r, a3_s, a3_r))
    b_copies = chain(sbs, sbr, sbm, sba, sbf, sb_out, (b1_s, b1_r, b2_s, b2_r, b3_s, b3_r))
    blank = jnp.zeros((f, f), F32)
    second_grads = pair_grads(act1, grad_lhs(sd3, 2))
    stage(sas, [second_grads[t // 3, t % 3] for t in range(9)] + [blank])
    for k in range(1, cols_of):
        a_copies[0](k).start()

    def first_back(m, carry):
        r0 = m * some
        out = conv(sd3, r0 + 1, some, whole, bwd2[...])
        for n in range(some):
            r = r0 + n - 1
            inside = in_rows(r) & win_cols
            put_back(fd3, r + 1, jnp.where(inside, out[n] * slope(pre1[r + 3, window, :]), 0.0))
        return carry

    lax.fori_loop(0, (pairs + 2) // some, first_back, 0)
    first_grads = pair_grads(act0, grad_lhs(fd3, 1))

    few = 6 if pairs % 6 == 0 else 2

    def stem_back(m, carry):
        r0 = m * few
        out = conv(fd3, r0 + 1, few, whole, bwd1[...])
        for n in range(few):
            r = r0 + n
            delta = jnp.where(mine, out[n] * slope(pre0[r + 3, window, :]), 0.0)
            td3[r] = jnp.concatenate(
                [shift_down(delta, 0), delta, shift_up(delta, 0)], axis=1).astype(BF)
        return carry

    lax.fori_loop(0, pairs // few, stem_back, 0)
    moments = []
    for v in range(4):
        lhs = jnp.concatenate([stem_lhs(g, v, window) for g in range(1, groups + 1)], axis=0)
        rhs = jnp.concatenate([td3[4 * g + v] for g in range(groups)], axis=0)
        got = outer(lhs, rhs).reshape(8, 16, 6 * feats)
        moments.append(pltpu.roll(got, 16 - 4 * v, 1) if v else got)
    moment = (moments[0] + moments[1] + (moments[2] + moments[3])).reshape(128, 6 * feats)
    total = jnp.zeros((feats, 48), F32)
    for s in range(3):
        for e in range(2):
            part = moment[:, 2 * f * s + f * e : 2 * f * s + f * (e + 1)].astype(BF)
            total = total + lax.dot_general(
                part, onehot[2 * s + e], (((0,), (0,)), ((), ())), preferred_element_type=F32)
    total = jnp.concatenate([total, jnp.zeros((feats, f - 48), F32)], axis=1)
    stage(sbs, [first_grads[t // 3, t % 3] for t in range(9)] + [total])
    for k in range(1, cols_of):
        b_copies[0](k).start()

    def entry_own(e):
        x = ed3[1, pl.ds(1 + e, pairs), 1 - e]
        return jnp.where(mine, x, jnp.zeros_like(x)).reshape(pairs * win, tail)

    own_even, own_odd = turn(entry_own(0)), turn(entry_own(1))
    grads = {}
    for q in range(3):
        taps = grad_taps(act2, q)
        ge, go = product(own_even, taps), product(own_odd, taps)
        grads[0, q] = ge[:, 3 * f :] + go[:, :f]
        grads[1, q] = ge[:, :f] + go[:, f : 2 * f]
        grads[2, q] = ge[:, f : 2 * f] + go[:, 2 * f : 3 * f]
    quarter = group // rows_of
    for t in range(0, 9, 2):
        two = [grads[(t + u) // 3, (t + u) % 3] if t + u < 9 else jnp.zeros((tail, f), F32) for u in range(2)]
        both = jnp.concatenate(two, axis=1).reshape(cols_of, rows_of, quarter, 2 * f)
        for r in range(rows_of):
            egs[r, :, t // 2] = both[:, r].astype(BF)

    def e1_copy(k):
        peer = lax.rem(row + k, rows_of)
        return remote(egs.at[peer], egr.at[k], e1_s.at[k], e1_r.at[k], (peer, col))

    def e2_copy(k):
        peer = lax.rem(col + k, cols_of)
        return remote(egm.at[peer], egq.at[k], e2_s.at[k], e2_r.at[k], (row, peer))

    def e3_copy(k):
        return remote(egn, eg_out.at[row], e3_s.at[k], e3_r.at[k], (lax.rem(row + k, rows_of), col))

    for k in range(1, rows_of):
        e1_copy(k).start()

    for part in range(2):
        for k in range(1, chips):
            gather_a(part, k).wait_send()
        for k in range(1, rows_of):
            for z in range(1, chips):
                gather_b(part, k, z).wait_send()
        for z in range(chips):
            gather_c(part, z).wait_send()
    for k in range(1, cols_of):
        pix_copy(k).wait_send()
        up_copy(k).wait_send()
    for side, there in sides:

        @pl.when(there)
        def _():
            for k in range(cols_of):
                pix_rim(side, k).wait_send()
                up_rim(side, k).wait_send()

    for k in range(1, rows_of):
        fg_copy(k).wait()

    def final_sum(t, carry):
        at = pl.ds(t * group, group)
        acc = fgbuf[0, at].astype(F32)
        for r in range(1, rows_of):
            acc = acc + fgbuf[r, at].astype(F32)
        facc[at] = acc
        return carry

    lax.fori_loop(0, 9, final_sum, 0)
    fg_store = pltpu.make_async_copy(facc, fg_out, out_sem)
    fg_store.start()

    def summed(mine_value, got, copy, count):
        acc = mine_value.astype(F32)
        for k in range(1, count):
            copy(k).wait_recv()
            acc = acc + got[k].astype(F32)
        return acc.astype(BF)

    for k in range(1, cols_of):
        a_copies[0](k).wait_send()
        b_copies[0](k).wait_send()
    for k in range(1, rows_of):
        e1_copy(k).wait_send()
    for (one_copy, two_copy, _), sent, got, mid, every in (
        (a_copies, sas, sar, sam, saa), (b_copies, sbs, sbr, sbm, sba)):
        value = summed(sent[col], got, one_copy, cols_of)
        mid[...] = value
        every[row] = value
        for k in range(1, rows_of):
            two_copy(k).start()
    egm[...] = summed(egs[row], egr, e1_copy, rows_of)
    for k in range(1, cols_of):
        e2_copy(k).start()
    for (_, two_copy, three_copy), every, last, out in (
        (a_copies, saa, saf, sa_out), (b_copies, sba, sbf, sb_out)):
        for k in range(1, rows_of):
            two_copy(k).wait_recv()
        acc = every[0].astype(F32)
        for r in range(1, rows_of):
            acc = acc + every[r].astype(F32)
        value = acc.astype(BF)
        last[...] = value
        out[col] = value
        for k in range(1, cols_of):
            three_copy(k).start()
    value = summed(egm[col], egq, e2_copy, cols_of)
    egn[...] = value
    eg_out[row] = value
    for k in range(1, rows_of):
        e3_copy(k).start()
    fg_store.wait()
    for k in range(1, cols_of):
        e2_copy(k).wait_send()
    for k in range(1, rows_of):
        a_copies[1](k).wait_send()
        b_copies[1](k).wait_send()
        e3_copy(k).wait()
    for k in range(1, cols_of):
        a_copies[2](k).wait()
        b_copies[2](k).wait()


def step(pix, stem, first, second, entry, final, up, tile, scale):
    rows_of, cols_of = lax.axis_size("row"), lax.axis_size("col")
    group, rows, cols = up.shape
    feats, tail = first.shape[1], final.shape[2]
    dims = (rows_of, cols_of, rows, cols, tile, group, feats, tail, scale)
    groups, wide, win, pairs, fours = rows // 8, cols + 16, tile + 16, rows // 2, rows // 4
    slots, _ = slab_table(rows_of)
    chips, share, quarter = cols_of // 2, feats // cols_of, group // rows_of
    act = pltpu.VMEM((3, pairs + 8, wide, 128), BF)
    pre = pltpu.VMEM((pairs + 6, wide, 128), F32)
    dma = pltpu.SemaphoreType.DMA
    mat = pltpu.VMEM((12 * feats, 2 * feats), BF)

    def vm(*shape, kind=BF):
        return pltpu.VMEM(shape, kind)

    scratch = [pltpu.VMEM(x.shape, x.dtype) for x in (pix, stem, first, second, entry, final, up)]
    scratch += [dma((7,)), dma(())]
    scratch += [
        vm(groups, tile, 128), vm(groups + 2, cols_of, tile, 128), vm(groups + 2, wide, 128),
        vm(wide, 128, kind=F32), vm(wide, 4 * group, kind=F32), vm(4, 128, 6 * feats), vm(6, 128, 48),
        mat, mat, mat, mat, vm(2, 12 * feats, tail),
        vm(12 * tail, 2 * feats), act, act, act, pre, pre, pre,
        vm(rows + 8, cols, tail), vm(rows + 8, wide, tail, kind=F32),
        vm(rows + 4, 3 * group, cols), vm(9 * group, tail, kind=F32),
        vm(rows, group, cols, kind=F32),
        vm(fours, wide, 4 * group), vm(cols_of, fours + 2, win, 4 * group),
        vm(3, rows + 8, win, tail), vm(3, pairs + 3, 2, win, tail),
        vm(3, pairs + 4, win, 128), vm(3, pairs + 2, win, 128), vm(pairs, win, 384),
        vm(slots, rows_of, tail, tail),
        vm(rows_of, 9 * group, tail),
        vm(rows_of, cols_of, 5, quarter, 128), vm(rows_of, cols_of, 5, quarter, 128), vm(cols_of, 5, quarter, 128),
        vm(cols_of, 5, quarter, 128), vm(5, quarter, 128),
        vm(cols_of, 5, share, 128), vm(cols_of, 5, share, 128), vm(5, share, 128),
        vm(rows_of, 5, share, 128), vm(5, share, 128),
        vm(cols_of, 5, share, 128), vm(cols_of, 5, share, 128), vm(5, share, 128),
        vm(rows_of, 5, share, 128), vm(5, share, 128),
    ]
    for shape in (
        (cols_of,), (2, cols_of), (cols_of,), (2, cols_of), (2, chips), (2, rows_of, chips), (2, chips), (rows_of,),
        (rows_of,), (cols_of,), (rows_of,),
        (cols_of,), (rows_of,), (cols_of,), (cols_of,), (rows_of,), (cols_of,),
    ):
        scratch += [dma(shape), dma(shape)]
    return pl.pallas_call(
        functools.partial(step_kernel, dims),
        out_shape=(
            jax.ShapeDtypeStruct((9 * group, tail), F32),
            jax.ShapeDtypeStruct((rows_of, 5, quarter, 128), BF),
            jax.ShapeDtypeStruct((cols_of, 5, share, 128), BF),
            jax.ShapeDtypeStruct((cols_of, 5, share, 128), BF),
        ),
        in_specs=[ANY] * 7,
        out_specs=(ANY,) + (VMEM,) * 3,
        scratch_shapes=scratch,
        compiler_params=pltpu.CompilerParams(
            collective_id=0, has_side_effects=True, vmem_limit_bytes=58 * 1024 * 1024),
    )(pix, stem, first, second, entry, final, up)


def finish_kernel(fg_ref, eg_ref, sa_ref, sb_ref, stem_out, first_out, second_out, entry_out, final_out):
    group, feats = entry_out.shape[1:]
    for p in range(3):
        for q in range(3):
            at = ((2 - p) * 3 + q) * group
            final_out[3 * p + q] = fg_ref[at : at + group]
    for t in range(5):
        entry = eg_ref[:, t].astype(F32).reshape(group, 2 * feats)
        second = sa_ref[:, t].astype(F32).reshape(feats, 2 * feats)
        first = sb_ref[:, t].astype(F32).reshape(feats, 2 * feats)
        for u in range(2):
            if 2 * t + u < 9:
                half = slice(u * feats, (u + 1) * feats)
                entry_out[2 * t + u] = entry[:, half]
                second_out[2 * t + u] = second[:, half]
                first_out[2 * t + u] = first[:, half]
    stem_out[...] = first.T[feats : feats + stem_out.shape[0]]


def finish(fg, eg, sa, sb, feats):
    group, tail = fg.shape[0] // 9, fg.shape[1]
    return pl.pallas_call(
        finish_kernel,
        out_shape=(
            jax.ShapeDtypeStruct((48, feats), F32),
            jax.ShapeDtypeStruct((9, feats, feats), F32),
            jax.ShapeDtypeStruct((9, feats, feats), F32),
            jax.ShapeDtypeStruct((9, group, feats), F32),
            jax.ShapeDtypeStruct((9, group, tail), F32),
        ),
        in_specs=[VMEM] * 4,
        out_specs=(VMEM,) * 5,
    )(fg, eg, sa, sb)


def per_device(pixels, stem_weight, first_weight, second_weight, entry_weight, final_weight, upstream):
    chans, pix_rows, pix_cols = pixels.shape
    rows, tile = pix_rows // 2, pix_cols // 2
    cols = tile * lax.axis_size("col")
    scale = 1.0 / math.sqrt(rows * lax.axis_size("row") * cols)

    def flat(kernel):
        return kernel.transpose(2, 3, 0, 1).reshape(9, kernel.shape[0], kernel.shape[1])

    stem = stem_weight.transpose(1, 2, 3, 0).reshape(chans * 16, stem_weight.shape[0])
    fg, eg, sa, sb = step(
        pixels.transpose(0, 2, 1), stem, flat(first_weight), flat(second_weight), flat(entry_weight),
        flat(final_weight), upstream, tile, scale)
    stem_grad, first_grad, second_grad, entry_grad, final_grad = finish(fg, eg, sa, sb, stem_weight.shape[0])

    def taps_last(grad):
        return grad.reshape(3, 3, grad.shape[1], grad.shape[2]).transpose(2, 3, 0, 1)

    return (
        stem_grad.reshape(chans, 4, 4, -1).transpose(3, 0, 1, 2),
        taps_last(first_grad),
        taps_last(second_grad),
        taps_last(entry_grad),
        taps_last(final_grad),
    )


def solution(mesh):
    return jax.shard_map(
        per_device,
        mesh=mesh,
        in_specs=(
            P(None, "row", "col"),
            P(),
            P(),
            P(),
            P("col", None, None, None),
            P("col", None, None, None),
            P("col", "row", None),
        ),
        out_specs=(P(), P(), P(), P("col", None, None, None), P("col", None, None, None)),
        check_vma=False,
    )
```

```python
import functools
import math

import jax
import jax.numpy as jnp
from jax import lax
from jax.experimental import pallas as pl
from jax.experimental.pallas import tpu as pltpu
from jax.sharding import PartitionSpec as P

BF = jnp.bfloat16
F32 = jnp.float32
MESH = pl.DeviceIdType.MESH
VMEM = pl.BlockSpec(memory_space=pltpu.VMEM)
ANY = pl.BlockSpec(memory_space=pl.ANY)
EDGE = 4
SLABS = 12


def silu(v):
    h = 0.5 * v
    return h + h * jnp.tanh(h)


def slope(v):
    h = 0.5 * v
    t = jnp.tanh(h)
    return (0.5 + 0.5 * t) * (1.0 + h * (1.0 - t))


def slab_table(rows_of):
    slots = -(-SLABS // rows_of)
    table, free = {}, [(i, r) for i in range(slots) for r in range(rows_of)]
    for n in range(3):
        table["e", n] = free.pop(0)
    free.sort(key=lambda at: (at[1], at[0]))
    for n in range(9):
        table["f", n] = free.pop(0)
    return slots, table


def shift_up(v, axis):
    return pltpu.roll(v, 1, axis)


def shift_down(v, axis):
    return pltpu.roll(v, v.shape[axis] - 1, axis)


def step_kernel(dims, *refs):
    rows_of, cols_of, rows, cols, tile, group, feats, tail, scale = dims
    given = refs[:7]
    fg_out, eg_out, sa_out, sb_out = refs[7:11]
    (pix_ref, stem_ref, first_ref, second_ref, entry_ref, final_ref, up_ref, in_sem, out_sem,
     qsend, pixbuf, quads, padf, padz, stem_mat, onehot, fwd1, fwd2, bwd1, bwd2, entry_mat,
     back_mat, act0, act1, act2, pre0, pre1, pre2, entry_act, entry_pre, upq, facc,
     up_rows, zsend, zbuf, up3, ed3, sd3, fd3, td3, wall, fgbuf,
     egs, egr, egm, egq, egn, sas, sar, sam, saa, saf, sbs, sbr, sbm, sba, sbf,
     pix_s, pix_r, prim_s, prim_r, up_s, up_r, urim_s, urim_r,
     wa_s, wa_r, wb_s, wb_r, wc_s, wc_r, fg_s, fg_r,
     e1_s, e1_r, e2_s, e2_r, e3_s, e3_r,
     a1_s, a1_r, a2_s, a2_r, a3_s, a3_r, b1_s, b1_r, b2_s, b2_r, b3_s, b3_r) = refs[11:]

    row, col = lax.axis_index("row"), lax.axis_index("col")
    core, chip = lax.rem(col, 2), lax.div(col, 2)
    chips = cols_of // 2
    groups = rows // 8
    wide, win = cols + 16, tile + 16
    span = rows * rows_of
    pairs = rows // 2
    wfrom = pl.multiple_of(col * tile, tile)
    not_first, not_last = row > 0, row < rows_of - 1
    slots, table = slab_table(rows_of)

    def remote(src, dst, send, recv, peer):
        return pltpu.make_async_remote_copy(
            src_ref=src, dst_ref=dst, send_sem=send, recv_sem=recv,
            device_id=peer, device_id_type=MESH)

    loads = {}
    for n, (src, dst) in enumerate(zip(
        given, (pix_ref, stem_ref, first_ref, second_ref, entry_ref, final_ref, up_ref))):
        loads[n] = pltpu.make_async_copy(src, dst, in_sem.at[n])
    for n in (0, 6, 4, 5, 1, 2, 3):
        loads[n].start()

    barrier = pltpu.get_barrier_semaphore()
    for k in range(1, cols_of):
        pl.semaphore_signal(barrier, inc=1, device_id=(row, lax.rem(col + k, cols_of)), device_id_type=MESH)
    for k in range(1, rows_of):
        pl.semaphore_signal(barrier, inc=1, device_id=(lax.rem(row + k, rows_of), col), device_id_type=MESH)
    for side, there in ((-1, not_first), (1, not_last)):

        @pl.when(there)
        def _():
            for k in range(1, cols_of):
                pl.semaphore_signal(
                    barrier, inc=1, device_id=(row + side, lax.rem(col + k, cols_of)), device_id_type=MESH)

    loads[0].wait()
    for g in range(groups):
        pieces = []
        for a in range(2):
            for c in range(3):
                pieces.append(pix_ref[c, pl.ds(a, tile, stride=2), :][:, 16 * g : 16 * g + 16])
            pieces.append(jnp.zeros((tile, 16), F32))
        qsend[g] = jnp.concatenate(pieces, axis=1).astype(BF)

    loads[4].wait()
    loads[5].wait()
    own = pl.ds(pl.multiple_of(group * col, group), group)
    for t in range(9):
        i, r = table["f", t]
        wall[i, r, own, :] = final_ref[t]
    for n in range(3):
        i, r = table["e", n]
        taps = [entry_ref[4 * n + u] if 4 * n + u < 9 else jnp.zeros((group, feats), BF) for u in range(4)]
        wall[i, r, own, :] = jnp.concatenate(taps, axis=1)

    loads[6].wait()
    up_rows[...] = up_ref[...].astype(F32).transpose(1, 0, 2)
    padz[...] = jnp.zeros_like(padz)
    padf[...] = jnp.zeros_like(padf)

    def spread_up(m, carry):
        x = up_rows[pl.ds(4 * m, 4)].reshape(4 * group, cols)
        padz[EDGE : EDGE + cols, :] = x.T
        zsend[m] = padz[...].astype(BF)
        return carry

    lax.fori_loop(0, rows // 4, spread_up, 0)

    adj = not_first.astype(jnp.int32) + not_last.astype(jnp.int32)
    pl.semaphore_wait(barrier, (cols_of - 1) * (1 + adj) + rows_of - 1)

    sides = ((-1, not_first), (1, not_last))

    def pix_copy(k):
        return remote(qsend, pixbuf.at[pl.ds(1, groups), col], pix_s.at[k], pix_r.at[k],
                      (row, lax.rem(col + k, cols_of)))

    def pix_rim(side, k):
        at = 0 if side < 0 else 1
        return remote(qsend.at[0 if side < 0 else groups - 1],
                      pixbuf.at[groups + 1 if side < 0 else 0, col],
                      prim_s.at[at, k], prim_r.at[at, k], (row + side, lax.rem(col + k, cols_of)))

    fours = rows // 4

    def up_window(k):
        peer = lax.rem(col + k, cols_of)
        return peer, pl.ds(pl.multiple_of(peer * tile, tile), tile + 8)

    def up_copy(k):
        peer, window = up_window(k)
        return remote(zsend.at[:, window], zbuf.at[col, pl.ds(1, fours), pl.ds(0, tile + 8)],
                      up_s.at[k], up_r.at[k], (row, peer))

    def up_rim(side, k):
        at = 0 if side < 0 else 1
        peer, window = up_window(k)
        return remote(zsend.at[0 if side < 0 else fours - 1, window],
                      zbuf.at[col, fours + 1 if side < 0 else 0, pl.ds(0, tile + 8)],
                      urim_s.at[at, k], urim_r.at[at, k], (row + side, peer))

    def shard(z, c):
        return pl.ds(pl.multiple_of(group * (2 * z + c), group), group)

    def gather_a(part, k):
        at = wall.at[0, row, shard(chip, core)] if part == 0 else wall.at[pl.ds(1, slots - 1), row, shard(chip, core)]
        return remote(at, at, wa_s.at[part, k], wa_r.at[part, k],
                      (row, 2 * lax.rem(chip + k, chips) + core))

    def gather_b(part, k, z):
        here = shard(lax.rem(chip + z, chips), core)
        at = wall.at[0, row, here] if part == 0 else wall.at[pl.ds(1, slots - 1), row, here]
        return remote(at, at, wb_s.at[part, k, z], wb_r.at[part, k, z], (lax.rem(row + k, rows_of), col))

    def gather_c(part, z):
        here = shard(z, core)
        at = wall.at[0, :, here] if part == 0 else wall.at[pl.ds(1, slots - 1), :, here]
        return remote(at, at, wc_s.at[part, z], wc_r.at[part, z], (row, 2 * chip + 1 - core))

    for k in range(1, cols_of):
        pix_copy(k).start()
    for side, there in sides:

        @pl.when(there)
        def _():
            for k in range(cols_of):
                pix_rim(side, k).start()

    for part in range(2):
        for k in range(1, chips):
            gather_a(part, k).start()
    pixbuf[pl.ds(1, groups), col] = qsend[...]
    zbuf[:, :, tile + 8 :, :] = jnp.zeros((cols_of, fours + 2, win - tile - 8, 4 * group), BF)
    zbuf[col, pl.ds(1, fours), 0 : tile + 8] = zsend[:, pl.ds(wfrom, tile + 8)]

    @pl.when(row == 0)
    def _():
        pixbuf[0] = jnp.zeros(pixbuf.shape[1:], BF)
        zbuf[:, 0] = jnp.zeros((cols_of,) + zbuf.shape[2:], BF)

    @pl.when(row == rows_of - 1)
    def _():
        pixbuf[groups + 1] = jnp.zeros(pixbuf.shape[1:], BF)
        zbuf[:, fours + 1] = jnp.zeros((cols_of,) + zbuf.shape[2:], BF)

    for n in (1, 2, 3):
        loads[n].wait()
    spot = lax.broadcasted_iota(jnp.int32, (128, 48), 0)
    want = lax.broadcasted_iota(jnp.int32, (128, 48), 1)
    la, lc, lr, lb = spot // 64, (spot // 16) % 4, (spot // 4) % 4, spot % 4
    d = (lr + 1) % 4 - 1
    base_mat = []
    for s in range(3):
        q = 2 * (s - 1) + la + 1
        for e in range(2):
            p = 4 * d + lb - 2 * e + 1
            fits = (lc < 3) & (p >= 0) & (p < 4) & (q >= 0) & (q < 4)
            hot = (fits & (want == lc * 16 + p * 4 + q)).astype(F32).astype(BF)
            onehot[2 * s + e] = hot
            base_mat.append(jnp.dot(hot, stem_ref[...], preferred_element_type=F32))
    for s in range(3):
        pair = jnp.concatenate(base_mat[2 * s : 2 * s + 2], axis=1).reshape(8, 16, 2 * feats)
        for v in range(4):
            turned = pltpu.roll(pair, 4 * v, 1) if v else pair
            stem_mat[v, :, 2 * feats * s : 2 * feats * (s + 1)] = turned.reshape(128, 2 * feats).astype(BF)

    zero = jnp.zeros((feats, feats), F32)
    for w_ref, fwd, bwd in ((first_ref, fwd1, bwd1), (second_ref, fwd2, bwd2)):
        for q in range(3):
            w = [w_ref[3 * p + q].astype(F32) for p in range(3)]
            even = jnp.concatenate([w[1], w[2], zero, w[0]], axis=1)
            odd = jnp.concatenate([w[0], w[1], w[2], zero], axis=1)
            both = jnp.concatenate([even, odd], axis=0)
            fwd[4 * feats * q : 4 * feats * (q + 1)] = both.T.astype(BF)
            lines = [[w[1], w[2]], [w[0], w[1]], [zero, w[0]], [w[2], zero]]
            back = jnp.concatenate([jnp.concatenate(line, axis=1) for line in lines], axis=0)
            bwd[4 * feats * q : 4 * feats * (q + 1)] = back.astype(BF)

    for at in (act0, act1, act2):
        for q in range(3):
            at[q, 0] = jnp.zeros((wide, 128), BF)
            at[q, pairs + 7] = jnp.zeros((wide, 128), BF)

    for k in range(1, cols_of):
        pix_copy(k).wait_recv()
    for side, there in sides:
        other = not_last if side < 0 else not_first

        @pl.when(other)
        def _():
            for k in range(cols_of):
                pix_rim(side, k).wait_recv()

    for g in range(groups + 2):
        padf[EDGE : EDGE + cols, :] = pixbuf[g].reshape(cols, 128).astype(F32)
        quads[g] = padf[...].astype(BF)

    for k in range(1, chips):
        gather_a(0, k).wait_recv()
    for k in range(1, rows_of):
        for z in range(1, chips):
            gather_b(0, k, z).start()
    for k in range(1, cols_of):
        up_copy(k).start()
    for side, there in sides:

        @pl.when(there)
        def _():
            for k in range(cols_of):
                up_rim(side, k).start()

    lane = lax.broadcasted_iota(jnp.int32, (1, 128), 1)
    upper = (lane >= feats).astype(jnp.int32)
    sub = lax.broadcasted_iota(jnp.int32, (wide, 1), 0) - EDGE
    in_cols = (sub >= 0) & (sub < cols)
    base = row * rows

    def in_rows(r):
        line = base + 2 * r + upper
        return (line >= 0) & (line < span)

    def put(dst, at, value):
        dst[0, at] = shift_up(value, 0).astype(BF)
        dst[1, at] = value.astype(BF)
        dst[2, at] = shift_down(value, 0).astype(BF)

    def stem_lhs(g, v, window):
        if v == 0:
            return jnp.where(lr_lane == 3, quads[g - 1, window, :], quads[g, window, :])
        if v == 3:
            return jnp.where(lr_lane == 0, quads[g + 1, window, :], quads[g, window, :])
        return quads[g, window, :]

    lr_lane = (lax.broadcasted_iota(jnp.int32, (1, 128), 1) // 4) % 4

    def stem_one(g, v):
        r = 4 * (g - 1) + v
        out = jnp.dot(stem_lhs(g, v, pl.ds(0, wide)), stem_mat[v], preferred_element_type=F32)
        n = 2 * feats
        pre = shift_up(out[:, :n], 0) + out[:, n : 2 * n] + shift_down(out[:, 2 * n :], 0)
        pre0[r + 3] = pre
        put(act0, r + 4, jnp.where(in_rows(r) & in_cols, silu(pre), 0.0))

    for v in (1, 2, 3):
        stem_one(0, v)

    def stem_group(g, carry):
        for v in range(4):
            stem_one(g, v)
        return carry

    lax.fori_loop(1, groups + 1, stem_group, 0)
    for v in (0, 1, 2):
        stem_one(groups + 1, v)

    low = lax.broadcasted_iota(jnp.int32, (1, 1, 128), 2) < feats

    def conv_lhs(src, at, n, window):
        size = window.size
        out = []
        for q in range(3):
            x = src[q, pl.ds(at, n), window, :]
            mix = jnp.where(low, src[q, pl.ds(at + 1, n), window, :], src[q, pl.ds(at - 1, n), window, :])
            out += [x.reshape(n * size, 128), mix.reshape(n * size, 128)]
        return out

    everything = pl.ds(0, wide)

    def conv(src, at, n, window, mat):
        parts = conv_lhs(src, at, n, window)
        lhs = jnp.concatenate(parts, axis=1)
        out = jnp.dot(lhs, mat, preferred_element_type=F32)
        return out.reshape(n, window.size, out.shape[1])

    def forward(src, mat, pre_ref, dst, first, count, lot):
        def one(m, carry):
            r = first + lot * m
            out = conv(src, r + 4, lot, everything, mat[...])
            for n in range(lot):
                pre_ref[r + n + 3] = out[n]
                put(dst, r + n + 4, jnp.where(in_rows(r + n) & in_cols, silu(out[n]), 0.0))
            return carry

        lax.fori_loop(0, count // lot, one, 0)

    for k in range(1, chips):
        gather_a(1, k).wait_recv()
    for k in range(1, rows_of):
        for z in range(1, chips):
            gather_b(1, k, z).start()
    forward(act0, fwd1, pre1, act1, -3, pairs + 6, 9)
    for k in range(1, rows_of):
        for z in range(1, chips):
            gather_b(0, k, z).wait_recv()
    for z in range(chips):
        gather_c(0, z).start()
    forward(act1, fwd2, pre2, act2, -2, pairs + 4, 8)

    def spread_final(i, carry):
        x = up_rows[i]
        at = lax.broadcasted_iota(jnp.int32, x.shape, 1)
        left = jnp.where(at == cols - 1, 0.0, shift_down(x, 1))
        right = jnp.where(at == 0, 0.0, shift_up(x, 1))
        upq[i + 2] = jnp.concatenate([left, x, right], axis=0).astype(BF)
        return carry

    for i in (0, 1, rows + 2, rows + 3):
        upq[i] = jnp.zeros(upq.shape[1:], BF)
    lax.fori_loop(0, rows, spread_final, 0)

    for z in range(chips):
        gather_c(0, z).wait_recv()

    def entry_tap(t):
        i, r = table["e", t // 4]
        u = t % 4
        return wall[i, r, :, feats * u : feats * (u + 1)]

    nil = jnp.zeros((tail, feats), BF)
    turned = []
    for t in range(0, 9, 2):
        i, r = table["e", t // 4]
        u = t % 4
        both = wall[i, r, :, feats * u : feats * (u + 2)].astype(F32).T.astype(BF)
        turned += [both[:feats], both[feats:]]
    empty = jnp.zeros((feats, tail), BF)
    for q in range(3):
        t = [turned[3 * p + q] for p in range(3)]
        for e, line in enumerate(([t[1], t[2], empty, t[0]], [t[0], t[1], t[2], empty])):
            for h in range(4):
                at = feats * (4 * q + h)
                entry_mat[e, at : at + feats, :] = line[h]

    def fill_back():
        for q in range(3):
            w = [entry_tap(3 * p + q) for p in range(3)]
            for a, pair in enumerate(([w[2], nil], [w[1], w[2]], [w[0], w[1]], [nil, w[0]])):
                back_mat[tail * (4 * q + a) : tail * (4 * q + a + 1), :] = jnp.concatenate(pair, axis=1)

    def entry_step(m, carry):
        r = 4 * m - 2
        lhs = jnp.concatenate(conv_lhs(act2, r + 4, 4, everything), axis=1)
        for e in range(2):
            out = jnp.dot(lhs, entry_mat[e], preferred_element_type=F32).reshape(4, wide, tail)
            for n in range(4):
                line = base + 2 * (r + n) + e
                inside = (line >= 0) & (line < span)
                at = 2 * (r + n + 2) + e
                entry_pre[at] = out[n]
                moved = pltpu.roll(silu(out[n]), wide - EDGE, 0)[:cols]
                entry_act[at] = jnp.where(inside, moved, 0.0).astype(BF)
        return carry

    lax.fori_loop(0, (pairs + 4) // 4, entry_step, 0, unroll=1)

    for k in range(1, rows_of):
        for z in range(1, chips):
            gather_b(1, k, z).wait_recv()
    for z in range(chips):
        gather_c(1, z).start()

    facc[...] = jnp.zeros_like(facc)
    three = 9 * group

    def final_step(m, carry):
        one = upq[pl.ds(2 * m, 3)].reshape(three, cols)
        two = upq[pl.ds(2 * m + 1, 3)].reshape(three, cols)
        rhs = entry_act[pl.ds(2 * m + 3, 2)].reshape(2 * cols, tail)
        facc[...] += jnp.dot(jnp.concatenate([one, two], axis=1), rhs, preferred_element_type=F32)
        return carry

    lax.fori_loop(0, rows // 2 + 1, final_step, 0)
    fgbuf[row] = (facc[...] * scale).astype(BF)

    def fg_copy(k):
        return remote(fgbuf.at[row], fgbuf.at[row], fg_s.at[k], fg_r.at[k], (lax.rem(row + k, rows_of), col))

    for k in range(1, rows_of):
        fg_copy(k).start()

    fill_back()

    for k in range(1, cols_of):
        up_copy(k).wait_recv()
    for side, there in sides:
        other = not_last if side < 0 else not_first

        @pl.when(other)
        def _():
            for k in range(cols_of):
                up_rim(side, k).wait_recv()

    def unpack_up(m, carry):
        got = [zbuf[s, m].astype(F32) for s in range(cols_of)]
        for r in range(4):
            x = jnp.concatenate([z[:, group * r : group * (r + 1)] for z in got], axis=1)
            at = 4 * m + r
            up3[0, at] = shift_down(x, 0).astype(BF)
            up3[1, at] = x.astype(BF)
            up3[2, at] = shift_up(x, 0).astype(BF)
        return carry

    lax.fori_loop(0, fours + 2, unpack_up, 0)
    for z in range(chips):
        gather_c(1, z).wait_recv()

    wsub = lax.broadcasted_iota(jnp.int32, (win, 1), 0) - EDGE
    wcol = wsub + wfrom
    win_cols = (wcol >= 0) & (wcol < cols)
    mine = (wsub >= 0) & (wsub < tile)
    window = pl.ds(wfrom, win)

    def put_back(dst, at, value):
        lead = at if isinstance(at, tuple) else (at,)
        dst[(0,) + lead] = shift_down(value, 0).astype(BF)
        dst[(1,) + lead] = value.astype(BF)
        dst[(2,) + lead] = shift_up(value, 0).astype(BF)

    lot = 15 if (rows + 6) % 15 == 0 else 2

    def entry_back(m, carry):
        k0 = m * lot
        total = jnp.zeros((lot * win, tail), F32)
        for p in range(3):
            for q in range(3):
                i, r = table["f", 3 * p + q]
                lhs = up3[q, pl.ds(k0 + 2 - p, lot)].reshape(lot * win, tail)
                total = total + jnp.dot(lhs, wall[i, r], preferred_element_type=F32)
        total = total.reshape(lot, win, tail)
        for n in range(lot):
            k = k0 + n
            line = base + k - 3
            inside = (line >= 0) & (line < span) & win_cols
            delta = jnp.where(inside, total[n] * slope(entry_pre[k + 1, window, :]), 0.0)
            put_back(ed3, (lax.div(k, 2), lax.rem(k, 2)), delta)
        return carry

    lax.fori_loop(0, (rows + 6) // lot, entry_back, 0)

    def grad_lhs(src, at):
        x = src[1, pl.ds(at, pairs)]
        return jnp.where(mine, x, jnp.zeros_like(x)).reshape(pairs * win, 2 * feats)

    def grad_taps(src, q):
        x = src[q, pl.ds(4, pairs), window, :]
        mix = jnp.where(low, src[q, pl.ds(5, pairs), window, :], src[q, pl.ds(3, pairs), window, :])
        return jnp.concatenate([x.reshape(pairs * win, 128), mix.reshape(pairs * win, 128)], axis=1)

    def turn(lhs):
        return lhs.astype(F32).T.astype(BF)

    def product(lhs, rhs):
        return jnp.dot(lhs, rhs, preferred_element_type=F32) * scale

    def outer(lhs, rhs):
        return lax.dot_general(lhs, rhs, (((0,), (0,)), ((), ())), preferred_element_type=F32) * scale

    f = feats

    some = 7 if (pairs + 2) % 7 == 0 else 2

    def second_back(m, carry):
        r0 = m * some
        lhs = [
            ed3[q, pl.ds(r0 + a // 2, some), a % 2].reshape(some * win, tail) for q in range(3) for a in range(4)
        ]
        total = jnp.dot(jnp.concatenate(lhs, axis=1), back_mat[...], preferred_element_type=F32)
        total = total.reshape(some, win, 2 * feats)
        for n in range(some):
            r = r0 + n - 1
            inside = in_rows(r) & win_cols
            put_back(sd3, r + 2, jnp.where(inside, total[n] * slope(pre2[r + 3, window, :]), 0.0))
        return carry

    for q in range(3):
        sd3[q, 0] = jnp.zeros((win, 128), BF)
        sd3[q, pairs + 3] = jnp.zeros((win, 128), BF)
    lax.fori_loop(0, (pairs + 2) // some, second_back, 0)

    def pair_grads(src, delta):
        out = {}
        delta = turn(delta)
        for q in range(3):
            g = product(delta, grad_taps(src, q))
            out[0, q] = g[:f, 3 * f :] + g[f:, :f]
            out[1, q] = g[:f, :f] + g[f:, f : 2 * f]
            out[2, q] = g[:f, f : 2 * f] + g[f:, 2 * f : 3 * f]
        return out

    whole = pl.ds(0, win)

    def stage(dst, taps):
        for t in range(0, len(taps), 2):
            both = jnp.concatenate(taps[t : t + 2], axis=1)
            dst[:, t // 2] = both.reshape(cols_of, feats // cols_of, 2 * f).astype(BF)

    def chain(sent, got, mid, every, last, out, sems):
        s1, r1, s2, r2, s3, r3 = sems

        def first_copy(k):
            peer = lax.rem(col + k, cols_of)
            return remote(sent.at[peer], got.at[k], s1.at[k], r1.at[k], (row, peer))

        def second_copy(k):
            return remote(mid, every.at[row], s2.at[k], r2.at[k], (lax.rem(row + k, rows_of), col))

        def third_copy(k):
            return remote(last, out.at[col], s3.at[k], r3.at[k], (row, lax.rem(col + k, cols_of)))

        return first_copy, second_copy, third_copy

    a_copies = chain(sas, sar, sam, saa, saf, sa_out, (a1_s, a1_r, a2_s, a2_r, a3_s, a3_r))
    b_copies = chain(sbs, sbr, sbm, sba, sbf, sb_out, (b1_s, b1_r, b2_s, b2_r, b3_s, b3_r))
    blank = jnp.zeros((f, f), F32)
    second_grads = pair_grads(act1, grad_lhs(sd3, 2))
    stage(sas, [second_grads[t // 3, t % 3] for t in range(9)] + [blank])
    for k in range(1, cols_of):
        a_copies[0](k).start()

    def entry_own(e):
        x = ed3[1, pl.ds(1 + e, pairs), 1 - e]
        return jnp.where(mine, x, jnp.zeros_like(x)).reshape(pairs * win, tail)

    own_even, own_odd = turn(entry_own(0)), turn(entry_own(1))
    grads = {}
    for q in range(3):
        taps = grad_taps(act2, q)
        ge, go = product(own_even, taps), product(own_odd, taps)
        grads[0, q] = ge[:, 3 * f :] + go[:, :f]
        grads[1, q] = ge[:, :f] + go[:, f : 2 * f]
        grads[2, q] = ge[:, f : 2 * f] + go[:, 2 * f : 3 * f]
    quarter = group // rows_of
    for t in range(0, 9, 2):
        two = [grads[(t + u) // 3, (t + u) % 3] if t + u < 9 else jnp.zeros((tail, f), F32) for u in range(2)]
        both = jnp.concatenate(two, axis=1).reshape(cols_of, rows_of, quarter, 2 * f)
        for r in range(rows_of):
            egs[r, :, t // 2] = both[:, r].astype(BF)

    def e1_copy(k):
        peer = lax.rem(row + k, rows_of)
        return remote(egs.at[peer], egr.at[k], e1_s.at[k], e1_r.at[k], (peer, col))

    def e2_copy(k):
        peer = lax.rem(col + k, cols_of)
        return remote(egm.at[peer], egq.at[k], e2_s.at[k], e2_r.at[k], (row, peer))

    def e3_copy(k):
        return remote(egn, eg_out.at[row], e3_s.at[k], e3_r.at[k], (lax.rem(row + k, rows_of), col))

    for k in range(1, rows_of):
        e1_copy(k).start()

    def first_back(m, carry):
        r0 = m * some
        out = conv(sd3, r0 + 1, some, whole, bwd2[...])
        for n in range(some):
            r = r0 + n - 1
            inside = in_rows(r) & win_cols
            put_back(fd3, r + 1, jnp.where(inside, out[n] * slope(pre1[r + 3, window, :]), 0.0))
        return carry

    lax.fori_loop(0, (pairs + 2) // some, first_back, 0)
    first_grads = pair_grads(act0, grad_lhs(fd3, 1))

    few = 6 if pairs % 6 == 0 else 2

    def stem_back(m, carry):
        r0 = m * few
        out = conv(fd3, r0 + 1, few, whole, bwd1[...])
        for n in range(few):
            r = r0 + n
            delta = jnp.where(mine, out[n] * slope(pre0[r + 3, window, :]), 0.0)
            td3[r] = jnp.concatenate(
                [shift_down(delta, 0), delta, shift_up(delta, 0)], axis=1).astype(BF)
        return carry

    lax.fori_loop(0, pairs // few, stem_back, 0)
    moments = []
    for v in range(4):
        lhs = jnp.concatenate([stem_lhs(g, v, window) for g in range(1, groups + 1)], axis=0)
        rhs = jnp.concatenate([td3[4 * g + v] for g in range(groups)], axis=0)
        got = outer(lhs, rhs).reshape(8, 16, 6 * feats)
        moments.append(pltpu.roll(got, 16 - 4 * v, 1) if v else got)
    moment = (moments[0] + moments[1] + (moments[2] + moments[3])).reshape(128, 6 * feats)
    total = jnp.zeros((feats, 48), F32)
    for s in range(3):
        for e in range(2):
            part = moment[:, 2 * f * s + f * e : 2 * f * s + f * (e + 1)].astype(BF)
            total = total + lax.dot_general(
                part, onehot[2 * s + e], (((0,), (0,)), ((), ())), preferred_element_type=F32)
    total = jnp.concatenate([total, jnp.zeros((feats, f - 48), F32)], axis=1)
    stage(sbs, [first_grads[t // 3, t % 3] for t in range(9)] + [total])
    for k in range(1, cols_of):
        b_copies[0](k).start()

    def summed(mine_value, got, copy, count):
        acc = mine_value.astype(F32)
        for k in range(1, count):
            copy(k).wait_recv()
            acc = acc + got[k].astype(F32)
        return acc.astype(BF)

    egm[...] = summed(egs[row], egr, e1_copy, rows_of)
    for k in range(1, cols_of):
        e2_copy(k).start()

    for part in range(2):
        for k in range(1, chips):
            gather_a(part, k).wait_send()
        for k in range(1, rows_of):
            for z in range(1, chips):
                gather_b(part, k, z).wait_send()
        for z in range(chips):
            gather_c(part, z).wait_send()
    for k in range(1, cols_of):
        pix_copy(k).wait_send()
        up_copy(k).wait_send()
    for side, there in sides:

        @pl.when(there)
        def _():
            for k in range(cols_of):
                pix_rim(side, k).wait_send()
                up_rim(side, k).wait_send()

    for k in range(1, rows_of):
        fg_copy(k).wait()

    def final_sum(t, carry):
        at = pl.ds(t * group, group)
        acc = fgbuf[0, at].astype(F32)
        for r in range(1, rows_of):
            acc = acc + fgbuf[r, at].astype(F32)
        facc[at] = acc
        return carry

    lax.fori_loop(0, 9, final_sum, 0)
    fg_store = pltpu.make_async_copy(facc, fg_out, out_sem)
    fg_store.start()

    for k in range(1, cols_of):
        a_copies[0](k).wait_send()
        b_copies[0](k).wait_send()
    for k in range(1, rows_of):
        e1_copy(k).wait_send()
    for (one_copy, two_copy, _), sent, got, mid, every in (
        (a_copies, sas, sar, sam, saa), (b_copies, sbs, sbr, sbm, sba)):
        value = summed(sent[col], got, one_copy, cols_of)
        mid[...] = value
        every[row] = value
        for k in range(1, rows_of):
            two_copy(k).start()
    value = summed(egm[col], egq, e2_copy, cols_of)
    egn[...] = value
    eg_out[row] = value
    for k in range(1, rows_of):
        e3_copy(k).start()
    for (_, two_copy, three_copy), every, last, out in (
        (a_copies, saa, saf, sa_out), (b_copies, sba, sbf, sb_out)):
        for k in range(1, rows_of):
            two_copy(k).wait_recv()
        acc = every[0].astype(F32)
        for r in range(1, rows_of):
            acc = acc + every[r].astype(F32)
        value = acc.astype(BF)
        last[...] = value
        out[col] = value
        for k in range(1, cols_of):
            three_copy(k).start()

    fg_store.wait()
    for k in range(1, cols_of):
        e2_copy(k).wait_send()
    for k in range(1, rows_of):
        a_copies[1](k).wait_send()
        b_copies[1](k).wait_send()
        e3_copy(k).wait()
    for k in range(1, cols_of):
        a_copies[2](k).wait()
        b_copies[2](k).wait()


def step(pix, stem, first, second, entry, final, up, tile, scale):
    rows_of, cols_of = lax.axis_size("row"), lax.axis_size("col")
    group, rows, cols = up.shape
    feats, tail = first.shape[1], final.shape[2]
    dims = (rows_of, cols_of, rows, cols, tile, group, feats, tail, scale)
    groups, wide, win, pairs, fours = rows // 8, cols + 16, tile + 16, rows // 2, rows // 4
    slots, _ = slab_table(rows_of)
    chips, share, quarter = cols_of // 2, feats // cols_of, group // rows_of
    act = pltpu.VMEM((3, pairs + 8, wide, 128), BF)
    pre = pltpu.VMEM((pairs + 6, wide, 128), F32)
    dma = pltpu.SemaphoreType.DMA
    mat = pltpu.VMEM((12 * feats, 2 * feats), BF)

    def vm(*shape, kind=BF):
        return pltpu.VMEM(shape, kind)

    scratch = [pltpu.VMEM(x.shape, x.dtype) for x in (pix, stem, first, second, entry, final, up)]
    scratch += [dma((7,)), dma(())]
    scratch += [
        vm(groups, tile, 128), vm(groups + 2, cols_of, tile, 128), vm(groups + 2, wide, 128),
        vm(wide, 128, kind=F32), vm(wide, 4 * group, kind=F32), vm(4, 128, 6 * feats), vm(6, 128, 48),
        mat, mat, mat, mat, vm(2, 12 * feats, tail),
        vm(12 * tail, 2 * feats), act, act, act, pre, pre, pre,
        vm(rows + 8, cols, tail), vm(rows + 8, wide, tail, kind=F32),
        vm(rows + 4, 3 * group, cols), vm(9 * group, tail, kind=F32),
        vm(rows, group, cols, kind=F32),
        vm(fours, wide, 4 * group), vm(cols_of, fours + 2, win, 4 * group),
        vm(3, rows + 8, win, tail), vm(3, pairs + 3, 2, win, tail),
        vm(3, pairs + 4, win, 128), vm(3, pairs + 2, win, 128), vm(pairs, win, 384),
        vm(slots, rows_of, tail, tail),
        vm(rows_of, 9 * group, tail),
        vm(rows_of, cols_of, 5, quarter, 128), vm(rows_of, cols_of, 5, quarter, 128), vm(cols_of, 5, quarter, 128),
        vm(cols_of, 5, quarter, 128), vm(5, quarter, 128),
        vm(cols_of, 5, share, 128), vm(cols_of, 5, share, 128), vm(5, share, 128),
        vm(rows_of, 5, share, 128), vm(5, share, 128),
        vm(cols_of, 5, share, 128), vm(cols_of, 5, share, 128), vm(5, share, 128),
        vm(rows_of, 5, share, 128), vm(5, share, 128),
    ]
    for shape in (
        (cols_of,), (2, cols_of), (cols_of,), (2, cols_of), (2, chips), (2, rows_of, chips), (2, chips), (rows_of,),
        (rows_of,), (cols_of,), (rows_of,),
        (cols_of,), (rows_of,), (cols_of,), (cols_of,), (rows_of,), (cols_of,),
    ):
        scratch += [dma(shape), dma(shape)]
    return pl.pallas_call(
        functools.partial(step_kernel, dims),
        out_shape=(
            jax.ShapeDtypeStruct((9 * group, tail), F32),
            jax.ShapeDtypeStruct((rows_of, 5, quarter, 128), BF),
            jax.ShapeDtypeStruct((cols_of, 5, share, 128), BF),
            jax.ShapeDtypeStruct((cols_of, 5, share, 128), BF),
        ),
        in_specs=[ANY] * 7,
        out_specs=(ANY,) + (VMEM,) * 3,
        scratch_shapes=scratch,
        compiler_params=pltpu.CompilerParams(
            collective_id=0, has_side_effects=True, vmem_limit_bytes=58 * 1024 * 1024),
    )(pix, stem, first, second, entry, final, up)


def finish_kernel(fg_ref, eg_ref, sa_ref, sb_ref, stem_out, first_out, second_out, entry_out, final_out):
    group, feats = entry_out.shape[1:]
    for p in range(3):
        for q in range(3):
            at = ((2 - p) * 3 + q) * group
            final_out[3 * p + q] = fg_ref[at : at + group]
    for t in range(5):
        entry = eg_ref[:, t].astype(F32).reshape(group, 2 * feats)
        second = sa_ref[:, t].astype(F32).reshape(feats, 2 * feats)
        first = sb_ref[:, t].astype(F32).reshape(feats, 2 * feats)
        for u in range(2):
            if 2 * t + u < 9:
                half = slice(u * feats, (u + 1) * feats)
                entry_out[2 * t + u] = entry[:, half]
                second_out[2 * t + u] = second[:, half]
                first_out[2 * t + u] = first[:, half]
    stem_out[...] = first.T[feats : feats + stem_out.shape[0]]


def finish(fg, eg, sa, sb, feats):
    group, tail = fg.shape[0] // 9, fg.shape[1]
    return pl.pallas_call(
        finish_kernel,
        out_shape=(
            jax.ShapeDtypeStruct((48, feats), F32),
            jax.ShapeDtypeStruct((9, feats, feats), F32),
            jax.ShapeDtypeStruct((9, feats, feats), F32),
            jax.ShapeDtypeStruct((9, group, feats), F32),
            jax.ShapeDtypeStruct((9, group, tail), F32),
        ),
        in_specs=[VMEM] * 4,
        out_specs=(VMEM,) * 5,
    )(fg, eg, sa, sb)


def per_device(pixels, stem_weight, first_weight, second_weight, entry_weight, final_weight, upstream):
    chans, pix_rows, pix_cols = pixels.shape
    rows, tile = pix_rows // 2, pix_cols // 2
    cols = tile * lax.axis_size("col")
    scale = 1.0 / math.sqrt(rows * lax.axis_size("row") * cols)

    def flat(kernel):
        return kernel.transpose(2, 3, 0, 1).reshape(9, kernel.shape[0], kernel.shape[1])

    stem = stem_weight.transpose(1, 2, 3, 0).reshape(chans * 16, stem_weight.shape[0])
    fg, eg, sa, sb = step(
        pixels.transpose(0, 2, 1), stem, flat(first_weight), flat(second_weight), flat(entry_weight),
        flat(final_weight), upstream, tile, scale)
    stem_grad, first_grad, second_grad, entry_grad, final_grad = finish(fg, eg, sa, sb, stem_weight.shape[0])

    def taps_last(grad):
        return grad.reshape(3, 3, grad.shape[1], grad.shape[2]).transpose(2, 3, 0, 1)

    return (
        stem_grad.reshape(chans, 4, 4, -1).transpose(3, 0, 1, 2),
        taps_last(first_grad),
        taps_last(second_grad),
        taps_last(entry_grad),
        taps_last(final_grad),
    )


def solution(mesh):
    return jax.shard_map(
        per_device,
        mesh=mesh,
        in_specs=(
            P(None, "row", "col"),
            P(),
            P(),
            P(),
            P("col", None, None, None),
            P("col", None, None, None),
            P("col", "row", None),
        ),
        out_specs=(P(), P(), P(), P("col", None, None, None), P("col", None, None, None)),
        check_vma=False,
    )
```

```python
import functools
import math

import jax
import jax.numpy as jnp
from jax import lax
from jax.experimental import pallas as pl
from jax.experimental.pallas import tpu as pltpu
from jax.sharding import PartitionSpec as P

BF = jnp.bfloat16
F32 = jnp.float32
MESH = pl.DeviceIdType.MESH
VMEM = pl.BlockSpec(memory_space=pltpu.VMEM)
ANY = pl.BlockSpec(memory_space=pl.ANY)
EDGE = 4
SLABS = 12


def silu(v):
    h = 0.5 * v
    return h + h * jnp.tanh(h)


def gated(v, half):
    h = half * v
    return h + h * jnp.tanh(h)


def slope(v):
    h = 0.5 * v
    t = jnp.tanh(h)
    return (0.5 + 0.5 * t) * (1.0 + h * (1.0 - t))


def slab_table(rows_of):
    slots = -(-SLABS // rows_of)
    table, free = {}, [(i, r) for i in range(slots) for r in range(rows_of)]
    for n in range(3):
        table["e", n] = free.pop(0)
    free.sort(key=lambda at: (at[1], at[0]))
    for n in range(9):
        table["f", n] = free.pop(0)
    return slots, table


def shift_up(v, axis):
    return pltpu.roll(v, 1, axis)


def shift_down(v, axis):
    return pltpu.roll(v, v.shape[axis] - 1, axis)


def step_kernel(dims, *refs):
    rows_of, cols_of, rows, cols, tile, group, feats, tail, scale = dims
    given = refs[:7]
    fg_out, eg_out, sa_out, sb_out = refs[7:11]
    (pix_ref, stem_ref, first_ref, second_ref, entry_ref, final_ref, up_ref, in_sem, out_sem, own_sem,
     qsend, pixbuf, quads, padf, padz, stem_mat, onehot, fwd1, fwd2, bwd1, bwd2, entry_mat,
     back_mat, act0, act1, act2, pre0, pre1, pre2, entry_act, entry_pre, upq, facc,
     up_rows, zsend, zbuf, up3, ed3, sd3, fd3, td3, wall, fgbuf,
     egs, egr, egm, egq, egn, sas, sar, sam, saa, saf, sbs, sbr, sbm, sba, sbf,
     pix_s, pix_r, prim_s, prim_r, up_s, up_r, urim_s, urim_r,
     wa_s, wa_r, wb_s, wb_r, wc_s, wc_r, fg_s, fg_r,
     e1_s, e1_r, e2_s, e2_r, e3_s, e3_r,
     a1_s, a1_r, a2_s, a2_r, a3_s, a3_r, b1_s, b1_r, b2_s, b2_r, b3_s, b3_r) = refs[11:]

    row, col = lax.axis_index("row"), lax.axis_index("col")
    core, chip = lax.rem(col, 2), lax.div(col, 2)
    chips = cols_of // 2
    groups = rows // 8
    wide, win = cols + 16, tile + 16
    span = rows * rows_of
    pairs = rows // 2
    wfrom = pl.multiple_of(col * tile, tile)
    not_first, not_last = row > 0, row < rows_of - 1
    slots, table = slab_table(rows_of)

    def remote(src, dst, send, recv, peer):
        return pltpu.make_async_remote_copy(
            src_ref=src, dst_ref=dst, send_sem=send, recv_sem=recv,
            device_id=peer, device_id_type=MESH)

    loads = {}
    for n, (src, dst) in enumerate(zip(
        given, (pix_ref, stem_ref, first_ref, second_ref, entry_ref, final_ref, up_ref))):
        loads[n] = pltpu.make_async_copy(src, dst, in_sem.at[n])
    for n in (0, 6, 4, 5, 1, 2, 3):
        loads[n].start()

    barrier = pltpu.get_barrier_semaphore()
    for k in range(1, cols_of):
        pl.semaphore_signal(barrier, inc=1, device_id=(row, lax.rem(col + k, cols_of)), device_id_type=MESH)
    for k in range(1, rows_of):
        pl.semaphore_signal(barrier, inc=1, device_id=(lax.rem(row + k, rows_of), col), device_id_type=MESH)
    for side, there in ((-1, not_first), (1, not_last)):

        @pl.when(there)
        def _():
            for k in range(1, cols_of):
                pl.semaphore_signal(
                    barrier, inc=1, device_id=(row + side, lax.rem(col + k, cols_of)), device_id_type=MESH)

    loads[0].wait()
    for g in range(groups):
        pieces = []
        for a in range(2):
            for c in range(3):
                pieces.append(pix_ref[c, pl.ds(a, tile, stride=2), :][:, 16 * g : 16 * g + 16])
            pieces.append(jnp.zeros((tile, 16), F32))
        qsend[g] = jnp.concatenate(pieces, axis=1).astype(BF)

    loads[4].wait()
    loads[5].wait()
    own = pl.ds(pl.multiple_of(group * col, group), group)
    for t in range(9):
        i, r = table["f", t]
        wall[i, r, own, :] = final_ref[t]
    for n in range(3):
        i, r = table["e", n]
        taps = [entry_ref[4 * n + u] if 4 * n + u < 9 else jnp.zeros((group, feats), BF) for u in range(4)]
        wall[i, r, own, :] = jnp.concatenate(taps, axis=1)

    loads[6].wait()
    up_rows[...] = up_ref[...].astype(F32).transpose(1, 0, 2)
    padz[...] = jnp.zeros_like(padz)
    padf[...] = jnp.zeros_like(padf)

    def spread_up(m, carry):
        x = up_rows[pl.ds(4 * m, 4)].reshape(4 * group, cols)
        padz[EDGE : EDGE + cols, :] = x.T
        zsend[m] = padz[...].astype(BF)
        return carry

    lax.fori_loop(0, rows // 4, spread_up, 0)

    adj = not_first.astype(jnp.int32) + not_last.astype(jnp.int32)
    pl.semaphore_wait(barrier, (cols_of - 1) * (1 + adj) + rows_of - 1)

    sides = ((-1, not_first), (1, not_last))

    def pix_copy(k):
        return remote(qsend, pixbuf.at[pl.ds(1, groups), col], pix_s.at[k], pix_r.at[k],
                      (row, lax.rem(col + k, cols_of)))

    def pix_rim(side, k):
        at = 0 if side < 0 else 1
        return remote(qsend.at[0 if side < 0 else groups - 1],
                      pixbuf.at[groups + 1 if side < 0 else 0, col],
                      prim_s.at[at, k], prim_r.at[at, k], (row + side, lax.rem(col + k, cols_of)))

    fours = rows // 4

    def up_window(k):
        peer = lax.rem(col + k, cols_of)
        return peer, pl.ds(pl.multiple_of(peer * tile, tile), tile + 8)

    def up_copy(k):
        peer, window = up_window(k)
        return remote(zsend.at[:, window], zbuf.at[col, pl.ds(1, fours), pl.ds(0, tile + 8)],
                      up_s.at[k], up_r.at[k], (row, peer))

    def up_rim(side, k):
        at = 0 if side < 0 else 1
        peer, window = up_window(k)
        return remote(zsend.at[0 if side < 0 else fours - 1, window],
                      zbuf.at[col, fours + 1 if side < 0 else 0, pl.ds(0, tile + 8)],
                      urim_s.at[at, k], urim_r.at[at, k], (row + side, peer))

    def shard(z, c):
        return pl.ds(pl.multiple_of(group * (2 * z + c), group), group)

    def gather_a(part, k):
        at = wall.at[0, row, shard(chip, core)] if part == 0 else wall.at[pl.ds(1, slots - 1), row, shard(chip, core)]
        return remote(at, at, wa_s.at[part, k], wa_r.at[part, k],
                      (row, 2 * lax.rem(chip + k, chips) + core))

    def gather_b(part, k, z):
        here = shard(lax.rem(chip + z, chips), core)
        at = wall.at[0, row, here] if part == 0 else wall.at[pl.ds(1, slots - 1), row, here]
        return remote(at, at, wb_s.at[part, k, z], wb_r.at[part, k, z], (lax.rem(row + k, rows_of), col))

    def gather_c(part, z):
        here = shard(z, core)
        at = wall.at[0, :, here] if part == 0 else wall.at[pl.ds(1, slots - 1), :, here]
        return remote(at, at, wc_s.at[part, z], wc_r.at[part, z], (row, 2 * chip + 1 - core))

    for k in range(1, cols_of):
        pix_copy(k).start()
    for side, there in sides:

        @pl.when(there)
        def _():
            for k in range(cols_of):
                pix_rim(side, k).start()

    for part in range(2):
        for k in range(1, chips):
            gather_a(part, k).start()
    pixbuf[pl.ds(1, groups), col] = qsend[...]
    zbuf[:, :, tile + 8 :, :] = jnp.zeros((cols_of, fours + 2, win - tile - 8, 4 * group), BF)
    zbuf[col, pl.ds(1, fours), 0 : tile + 8] = zsend[:, pl.ds(wfrom, tile + 8)]

    @pl.when(row == 0)
    def _():
        pixbuf[0] = jnp.zeros(pixbuf.shape[1:], BF)
        zbuf[:, 0] = jnp.zeros((cols_of,) + zbuf.shape[2:], BF)

    @pl.when(row == rows_of - 1)
    def _():
        pixbuf[groups + 1] = jnp.zeros(pixbuf.shape[1:], BF)
        zbuf[:, fours + 1] = jnp.zeros((cols_of,) + zbuf.shape[2:], BF)

    for n in (1, 2, 3):
        loads[n].wait()
    spot = lax.broadcasted_iota(jnp.int32, (128, 48), 0)
    want = lax.broadcasted_iota(jnp.int32, (128, 48), 1)
    la, lc, lr, lb = spot // 64, (spot // 16) % 4, (spot // 4) % 4, spot % 4
    d = (lr + 1) % 4 - 1
    base_mat = []
    for s in range(3):
        q = 2 * (s - 1) + la + 1
        for e in range(2):
            p = 4 * d + lb - 2 * e + 1
            fits = (lc < 3) & (p >= 0) & (p < 4) & (q >= 0) & (q < 4)
            hot = (fits & (want == lc * 16 + p * 4 + q)).astype(F32).astype(BF)
            onehot[2 * s + e] = hot
            base_mat.append(jnp.dot(hot, stem_ref[...], preferred_element_type=F32))
    for s in range(3):
        pair = jnp.concatenate(base_mat[2 * s : 2 * s + 2], axis=1).reshape(8, 16, 2 * feats)
        for v in range(4):
            turned = pltpu.roll(pair, 4 * v, 1) if v else pair
            stem_mat[v, :, 2 * feats * s : 2 * feats * (s + 1)] = turned.reshape(128, 2 * feats).astype(BF)

    zero = jnp.zeros((feats, feats), F32)
    for w_ref, fwd, bwd in ((first_ref, fwd1, bwd1), (second_ref, fwd2, bwd2)):
        for q in range(3):
            w = [w_ref[3 * p + q].astype(F32) for p in range(3)]
            even = jnp.concatenate([w[1], w[2], zero, w[0]], axis=1)
            odd = jnp.concatenate([w[0], w[1], w[2], zero], axis=1)
            both = jnp.concatenate([even, odd], axis=0)
            fwd[4 * feats * q : 4 * feats * (q + 1)] = both.T.astype(BF)
            lines = [[w[1], w[2]], [w[0], w[1]], [zero, w[0]], [w[2], zero]]
            back = jnp.concatenate([jnp.concatenate(line, axis=1) for line in lines], axis=0)
            bwd[4 * feats * q : 4 * feats * (q + 1)] = back.astype(BF)

    for at in (act0, act1, act2):
        for q in range(3):
            at[q, 0] = jnp.zeros((wide, 128), BF)
            at[q, pairs + 7] = jnp.zeros((wide, 128), BF)

    for k in range(1, cols_of):
        pix_copy(k).wait_recv()
    for side, there in sides:
        other = not_last if side < 0 else not_first

        @pl.when(other)
        def _():
            for k in range(cols_of):
                pix_rim(side, k).wait_recv()

    for g in range(groups + 2):
        padf[EDGE : EDGE + cols, :] = pixbuf[g].reshape(cols, 128).astype(F32)
        quads[g] = padf[...].astype(BF)

    for k in range(1, chips):
        gather_a(0, k).wait_recv()
    for k in range(1, rows_of):
        for z in range(1, chips):
            gather_b(0, k, z).start()
    for k in range(1, cols_of):
        up_copy(k).start()
    for side, there in sides:

        @pl.when(there)
        def _():
            for k in range(cols_of):
                up_rim(side, k).start()

    lane = lax.broadcasted_iota(jnp.int32, (1, 128), 1)
    upper = (lane >= feats).astype(jnp.int32)
    sub = lax.broadcasted_iota(jnp.int32, (wide, 1), 0) - EDGE
    in_cols = (sub >= 0) & (sub < cols)
    base = row * rows

    def in_rows(r):
        line = base + 2 * r + upper
        return (line >= 0) & (line < span)

    def half_of(r):
        line = base + 2 * r
        return jnp.where((line >= 0) & (line < span), 0.5, 0.0).astype(F32)

    ends = (sub[:8] >= 0, sub[cols:] < cols)

    def act_of(pre, r):
        value = gated(pre, half_of(r))
        head = jnp.where(ends[0], value[:8], 0.0)
        last = jnp.where(ends[1], value[cols:], 0.0)
        return jnp.concatenate([head, value[8:cols], last], axis=0)

    def put(dst, at, value):
        dst[0, at] = shift_up(value, 0).astype(BF)
        dst[1, at] = value.astype(BF)
        dst[2, at] = shift_down(value, 0).astype(BF)

    def stem_lhs(g, v, window):
        if v == 0:
            return jnp.where(lr_lane == 3, quads[g - 1, window, :], quads[g, window, :])
        if v == 3:
            return jnp.where(lr_lane == 0, quads[g + 1, window, :], quads[g, window, :])
        return quads[g, window, :]

    lr_lane = (lax.broadcasted_iota(jnp.int32, (1, 128), 1) // 4) % 4

    def stem_one(g, v):
        r = 4 * (g - 1) + v
        out = jnp.dot(stem_lhs(g, v, pl.ds(0, wide)), stem_mat[v], preferred_element_type=F32)
        n = 2 * feats
        pre = shift_up(out[:, :n], 0) + out[:, n : 2 * n] + shift_down(out[:, 2 * n :], 0)
        pre0[r + 3] = pre
        put(act0, r + 4, act_of(pre, r))

    for v in (1, 2, 3):
        stem_one(0, v)

    def stem_group(g, carry):
        for v in range(4):
            stem_one(g, v)
        return carry

    lax.fori_loop(1, groups + 1, stem_group, 0)
    for v in (0, 1, 2):
        stem_one(groups + 1, v)

    low = lax.broadcasted_iota(jnp.int32, (1, 1, 128), 2) < feats

    def conv_lhs(src, at, n, window):
        size = window.size
        out = []
        for q in range(3):
            x = src[q, pl.ds(at, n), window, :]
            mix = jnp.where(low, src[q, pl.ds(at + 1, n), window, :], src[q, pl.ds(at - 1, n), window, :])
            out += [x.reshape(n * size, 128), mix.reshape(n * size, 128)]
        return out

    everything = pl.ds(0, wide)

    def conv(src, at, n, window, mat):
        parts = conv_lhs(src, at, n, window)
        lhs = jnp.concatenate(parts, axis=1)
        out = jnp.dot(lhs, mat, preferred_element_type=F32)
        return out.reshape(n, window.size, out.shape[1])

    def forward(src, mat, pre_ref, dst, first, count, lot):
        def one(m, carry):
            r = first + lot * m
            out = conv(src, r + 4, lot, everything, mat[...])
            for n in range(lot):
                pre_ref[r + n + 3] = out[n]
                put(dst, r + n + 4, act_of(out[n], r + n))
            return carry

        lax.fori_loop(0, count // lot, one, 0)

    for k in range(1, chips):
        gather_a(1, k).wait_recv()
    for k in range(1, rows_of):
        for z in range(1, chips):
            gather_b(1, k, z).start()
    forward(act0, fwd1, pre1, act1, -3, pairs + 6, 9)
    for k in range(1, rows_of):
        for z in range(1, chips):
            gather_b(0, k, z).wait_recv()
    for z in range(chips):
        gather_c(0, z).start()
    forward(act1, fwd2, pre2, act2, -2, pairs + 4, 8)

    def spread_final(i, carry):
        x = up_rows[i]
        at = lax.broadcasted_iota(jnp.int32, x.shape, 1)
        left = jnp.where(at == cols - 1, 0.0, shift_down(x, 1))
        right = jnp.where(at == 0, 0.0, shift_up(x, 1))
        upq[i + 2] = jnp.concatenate([left, x, right], axis=0).astype(BF)
        return carry

    for i in (0, 1, rows + 2, rows + 3):
        upq[i] = jnp.zeros(upq.shape[1:], BF)
    lax.fori_loop(0, rows, spread_final, 0)

    for z in range(chips):
        gather_c(0, z).wait_recv()

    def entry_tap(t):
        i, r = table["e", t // 4]
        u = t % 4
        return wall[i, r, :, feats * u : feats * (u + 1)]

    nil = jnp.zeros((tail, feats), BF)
    turned = []
    for t in range(0, 9, 2):
        i, r = table["e", t // 4]
        u = t % 4
        both = wall[i, r, :, feats * u : feats * (u + 2)].astype(F32).T.astype(BF)
        turned += [both[:feats], both[feats:]]
    empty = jnp.zeros((feats, tail), BF)
    for q in range(3):
        t = [turned[3 * p + q] for p in range(3)]
        for e, line in enumerate(([t[1], t[2], empty, t[0]], [t[0], t[1], t[2], empty])):
            for h in range(4):
                at = feats * (4 * q + h)
                entry_mat[e, at : at + feats, :] = line[h]

    def fill_back():
        for q in range(3):
            w = [entry_tap(3 * p + q) for p in range(3)]
            for a, pair in enumerate(([w[2], nil], [w[1], w[2]], [w[0], w[1]], [nil, w[0]])):
                back_mat[tail * (4 * q + a) : tail * (4 * q + a + 1), :] = jnp.concatenate(pair, axis=1)

    def entry_step(m, carry):
        r = 4 * m - 2
        lhs = jnp.concatenate(conv_lhs(act2, r + 4, 4, everything), axis=1)
        for e in range(2):
            out = jnp.dot(lhs, entry_mat[e], preferred_element_type=F32).reshape(4, wide, tail)
            for n in range(4):
                at = 2 * (r + n + 2) + e
                entry_pre[at] = out[n]
                moved = pltpu.roll(gated(out[n], half_of(r + n)), wide - EDGE, 0)[:cols]
                entry_act[at] = moved.astype(BF)
        return carry

    lax.fori_loop(0, (pairs + 4) // 4, entry_step, 0, unroll=1)

    for k in range(1, rows_of):
        for z in range(1, chips):
            gather_b(1, k, z).wait_recv()
    for z in range(chips):
        gather_c(1, z).start()

    facc[...] = jnp.zeros_like(facc)
    three = 9 * group

    def final_step(m, carry):
        one = upq[pl.ds(2 * m, 3)].reshape(three, cols)
        two = upq[pl.ds(2 * m + 1, 3)].reshape(three, cols)
        rhs = entry_act[pl.ds(2 * m + 3, 2)].reshape(2 * cols, tail)
        facc[...] += jnp.dot(jnp.concatenate([one, two], axis=1), rhs, preferred_element_type=F32)
        return carry

    lax.fori_loop(0, rows // 2 + 1, final_step, 0)
    fgbuf[row] = (facc[...] * scale).astype(BF)

    def fg_copy(k):
        return remote(fgbuf.at[row], fgbuf.at[row], fg_s.at[k], fg_r.at[k], (lax.rem(row + k, rows_of), col))

    for k in range(1, rows_of):
        fg_copy(k).start()

    fill_back()

    for k in range(1, cols_of):
        up_copy(k).wait_recv()
    for side, there in sides:
        other = not_last if side < 0 else not_first

        @pl.when(other)
        def _():
            for k in range(cols_of):
                up_rim(side, k).wait_recv()

    def unpack_up(m, carry):
        got = [zbuf[s, m].astype(F32) for s in range(cols_of)]
        for r in range(4):
            x = jnp.concatenate([z[:, group * r : group * (r + 1)] for z in got], axis=1)
            at = 4 * m + r
            up3[0, at] = shift_down(x, 0).astype(BF)
            up3[1, at] = x.astype(BF)
            up3[2, at] = shift_up(x, 0).astype(BF)
        return carry

    lax.fori_loop(0, fours + 2, unpack_up, 0)
    for z in range(chips):
        gather_c(1, z).wait_recv()

    wsub = lax.broadcasted_iota(jnp.int32, (win, 1), 0) - EDGE
    wcol = wsub + wfrom
    win_cols = (wcol >= 0) & (wcol < cols)
    mine = (wsub >= 0) & (wsub < tile)
    window = pl.ds(wfrom, win)

    def put_back(dst, at, value):
        lead = at if isinstance(at, tuple) else (at,)
        dst[(0,) + lead] = shift_down(value, 0).astype(BF)
        dst[(1,) + lead] = value.astype(BF)
        dst[(2,) + lead] = shift_up(value, 0).astype(BF)

    lot = 15 if (rows + 6) % 15 == 0 else 2

    def entry_back(m, carry):
        k0 = m * lot
        total = jnp.zeros((lot * win, tail), F32)
        for p in range(3):
            for q in range(3):
                i, r = table["f", 3 * p + q]
                lhs = up3[q, pl.ds(k0 + 2 - p, lot)].reshape(lot * win, tail)
                total = total + jnp.dot(lhs, wall[i, r], preferred_element_type=F32)
        total = total.reshape(lot, win, tail)
        for n in range(lot):
            k = k0 + n
            line = base + k - 3
            inside = (line >= 0) & (line < span) & win_cols
            delta = jnp.where(inside, total[n] * slope(entry_pre[k + 1, window, :]), 0.0)
            put_back(ed3, (lax.div(k, 2), lax.rem(k, 2)), delta)
        return carry

    lax.fori_loop(0, (rows + 6) // lot, entry_back, 0)

    def grad_lhs(src, at):
        x = src[1, pl.ds(at, pairs)]
        return jnp.where(mine, x, jnp.zeros_like(x)).reshape(pairs * win, 2 * feats)

    def grad_taps(src, q):
        x = src[q, pl.ds(4, pairs), window, :]
        mix = jnp.where(low, src[q, pl.ds(5, pairs), window, :], src[q, pl.ds(3, pairs), window, :])
        return jnp.concatenate([x.reshape(pairs * win, 128), mix.reshape(pairs * win, 128)], axis=1)

    def turn(lhs):
        return lhs.T

    def product(lhs, rhs):
        return jnp.dot(lhs, rhs, preferred_element_type=F32) * scale

    def outer(lhs, rhs):
        return lax.dot_general(lhs, rhs, (((0,), (0,)), ((), ())), preferred_element_type=F32) * scale

    f = feats

    some = 7 if (pairs + 2) % 7 == 0 else 2

    def second_back(m, carry):
        r0 = m * some
        lhs = [
            ed3[q, pl.ds(r0 + a // 2, some), a % 2].reshape(some * win, tail) for q in range(3) for a in range(4)
        ]
        total = jnp.dot(jnp.concatenate(lhs, axis=1), back_mat[...], preferred_element_type=F32)
        total = total.reshape(some, win, 2 * feats)
        for n in range(some):
            r = r0 + n - 1
            inside = in_rows(r) & win_cols
            put_back(sd3, r + 2, jnp.where(inside, total[n] * slope(pre2[r + 3, window, :]), 0.0))
        return carry

    for q in range(3):
        sd3[q, 0] = jnp.zeros((win, 128), BF)
        sd3[q, pairs + 3] = jnp.zeros((win, 128), BF)
    lax.fori_loop(0, (pairs + 2) // some, second_back, 0)

    def pair_grads(src, delta):
        out = {}
        delta = turn(delta)
        for q in range(3):
            g = product(delta, grad_taps(src, q))
            out[0, q] = g[:f, 3 * f :] + g[f:, :f]
            out[1, q] = g[:f, :f] + g[f:, f : 2 * f]
            out[2, q] = g[:f, f : 2 * f] + g[f:, 2 * f : 3 * f]
        return out

    whole = pl.ds(0, win)

    def stage(dst, taps):
        for t in range(0, len(taps), 2):
            both = jnp.concatenate(taps[t : t + 2], axis=1)
            dst[:, t // 2] = both.reshape(cols_of, feats // cols_of, 2 * f).astype(BF)

    def chain(sent, got, mid, every, last, out, sems):
        s1, r1, s2, r2, s3, r3 = sems

        def first_copy(k):
            peer = lax.rem(col + k, cols_of)
            return remote(sent.at[peer], got.at[k], s1.at[k], r1.at[k], (row, peer))

        def second_copy(k):
            return remote(mid, every.at[row], s2.at[k], r2.at[k], (lax.rem(row + k, rows_of), col))

        def third_copy(k):
            return remote(last, out.at[col], s3.at[k], r3.at[k], (row, lax.rem(col + k, cols_of)))

        return first_copy, second_copy, third_copy

    a_copies = chain(sas, sar, sam, saa, saf, sa_out, (a1_s, a1_r, a2_s, a2_r, a3_s, a3_r))
    b_copies = chain(sbs, sbr, sbm, sba, sbf, sb_out, (b1_s, b1_r, b2_s, b2_r, b3_s, b3_r))
    blank = jnp.zeros((f, f), F32)
    second_grads = pair_grads(act1, grad_lhs(sd3, 2))
    stage(sas, [second_grads[t // 3, t % 3] for t in range(9)] + [blank])
    for k in range(1, cols_of):
        a_copies[0](k).start()

    def entry_own(e):
        x = ed3[1, pl.ds(1 + e, pairs), 1 - e]
        return jnp.where(mine, x, jnp.zeros_like(x)).reshape(pairs * win, tail)

    own_even, own_odd = turn(entry_own(0)), turn(entry_own(1))
    grads = {}
    for q in range(3):
        taps = grad_taps(act2, q)
        ge, go = product(own_even, taps), product(own_odd, taps)
        grads[0, q] = ge[:, 3 * f :] + go[:, :f]
        grads[1, q] = ge[:, :f] + go[:, f : 2 * f]
        grads[2, q] = ge[:, f : 2 * f] + go[:, 2 * f : 3 * f]
    quarter = group // rows_of
    for t in range(0, 9, 2):
        two = [grads[(t + u) // 3, (t + u) % 3] if t + u < 9 else jnp.zeros((tail, f), F32) for u in range(2)]
        both = jnp.concatenate(two, axis=1).reshape(cols_of, rows_of, quarter, 2 * f)
        for r in range(rows_of):
            egs[r, :, t // 2] = both[:, r].astype(BF)

    def e1_copy(k):
        peer = lax.rem(row + k, rows_of)
        return remote(egs.at[peer], egr.at[k], e1_s.at[k], e1_r.at[k], (peer, col))

    def e2_copy(k):
        peer = lax.rem(col + k, cols_of)
        return remote(egm.at[peer], egq.at[k], e2_s.at[k], e2_r.at[k], (row, peer))

    def e3_copy(k):
        return remote(egn, eg_out.at[row], e3_s.at[k], e3_r.at[k], (lax.rem(row + k, rows_of), col))

    for k in range(1, rows_of):
        e1_copy(k).start()

    def first_back(m, carry):
        r0 = m * some
        out = conv(sd3, r0 + 1, some, whole, bwd2[...])
        for n in range(some):
            r = r0 + n - 1
            inside = in_rows(r) & win_cols
            put_back(fd3, r + 1, jnp.where(inside, out[n] * slope(pre1[r + 3, window, :]), 0.0))
        return carry

    lax.fori_loop(0, (pairs + 2) // some, first_back, 0)
    first_grads = pair_grads(act0, grad_lhs(fd3, 1))

    few = 6 if pairs % 6 == 0 else 2

    def stem_back(m, carry):
        r0 = m * few
        out = conv(fd3, r0 + 1, few, whole, bwd1[...])
        for n in range(few):
            r = r0 + n
            delta = jnp.where(mine, out[n] * slope(pre0[r + 3, window, :]), 0.0)
            td3[r] = jnp.concatenate(
                [shift_down(delta, 0), delta, shift_up(delta, 0)], axis=1).astype(BF)
        return carry

    lax.fori_loop(0, pairs // few, stem_back, 0)
    moments = []
    for v in range(4):
        lhs = jnp.concatenate([stem_lhs(g, v, window) for g in range(1, groups + 1)], axis=0)
        rhs = jnp.concatenate([td3[4 * g + v] for g in range(groups)], axis=0)
        got = outer(lhs, rhs).reshape(8, 16, 6 * feats)
        moments.append(pltpu.roll(got, 16 - 4 * v, 1) if v else got)
    moment = (moments[0] + moments[1] + (moments[2] + moments[3])).reshape(128, 6 * feats)
    total = jnp.zeros((feats, 48), F32)
    for s in range(3):
        for e in range(2):
            part = moment[:, 2 * f * s + f * e : 2 * f * s + f * (e + 1)].astype(BF)
            total = total + lax.dot_general(
                part, onehot[2 * s + e], (((0,), (0,)), ((), ())), preferred_element_type=F32)
    total = jnp.concatenate([total, jnp.zeros((feats, f - 48), F32)], axis=1)
    stage(sbs, [first_grads[t // 3, t % 3] for t in range(9)] + [total])
    for k in range(1, cols_of):
        b_copies[0](k).start()

    def summed(mine_value, got, copy, count):
        acc = mine_value.astype(F32)
        for k in range(1, count):
            copy(k).wait_recv()
            acc = acc + got[k].astype(F32)
        return acc.astype(BF)

    egm[...] = summed(egs[row], egr, e1_copy, rows_of)
    for k in range(1, cols_of):
        e2_copy(k).start()

    for part in range(2):
        for k in range(1, chips):
            gather_a(part, k).wait_send()
        for k in range(1, rows_of):
            for z in range(1, chips):
                gather_b(part, k, z).wait_send()
        for z in range(chips):
            gather_c(part, z).wait_send()
    for k in range(1, cols_of):
        pix_copy(k).wait_send()
        up_copy(k).wait_send()
    for side, there in sides:

        @pl.when(there)
        def _():
            for k in range(cols_of):
                pix_rim(side, k).wait_send()
                up_rim(side, k).wait_send()

    for k in range(1, rows_of):
        fg_copy(k).wait()

    def final_sum(t, carry):
        at = pl.ds(t * group, group)
        acc = fgbuf[0, at].astype(F32)
        for r in range(1, rows_of):
            acc = acc + fgbuf[r, at].astype(F32)
        facc[at] = acc
        return carry

    lax.fori_loop(0, 9, final_sum, 0)
    fg_store = pltpu.make_async_copy(facc, fg_out, out_sem)
    fg_store.start()

    for k in range(1, cols_of):
        a_copies[0](k).wait_send()
        b_copies[0](k).wait_send()
    for k in range(1, rows_of):
        e1_copy(k).wait_send()
    for (one_copy, two_copy, _), sent, got, mid, every in (
        (a_copies, sas, sar, sam, saa), (b_copies, sbs, sbr, sbm, sba)):
        value = summed(sent[col], got, one_copy, cols_of)
        mid[...] = value
        every[row] = value
        for k in range(1, rows_of):
            two_copy(k).start()
    value = summed(egm[col], egq, e2_copy, cols_of)
    egn[...] = value
    kept = [pltpu.make_async_copy(egn, eg_out.at[row], own_sem.at[0])]
    kept[0].start()
    for k in range(1, rows_of):
        e3_copy(k).start()
    for (_, two_copy, three_copy), every, last, out in (
        (a_copies, saa, saf, sa_out), (b_copies, sba, sbf, sb_out)):
        for k in range(1, rows_of):
            two_copy(k).wait_recv()
        acc = every[0].astype(F32)
        for r in range(1, rows_of):
            acc = acc + every[r].astype(F32)
        value = acc.astype(BF)
        last[...] = value
        keep = pltpu.make_async_copy(last, out.at[col], own_sem.at[len(kept)])
        keep.start()
        kept.append(keep)
        for k in range(1, cols_of):
            three_copy(k).start()

    fg_store.wait()
    for keep in kept:
        keep.wait()
    for k in range(1, cols_of):
        e2_copy(k).wait_send()
    for k in range(1, rows_of):
        a_copies[1](k).wait_send()
        b_copies[1](k).wait_send()
        e3_copy(k).wait()
    for k in range(1, cols_of):
        a_copies[2](k).wait()
        b_copies[2](k).wait()


def step(pix, stem, first, second, entry, final, up, tile, scale):
    rows_of, cols_of = lax.axis_size("row"), lax.axis_size("col")
    group, rows, cols = up.shape
    feats, tail = first.shape[1], final.shape[2]
    dims = (rows_of, cols_of, rows, cols, tile, group, feats, tail, scale)
    groups, wide, win, pairs, fours = rows // 8, cols + 16, tile + 16, rows // 2, rows // 4
    slots, _ = slab_table(rows_of)
    chips, share, quarter = cols_of // 2, feats // cols_of, group // rows_of
    act = pltpu.VMEM((3, pairs + 8, wide, 128), BF)
    pre = pltpu.VMEM((pairs + 6, wide, 128), F32)
    dma = pltpu.SemaphoreType.DMA
    mat = pltpu.VMEM((12 * feats, 2 * feats), BF)

    def vm(*shape, kind=BF):
        return pltpu.VMEM(shape, kind)

    scratch = [pltpu.VMEM(x.shape, x.dtype) for x in (pix, stem, first, second, entry, final, up)]
    scratch += [dma((7,)), dma(()), dma((3,))]
    scratch += [
        vm(groups, tile, 128), vm(groups + 2, cols_of, tile, 128), vm(groups + 2, wide, 128),
        vm(wide, 128, kind=F32), vm(wide, 4 * group, kind=F32), vm(4, 128, 6 * feats), vm(6, 128, 48),
        mat, mat, mat, mat, vm(2, 12 * feats, tail),
        vm(12 * tail, 2 * feats), act, act, act, pre, pre, pre,
        vm(rows + 8, cols, tail), vm(rows + 8, wide, tail, kind=F32),
        vm(rows + 4, 3 * group, cols), vm(9 * group, tail, kind=F32),
        vm(rows, group, cols, kind=F32),
        vm(fours, wide, 4 * group), vm(cols_of, fours + 2, win, 4 * group),
        vm(3, rows + 8, win, tail), vm(3, pairs + 3, 2, win, tail),
        vm(3, pairs + 4, win, 128), vm(3, pairs + 2, win, 128), vm(pairs, win, 384),
        vm(slots, rows_of, tail, tail),
        vm(rows_of, 9 * group, tail),
        vm(rows_of, cols_of, 5, quarter, 128), vm(rows_of, cols_of, 5, quarter, 128), vm(cols_of, 5, quarter, 128),
        vm(cols_of, 5, quarter, 128), vm(5, quarter, 128),
        vm(cols_of, 5, share, 128), vm(cols_of, 5, share, 128), vm(5, share, 128),
        vm(rows_of, 5, share, 128), vm(5, share, 128),
        vm(cols_of, 5, share, 128), vm(cols_of, 5, share, 128), vm(5, share, 128),
        vm(rows_of, 5, share, 128), vm(5, share, 128),
    ]
    for shape in (
        (cols_of,), (2, cols_of), (cols_of,), (2, cols_of), (2, chips), (2, rows_of, chips), (2, chips), (rows_of,),
        (rows_of,), (cols_of,), (rows_of,),
        (cols_of,), (rows_of,), (cols_of,), (cols_of,), (rows_of,), (cols_of,),
    ):
        scratch += [dma(shape), dma(shape)]
    return pl.pallas_call(
        functools.partial(step_kernel, dims),
        out_shape=(
            jax.ShapeDtypeStruct((9 * group, tail), F32),
            jax.ShapeDtypeStruct((rows_of, 5, quarter, 128), BF),
            jax.ShapeDtypeStruct((cols_of, 5, share, 128), BF),
            jax.ShapeDtypeStruct((cols_of, 5, share, 128), BF),
        ),
        in_specs=[ANY] * 7,
        out_specs=(ANY,) * 4,
        scratch_shapes=scratch,
        compiler_params=pltpu.CompilerParams(
            collective_id=0, has_side_effects=True, vmem_limit_bytes=58 * 1024 * 1024),
    )(pix, stem, first, second, entry, final, up)


def finish_kernel(fg_ref, eg_ref, sa_ref, sb_ref, stem_out, first_out, second_out, entry_out, final_out):
    group, feats = entry_out.shape[1:]
    for p in range(3):
        for q in range(3):
            at = ((2 - p) * 3 + q) * group
            final_out[3 * p + q] = fg_ref[at : at + group]
    for t in range(5):
        entry = eg_ref[:, t].astype(F32).reshape(group, 2 * feats)
        second = sa_ref[:, t].astype(F32).reshape(feats, 2 * feats)
        first = sb_ref[:, t].astype(F32).reshape(feats, 2 * feats)
        for u in range(2):
            if 2 * t + u < 9:
                half = slice(u * feats, (u + 1) * feats)
                entry_out[2 * t + u] = entry[:, half]
                second_out[2 * t + u] = second[:, half]
                first_out[2 * t + u] = first[:, half]
    stem_out[...] = first.T[feats : feats + stem_out.shape[0]]


def finish(fg, eg, sa, sb, feats):
    group, tail = fg.shape[0] // 9, fg.shape[1]
    return pl.pallas_call(
        finish_kernel,
        out_shape=(
            jax.ShapeDtypeStruct((48, feats), F32),
            jax.ShapeDtypeStruct((9, feats, feats), F32),
            jax.ShapeDtypeStruct((9, feats, feats), F32),
            jax.ShapeDtypeStruct((9, group, feats), F32),
            jax.ShapeDtypeStruct((9, group, tail), F32),
        ),
        in_specs=[VMEM] * 4,
        out_specs=(VMEM,) * 5,
    )(fg, eg, sa, sb)


def per_device(pixels, stem_weight, first_weight, second_weight, entry_weight, final_weight, upstream):
    chans, pix_rows, pix_cols = pixels.shape
    rows, tile = pix_rows // 2, pix_cols // 2
    cols = tile * lax.axis_size("col")
    scale = 1.0 / math.sqrt(rows * lax.axis_size("row") * cols)

    def flat(kernel):
        return kernel.transpose(2, 3, 0, 1).reshape(9, kernel.shape[0], kernel.shape[1])

    stem = stem_weight.transpose(1, 2, 3, 0).reshape(chans * 16, stem_weight.shape[0])
    fg, eg, sa, sb = step(
        pixels.transpose(0, 2, 1), stem, flat(first_weight), flat(second_weight), flat(entry_weight),
        flat(final_weight), upstream, tile, scale)
    stem_grad, first_grad, second_grad, entry_grad, final_grad = finish(fg, eg, sa, sb, stem_weight.shape[0])

    def taps_last(grad):
        return grad.reshape(3, 3, grad.shape[1], grad.shape[2]).transpose(2, 3, 0, 1)

    return (
        stem_grad.reshape(chans, 4, 4, -1).transpose(3, 0, 1, 2),
        taps_last(first_grad),
        taps_last(second_grad),
        taps_last(entry_grad),
        taps_last(final_grad),
    )


def solution(mesh):
    return jax.shard_map(
        per_device,
        mesh=mesh,
        in_specs=(
            P(None, "row", "col"),
            P(),
            P(),
            P(),
            P("col", None, None, None),
            P("col", None, None, None),
            P("col", "row", None),
        ),
        out_specs=(P(), P(), P(), P("col", None, None, None), P("col", None, None, None)),
        check_vma=False,
    )
```

```python
import functools
import math

import jax
import jax.numpy as jnp
from jax import lax
from jax.experimental import pallas as pl
from jax.experimental.pallas import tpu as pltpu
from jax.sharding import PartitionSpec as P

BF = jnp.bfloat16
F32 = jnp.float32
MESH = pl.DeviceIdType.MESH
VMEM = pl.BlockSpec(memory_space=pltpu.VMEM)
ANY = pl.BlockSpec(memory_space=pl.ANY)
EDGE = 4
SLABS = 12


def silu(v):
    h = 0.5 * v
    return h + h * jnp.tanh(h)


def gated(v, half):
    h = half * v
    return h + h * jnp.tanh(h)


def slope(v):
    h = 0.5 * v
    t = jnp.tanh(h)
    return (0.5 + 0.5 * t) * (1.0 + h * (1.0 - t))


def slab_table(rows_of):
    slots = -(-SLABS // rows_of)
    table, free = {}, [(i, r) for i in range(slots) for r in range(rows_of)]
    for n in range(3):
        table["e", n] = free.pop(0)
    free.sort(key=lambda at: (at[1], at[0]))
    for n in range(9):
        table["f", n] = free.pop(0)
    return slots, table


def shift_up(v, axis):
    return pltpu.roll(v, 1, axis)


def shift_down(v, axis):
    return pltpu.roll(v, v.shape[axis] - 1, axis)


def step_kernel(dims, *refs):
    rows_of, cols_of, rows, cols, tile, group, feats, tail, scale = dims
    given = refs[:7]
    fg_out, eg_out, sa_out, sb_out = refs[7:11]
    (pix_ref, stem_ref, first_ref, second_ref, entry_ref, final_ref, up_ref, in_sem, out_sem, own_sem,
     qsend, pixbuf, quads, padf, padz, stem_mat, onehot, fwd1, fwd2, bwd1, bwd2, entry_mat,
     back_mat, act0, act1, act2, pre0, pre1, pre2, entry_act, entry_pre, upq, facc,
     up_rows, zsend, zbuf, up3, ed3, sd3, fd3, td3, wall, fgbuf,
     egs, egr, egm, egq, egn, sas, sar, sam, saa, saf, sbs, sbr, sbm, sba, sbf,
     pix_s, pix_r, prim_s, prim_r, up_s, up_r, urim_s, urim_r,
     wa_s, wa_r, wb_s, wb_r, wc_s, wc_r, fg_s, fg_r,
     e1_s, e1_r, e2_s, e2_r, e3_s, e3_r,
     a1_s, a1_r, a2_s, a2_r, a3_s, a3_r, b1_s, b1_r, b2_s, b2_r, b3_s, b3_r) = refs[11:]

    row, col = lax.axis_index("row"), lax.axis_index("col")
    core, chip = lax.rem(col, 2), lax.div(col, 2)
    chips = cols_of // 2
    groups = rows // 8
    wide, win = cols + 16, tile + 16
    span = rows * rows_of
    pairs = rows // 2
    wfrom = pl.multiple_of(col * tile, tile)
    not_first, not_last = row > 0, row < rows_of - 1
    slots, table = slab_table(rows_of)

    def remote(src, dst, send, recv, peer):
        return pltpu.make_async_remote_copy(
            src_ref=src, dst_ref=dst, send_sem=send, recv_sem=recv,
            device_id=peer, device_id_type=MESH)

    loads = {}
    for n, (src, dst) in enumerate(zip(
        given, (pix_ref, stem_ref, first_ref, second_ref, entry_ref, final_ref, up_ref))):
        loads[n] = pltpu.make_async_copy(src, dst, in_sem.at[n])
    for n in (0, 6, 4, 5, 1, 2, 3):
        loads[n].start()

    barrier = pltpu.get_barrier_semaphore()
    for k in range(1, cols_of):
        pl.semaphore_signal(barrier, inc=1, device_id=(row, lax.rem(col + k, cols_of)), device_id_type=MESH)
    for k in range(1, rows_of):
        pl.semaphore_signal(barrier, inc=1, device_id=(lax.rem(row + k, rows_of), col), device_id_type=MESH)
    for side, there in ((-1, not_first), (1, not_last)):

        @pl.when(there)
        def _():
            for k in range(1, cols_of):
                pl.semaphore_signal(
                    barrier, inc=1, device_id=(row + side, lax.rem(col + k, cols_of)), device_id_type=MESH)

    loads[0].wait()
    for g in range(groups):
        pieces = []
        for a in range(2):
            for c in range(3):
                pieces.append(pix_ref[c, pl.ds(a, tile, stride=2), :][:, 16 * g : 16 * g + 16])
            pieces.append(jnp.zeros((tile, 16), F32))
        qsend[g] = jnp.concatenate(pieces, axis=1).astype(BF)

    loads[4].wait()
    loads[5].wait()
    own = pl.ds(pl.multiple_of(group * col, group), group)
    for t in range(9):
        i, r = table["f", t]
        wall[i, r, own, :] = final_ref[t]
    for n in range(3):
        i, r = table["e", n]
        taps = [entry_ref[4 * n + u] if 4 * n + u < 9 else jnp.zeros((group, feats), BF) for u in range(4)]
        wall[i, r, own, :] = jnp.concatenate(taps, axis=1)

    loads[6].wait()
    up_rows[...] = up_ref[...].astype(F32).transpose(1, 0, 2)
    padz[...] = jnp.zeros_like(padz)
    padf[...] = jnp.zeros_like(padf)

    def spread_up(m, carry):
        x = up_rows[pl.ds(4 * m, 4)].reshape(4 * group, cols)
        padz[EDGE : EDGE + cols, :] = x.T
        zsend[m] = padz[...].astype(BF)
        return carry

    lax.fori_loop(0, rows // 4, spread_up, 0)

    adj = not_first.astype(jnp.int32) + not_last.astype(jnp.int32)
    pl.semaphore_wait(barrier, (cols_of - 1) * (1 + adj) + rows_of - 1)

    sides = ((-1, not_first), (1, not_last))

    def pix_copy(k):
        return remote(qsend, pixbuf.at[pl.ds(1, groups), col], pix_s.at[k], pix_r.at[k],
                      (row, lax.rem(col + k, cols_of)))

    def pix_rim(side, k):
        at = 0 if side < 0 else 1
        return remote(qsend.at[0 if side < 0 else groups - 1],
                      pixbuf.at[groups + 1 if side < 0 else 0, col],
                      prim_s.at[at, k], prim_r.at[at, k], (row + side, lax.rem(col + k, cols_of)))

    fours = rows // 4

    def up_window(k):
        peer = lax.rem(col + k, cols_of)
        return peer, pl.ds(pl.multiple_of(peer * tile, tile), tile + 8)

    def up_copy(k):
        peer, window = up_window(k)
        return remote(zsend.at[:, window], zbuf.at[col, pl.ds(1, fours), pl.ds(0, tile + 8)],
                      up_s.at[k], up_r.at[k], (row, peer))

    def up_rim(side, k):
        at = 0 if side < 0 else 1
        peer, window = up_window(k)
        return remote(zsend.at[0 if side < 0 else fours - 1, window],
                      zbuf.at[col, fours + 1 if side < 0 else 0, pl.ds(0, tile + 8)],
                      urim_s.at[at, k], urim_r.at[at, k], (row + side, peer))

    def shard(z, c):
        return pl.ds(pl.multiple_of(group * (2 * z + c), group), group)

    def gather_a(part, k):
        at = wall.at[0, row, shard(chip, core)] if part == 0 else wall.at[pl.ds(1, slots - 1), row, shard(chip, core)]
        return remote(at, at, wa_s.at[part, k], wa_r.at[part, k],
                      (row, 2 * lax.rem(chip + k, chips) + core))

    def gather_b(part, k, z):
        here = shard(lax.rem(chip + z, chips), core)
        at = wall.at[0, row, here] if part == 0 else wall.at[pl.ds(1, slots - 1), row, here]
        return remote(at, at, wb_s.at[part, k, z], wb_r.at[part, k, z], (lax.rem(row + k, rows_of), col))

    def gather_c(part, z):
        here = shard(z, core)
        at = wall.at[0, :, here] if part == 0 else wall.at[pl.ds(1, slots - 1), :, here]
        return remote(at, at, wc_s.at[part, z], wc_r.at[part, z], (row, 2 * chip + 1 - core))

    for k in range(1, cols_of):
        pix_copy(k).start()
    for side, there in sides:

        @pl.when(there)
        def _():
            for k in range(cols_of):
                pix_rim(side, k).start()

    for part in range(2):
        for k in range(1, chips):
            gather_a(part, k).start()
    pixbuf[pl.ds(1, groups), col] = qsend[...]
    zbuf[:, :, tile + 8 :, :] = jnp.zeros((cols_of, fours + 2, win - tile - 8, 4 * group), BF)
    zbuf[col, pl.ds(1, fours), 0 : tile + 8] = zsend[:, pl.ds(wfrom, tile + 8)]

    @pl.when(row == 0)
    def _():
        pixbuf[0] = jnp.zeros(pixbuf.shape[1:], BF)
        zbuf[:, 0] = jnp.zeros((cols_of,) + zbuf.shape[2:], BF)

    @pl.when(row == rows_of - 1)
    def _():
        pixbuf[groups + 1] = jnp.zeros(pixbuf.shape[1:], BF)
        zbuf[:, fours + 1] = jnp.zeros((cols_of,) + zbuf.shape[2:], BF)

    for n in (1, 2, 3):
        loads[n].wait()
    spot = lax.broadcasted_iota(jnp.int32, (128, 48), 0)
    want = lax.broadcasted_iota(jnp.int32, (128, 48), 1)
    la, lc, lr, lb = spot // 64, (spot // 16) % 4, (spot // 4) % 4, spot % 4
    d = (lr + 1) % 4 - 1
    base_mat = []
    for s in range(3):
        q = 2 * (s - 1) + la + 1
        for e in range(2):
            p = 4 * d + lb - 2 * e + 1
            fits = (lc < 3) & (p >= 0) & (p < 4) & (q >= 0) & (q < 4)
            hot = (fits & (want == lc * 16 + p * 4 + q)).astype(F32).astype(BF)
            onehot[2 * s + e] = hot
            base_mat.append(jnp.dot(hot, stem_ref[...], preferred_element_type=F32))
    for s in range(3):
        pair = jnp.concatenate(base_mat[2 * s : 2 * s + 2], axis=1).reshape(8, 16, 2 * feats)
        for v in range(4):
            turned = pltpu.roll(pair, 4 * v, 1) if v else pair
            stem_mat[v, :, 2 * feats * s : 2 * feats * (s + 1)] = turned.reshape(128, 2 * feats).astype(BF)

    zero = jnp.zeros((feats, feats), F32)
    for w_ref, fwd, bwd in ((first_ref, fwd1, bwd1), (second_ref, fwd2, bwd2)):
        for q in range(3):
            w = [w_ref[3 * p + q].astype(F32) for p in range(3)]
            even = jnp.concatenate([w[1], w[2], zero, w[0]], axis=1)
            odd = jnp.concatenate([w[0], w[1], w[2], zero], axis=1)
            both = jnp.concatenate([even, odd], axis=0)
            fwd[4 * feats * q : 4 * feats * (q + 1)] = both.T.astype(BF)
            lines = [[w[1], w[2]], [w[0], w[1]], [zero, w[0]], [w[2], zero]]
            back = jnp.concatenate([jnp.concatenate(line, axis=1) for line in lines], axis=0)
            bwd[4 * feats * q : 4 * feats * (q + 1)] = back.astype(BF)

    for at in (act0, act1, act2):
        for q in range(3):
            at[q, 0] = jnp.zeros((wide, 128), BF)
            at[q, pairs + 7] = jnp.zeros((wide, 128), BF)
    for q in range(3):
        act2[q, 1] = jnp.zeros((wide, 128), BF)
        act2[q, pairs + 6] = jnp.zeros((wide, 128), BF)

    for k in range(1, cols_of):
        pix_copy(k).wait_recv()
    for side, there in sides:
        other = not_last if side < 0 else not_first

        @pl.when(other)
        def _():
            for k in range(cols_of):
                pix_rim(side, k).wait_recv()

    for g in range(groups + 2):
        padf[EDGE : EDGE + cols, :] = pixbuf[g].reshape(cols, 128).astype(F32)
        quads[g] = padf[...].astype(BF)

    for k in range(1, chips):
        gather_a(0, k).wait_recv()
    for k in range(1, rows_of):
        for z in range(1, chips):
            gather_b(0, k, z).start()
    for k in range(1, cols_of):
        up_copy(k).start()
    for side, there in sides:

        @pl.when(there)
        def _():
            for k in range(cols_of):
                up_rim(side, k).start()

    lane = lax.broadcasted_iota(jnp.int32, (1, 128), 1)
    upper = (lane >= feats).astype(jnp.int32)
    sub = lax.broadcasted_iota(jnp.int32, (wide, 1), 0) - EDGE
    in_cols = (sub >= 0) & (sub < cols)
    base = row * rows

    def in_rows(r):
        line = base + 2 * r + upper
        return (line >= 0) & (line < span)

    def half_of(r):
        line = base + 2 * r
        return jnp.where((line >= 0) & (line < span), 0.5, 0.0).astype(F32)

    ends = (sub[:8] >= 0, sub[cols:] < cols)

    def act_of(pre, r):
        value = gated(pre, half_of(r))
        head = jnp.where(ends[0], value[:8], 0.0)
        last = jnp.where(ends[1], value[cols:], 0.0)
        return jnp.concatenate([head, value[8:cols], last], axis=0)

    def put(dst, at, value):
        dst[0, at] = shift_up(value, 0).astype(BF)
        dst[1, at] = value.astype(BF)
        dst[2, at] = shift_down(value, 0).astype(BF)

    def stem_lhs(g, v, window):
        if v == 0:
            return jnp.where(lr_lane == 3, quads[g - 1, window, :], quads[g, window, :])
        if v == 3:
            return jnp.where(lr_lane == 0, quads[g + 1, window, :], quads[g, window, :])
        return quads[g, window, :]

    lr_lane = (lax.broadcasted_iota(jnp.int32, (1, 128), 1) // 4) % 4

    def stem_one(g, v):
        r = 4 * (g - 1) + v
        out = jnp.dot(stem_lhs(g, v, pl.ds(0, wide)), stem_mat[v], preferred_element_type=F32)
        n = 2 * feats
        pre = shift_up(out[:, :n], 0) + out[:, n : 2 * n] + shift_down(out[:, 2 * n :], 0)
        pre0[r + 3] = pre
        put(act0, r + 4, act_of(pre, r))

    for v in (1, 2, 3):
        stem_one(0, v)

    def stem_group(g, carry):
        for v in range(4):
            stem_one(g, v)
        return carry

    lax.fori_loop(1, groups + 1, stem_group, 0)
    for v in (0, 1, 2):
        stem_one(groups + 1, v)

    low = lax.broadcasted_iota(jnp.int32, (1, 1, 128), 2) < feats

    def conv_lhs(src, at, n, window):
        size = window.size
        out = []
        for q in range(3):
            x = src[q, pl.ds(at, n), window, :]
            mix = jnp.where(low, src[q, pl.ds(at + 1, n), window, :], src[q, pl.ds(at - 1, n), window, :])
            out += [x.reshape(n * size, 128), mix.reshape(n * size, 128)]
        return out

    everything = pl.ds(0, wide)

    def conv(src, at, n, window, mat):
        parts = conv_lhs(src, at, n, window)
        lhs = jnp.concatenate(parts, axis=1)
        out = jnp.dot(lhs, mat, preferred_element_type=F32)
        return out.reshape(n, window.size, out.shape[1])

    def forward(src, mat, pre_ref, dst, first, count, lot):
        def one(m, carry):
            r = first + lot * m
            out = conv(src, r + 4, lot, everything, mat[...])
            for n in range(lot):
                pre_ref[r + n + 3] = out[n]
                put(dst, r + n + 4, act_of(out[n], r + n))
            return carry

        lax.fori_loop(0, count // lot, one, 0)

    for k in range(1, chips):
        gather_a(1, k).wait_recv()
    for k in range(1, rows_of):
        for z in range(1, chips):
            gather_b(1, k, z).start()
    forward(act0, fwd1, pre1, act1, -3, pairs + 6, 9)
    for k in range(1, rows_of):
        for z in range(1, chips):
            gather_b(0, k, z).wait_recv()
    for z in range(chips):
        gather_c(0, z).start()
    forward(act1, fwd2, pre2, act2, -2, pairs + 4, 8)

    def spread_final(i, carry):
        x = up_rows[i]
        at = lax.broadcasted_iota(jnp.int32, x.shape, 1)
        left = jnp.where(at == cols - 1, 0.0, shift_down(x, 1))
        right = jnp.where(at == 0, 0.0, shift_up(x, 1))
        upq[i + 2] = jnp.concatenate([left, x, right], axis=0).astype(BF)
        return carry

    for i in (0, 1, rows + 2, rows + 3):
        upq[i] = jnp.zeros(upq.shape[1:], BF)
    lax.fori_loop(0, rows, spread_final, 0)

    for z in range(chips):
        gather_c(0, z).wait_recv()

    def entry_tap(t):
        i, r = table["e", t // 4]
        u = t % 4
        return wall[i, r, :, feats * u : feats * (u + 1)]

    nil = jnp.zeros((tail, feats), BF)
    turned = []
    for t in range(0, 9, 2):
        i, r = table["e", t // 4]
        u = t % 4
        both = wall[i, r, :, feats * u : feats * (u + 2)].astype(F32).T.astype(BF)
        turned += [both[:feats], both[feats:]]
    empty = jnp.zeros((feats, tail), BF)
    for q in range(3):
        t = [turned[3 * p + q] for p in range(3)]
        for e, line in enumerate(([t[1], t[2], empty, t[0]], [t[0], t[1], t[2], empty])):
            for h in range(4):
                at = feats * (4 * q + h)
                entry_mat[e, at : at + feats, :] = line[h]

    def fill_back():
        for q in range(3):
            w = [entry_tap(3 * p + q) for p in range(3)]
            for a, pair in enumerate(([w[2], nil], [w[1], w[2]], [w[0], w[1]], [nil, w[0]])):
                back_mat[tail * (4 * q + a) : tail * (4 * q + a + 1), :] = jnp.concatenate(pair, axis=1)

    def entry_step(m, carry):
        r = 4 * m - 2
        lhs = jnp.concatenate(conv_lhs(act2, r + 4, 4, everything), axis=1)
        for e in range(2):
            out = jnp.dot(lhs, entry_mat[e], preferred_element_type=F32).reshape(4, wide, tail)
            for n in range(4):
                at = 2 * (r + n + 2) + e
                entry_pre[at] = out[n]
                moved = pltpu.roll(gated(out[n], half_of(r + n)), wide - EDGE, 0)[:cols]
                entry_act[at] = moved.astype(BF)
        return carry

    lax.fori_loop(0, (pairs + 4) // 4, entry_step, 0, unroll=1)

    for k in range(1, rows_of):
        for z in range(1, chips):
            gather_b(1, k, z).wait_recv()
    for z in range(chips):
        gather_c(1, z).start()

    facc[...] = jnp.zeros_like(facc)
    three = 9 * group

    def final_step(m, carry):
        one = upq[pl.ds(2 * m, 3)].reshape(three, cols)
        two = upq[pl.ds(2 * m + 1, 3)].reshape(three, cols)
        rhs = entry_act[pl.ds(2 * m + 3, 2)].reshape(2 * cols, tail)
        facc[...] += jnp.dot(jnp.concatenate([one, two], axis=1), rhs, preferred_element_type=F32)
        return carry

    lax.fori_loop(0, rows // 2 + 1, final_step, 0)
    fgbuf[row] = (facc[...] * scale).astype(BF)

    def fg_copy(k):
        return remote(fgbuf.at[row], fgbuf.at[row], fg_s.at[k], fg_r.at[k], (lax.rem(row + k, rows_of), col))

    for k in range(1, rows_of):
        fg_copy(k).start()

    fill_back()

    for k in range(1, cols_of):
        up_copy(k).wait_recv()
    for side, there in sides:
        other = not_last if side < 0 else not_first

        @pl.when(other)
        def _():
            for k in range(cols_of):
                up_rim(side, k).wait_recv()

    def unpack_up(m, carry):
        got = [zbuf[s, m].astype(F32) for s in range(cols_of)]
        for r in range(4):
            x = jnp.concatenate([z[:, group * r : group * (r + 1)] for z in got], axis=1)
            at = 4 * m + r
            up3[0, at] = shift_down(x, 0).astype(BF)
            up3[1, at] = x.astype(BF)
            up3[2, at] = shift_up(x, 0).astype(BF)
        return carry

    lax.fori_loop(0, fours + 2, unpack_up, 0)
    for z in range(chips):
        gather_c(1, z).wait_recv()

    wsub = lax.broadcasted_iota(jnp.int32, (win, 1), 0) - EDGE
    wcol = wsub + wfrom
    win_cols = (wcol >= 0) & (wcol < cols)
    mine = (wsub >= 0) & (wsub < tile)
    window = pl.ds(wfrom, win)

    def put_back(dst, at, value):
        lead = at if isinstance(at, tuple) else (at,)
        dst[(0,) + lead] = shift_down(value, 0).astype(BF)
        dst[(1,) + lead] = value.astype(BF)
        dst[(2,) + lead] = shift_up(value, 0).astype(BF)

    lot = 15 if (rows + 6) % 15 == 0 else 2

    def entry_back(m, carry):
        k0 = m * lot
        total = jnp.zeros((lot * win, tail), F32)
        for p in range(3):
            for q in range(3):
                i, r = table["f", 3 * p + q]
                lhs = up3[q, pl.ds(k0 + 2 - p, lot)].reshape(lot * win, tail)
                total = total + jnp.dot(lhs, wall[i, r], preferred_element_type=F32)
        total = total.reshape(lot, win, tail)
        for n in range(lot):
            k = k0 + n
            line = base + k - 3
            inside = (line >= 0) & (line < span) & win_cols
            delta = jnp.where(inside, total[n] * slope(entry_pre[k + 1, window, :]), 0.0)
            put_back(ed3, (lax.div(k, 2), lax.rem(k, 2)), delta)
        return carry

    lax.fori_loop(0, (rows + 6) // lot, entry_back, 0)

    def grad_lhs(src, at):
        x = src[1, pl.ds(at, pairs)]
        return jnp.where(mine, x, jnp.zeros_like(x)).reshape(pairs * win, 2 * feats)

    def grad_taps(src, q):
        x = src[q, pl.ds(4, pairs), window, :]
        mix = jnp.where(low, src[q, pl.ds(5, pairs), window, :], src[q, pl.ds(3, pairs), window, :])
        return jnp.concatenate([x.reshape(pairs * win, 128), mix.reshape(pairs * win, 128)], axis=1)

    def turn(lhs):
        return lhs.T

    def product(lhs, rhs):
        return jnp.dot(lhs, rhs, preferred_element_type=F32) * scale

    def outer(lhs, rhs):
        return lax.dot_general(lhs, rhs, (((0,), (0,)), ((), ())), preferred_element_type=F32) * scale

    f = feats

    some = 7 if (pairs + 2) % 7 == 0 else 2

    def second_back(m, carry):
        r0 = m * some
        lhs = [
            ed3[q, pl.ds(r0 + a // 2, some), a % 2].reshape(some * win, tail) for q in range(3) for a in range(4)
        ]
        total = jnp.dot(jnp.concatenate(lhs, axis=1), back_mat[...], preferred_element_type=F32)
        total = total.reshape(some, win, 2 * feats)
        for n in range(some):
            r = r0 + n - 1
            inside = in_rows(r) & win_cols
            put_back(sd3, r + 2, jnp.where(inside, total[n] * slope(pre2[r + 3, window, :]), 0.0))
        return carry

    for q in range(3):
        sd3[q, 0] = jnp.zeros((win, 128), BF)
        sd3[q, pairs + 3] = jnp.zeros((win, 128), BF)
    lax.fori_loop(0, (pairs + 2) // some, second_back, 0)

    def pair_grads(src, delta):
        out = {}
        delta = turn(delta)
        for q in range(3):
            g = product(delta, grad_taps(src, q))
            out[0, q] = g[:f, 3 * f :] + g[f:, :f]
            out[1, q] = g[:f, :f] + g[f:, f : 2 * f]
            out[2, q] = g[:f, f : 2 * f] + g[f:, 2 * f : 3 * f]
        return out

    whole = pl.ds(0, win)

    def stage(dst, taps):
        for t in range(0, len(taps), 2):
            both = jnp.concatenate(taps[t : t + 2], axis=1)
            dst[:, t // 2] = both.reshape(cols_of, feats // cols_of, 2 * f).astype(BF)

    def chain(sent, got, mid, every, last, out, sems):
        s1, r1, s2, r2, s3, r3 = sems

        def first_copy(k):
            peer = lax.rem(col + k, cols_of)
            return remote(sent.at[peer], got.at[k], s1.at[k], r1.at[k], (row, peer))

        def second_copy(k):
            return remote(mid, every.at[row], s2.at[k], r2.at[k], (lax.rem(row + k, rows_of), col))

        def third_copy(k):
            return remote(last, out.at[col], s3.at[k], r3.at[k], (row, lax.rem(col + k, cols_of)))

        return first_copy, second_copy, third_copy

    a_copies = chain(sas, sar, sam, saa, saf, sa_out, (a1_s, a1_r, a2_s, a2_r, a3_s, a3_r))
    b_copies = chain(sbs, sbr, sbm, sba, sbf, sb_out, (b1_s, b1_r, b2_s, b2_r, b3_s, b3_r))
    blank = jnp.zeros((f, f), F32)
    second_grads = pair_grads(act1, grad_lhs(sd3, 2))
    stage(sas, [second_grads[t // 3, t % 3] for t in range(9)] + [blank])
    for k in range(1, cols_of):
        a_copies[0](k).start()

    def entry_own(e):
        x = ed3[1, pl.ds(1 + e, pairs), 1 - e]
        return jnp.where(mine, x, jnp.zeros_like(x)).reshape(pairs * win, tail)

    own_even, own_odd = turn(entry_own(0)), turn(entry_own(1))
    grads = {}
    for q in range(3):
        taps = grad_taps(act2, q)
        ge, go = product(own_even, taps), product(own_odd, taps)
        grads[0, q] = ge[:, 3 * f :] + go[:, :f]
        grads[1, q] = ge[:, :f] + go[:, f : 2 * f]
        grads[2, q] = ge[:, f : 2 * f] + go[:, 2 * f : 3 * f]
    quarter = group // rows_of
    for t in range(0, 9, 2):
        two = [grads[(t + u) // 3, (t + u) % 3] if t + u < 9 else jnp.zeros((tail, f), F32) for u in range(2)]
        both = jnp.concatenate(two, axis=1).reshape(cols_of, rows_of, quarter, 2 * f)
        for r in range(rows_of):
            egs[r, :, t // 2] = both[:, r].astype(BF)

    def e1_copy(k):
        peer = lax.rem(row + k, rows_of)
        return remote(egs.at[peer], egr.at[k], e1_s.at[k], e1_r.at[k], (peer, col))

    def e2_copy(k):
        peer = lax.rem(col + k, cols_of)
        return remote(egm.at[peer], egq.at[k], e2_s.at[k], e2_r.at[k], (row, peer))

    def e3_copy(k):
        return remote(egn, eg_out.at[row], e3_s.at[k], e3_r.at[k], (lax.rem(row + k, rows_of), col))

    for k in range(1, rows_of):
        e1_copy(k).start()

    def first_back(m, carry):
        r0 = m * some
        out = conv(sd3, r0 + 1, some, whole, bwd2[...])
        for n in range(some):
            r = r0 + n - 1
            inside = in_rows(r) & win_cols
            put_back(fd3, r + 1, jnp.where(inside, out[n] * slope(pre1[r + 3, window, :]), 0.0))
        return carry

    lax.fori_loop(0, (pairs + 2) // some, first_back, 0)
    first_grads = pair_grads(act0, grad_lhs(fd3, 1))

    few = 6 if pairs % 6 == 0 else 2

    def stem_back(m, carry):
        r0 = m * few
        out = conv(fd3, r0 + 1, few, whole, bwd1[...])
        for n in range(few):
            r = r0 + n
            delta = jnp.where(mine, out[n] * slope(pre0[r + 3, window, :]), 0.0)
            td3[r] = jnp.concatenate(
                [shift_down(delta, 0), delta, shift_up(delta, 0)], axis=1).astype(BF)
        return carry

    lax.fori_loop(0, pairs // few, stem_back, 0)
    moments = []
    for v in range(4):
        lhs = jnp.concatenate([stem_lhs(g, v, window) for g in range(1, groups + 1)], axis=0)
        rhs = jnp.concatenate([td3[4 * g + v] for g in range(groups)], axis=0)
        got = outer(lhs, rhs).reshape(8, 16, 6 * feats)
        moments.append(pltpu.roll(got, 16 - 4 * v, 1) if v else got)
    moment = (moments[0] + moments[1] + (moments[2] + moments[3])).reshape(128, 6 * feats)
    total = jnp.zeros((feats, 48), F32)
    for s in range(3):
        for e in range(2):
            part = moment[:, 2 * f * s + f * e : 2 * f * s + f * (e + 1)].astype(BF)
            total = total + lax.dot_general(
                part, onehot[2 * s + e], (((0,), (0,)), ((), ())), preferred_element_type=F32)
    total = jnp.concatenate([total, jnp.zeros((feats, f - 48), F32)], axis=1)
    stage(sbs, [first_grads[t // 3, t % 3] for t in range(9)] + [total])
    for k in range(1, cols_of):
        b_copies[0](k).start()

    def summed(mine_value, got, copy, count):
        acc = mine_value.astype(F32)
        for k in range(1, count):
            copy(k).wait_recv()
            acc = acc + got[k].astype(F32)
        return acc.astype(BF)

    egm[...] = summed(egs[row], egr, e1_copy, rows_of)
    for k in range(1, cols_of):
        e2_copy(k).start()

    for part in range(2):
        for k in range(1, chips):
            gather_a(part, k).wait_send()
        for k in range(1, rows_of):
            for z in range(1, chips):
                gather_b(part, k, z).wait_send()
        for z in range(chips):
            gather_c(part, z).wait_send()
    for k in range(1, cols_of):
        pix_copy(k).wait_send()
        up_copy(k).wait_send()
    for side, there in sides:

        @pl.when(there)
        def _():
            for k in range(cols_of):
                pix_rim(side, k).wait_send()
                up_rim(side, k).wait_send()

    for k in range(1, rows_of):
        fg_copy(k).wait()

    def final_sum(t, carry):
        at = pl.ds(t * group, group)
        acc = fgbuf[0, at].astype(F32)
        for r in range(1, rows_of):
            acc = acc + fgbuf[r, at].astype(F32)
        facc[at] = acc
        return carry

    lax.fori_loop(0, 9, final_sum, 0)
    fg_store = pltpu.make_async_copy(facc, fg_out, out_sem)
    fg_store.start()

    for k in range(1, cols_of):
        a_copies[0](k).wait_send()
        b_copies[0](k).wait_send()
    for k in range(1, rows_of):
        e1_copy(k).wait_send()
    for (one_copy, two_copy, _), sent, got, mid, every in (
        (a_copies, sas, sar, sam, saa), (b_copies, sbs, sbr, sbm, sba)):
        value = summed(sent[col], got, one_copy, cols_of)
        mid[...] = value
        every[row] = value
        for k in range(1, rows_of):
            two_copy(k).start()
    value = summed(egm[col], egq, e2_copy, cols_of)
    egn[...] = value
    kept = [pltpu.make_async_copy(egn, eg_out.at[row], own_sem.at[0])]
    kept[0].start()
    for k in range(1, rows_of):
        e3_copy(k).start()
    for (_, two_copy, three_copy), every, last, out in (
        (a_copies, saa, saf, sa_out), (b_copies, sba, sbf, sb_out)):
        for k in range(1, rows_of):
            two_copy(k).wait_recv()
        acc = every[0].astype(F32)
        for r in range(1, rows_of):
            acc = acc + every[r].astype(F32)
        value = acc.astype(BF)
        last[...] = value
        keep = pltpu.make_async_copy(last, out.at[col], own_sem.at[len(kept)])
        keep.start()
        kept.append(keep)
        for k in range(1, cols_of):
            three_copy(k).start()

    fg_store.wait()
    for keep in kept:
        keep.wait()
    for k in range(1, cols_of):
        e2_copy(k).wait_send()
    for k in range(1, rows_of):
        a_copies[1](k).wait_send()
        b_copies[1](k).wait_send()
        e3_copy(k).wait()
    for k in range(1, cols_of):
        a_copies[2](k).wait()
        b_copies[2](k).wait()


def step(pix, stem, first, second, entry, final, up, tile, scale):
    rows_of, cols_of = lax.axis_size("row"), lax.axis_size("col")
    group, rows, cols = up.shape
    feats, tail = first.shape[1], final.shape[2]
    dims = (rows_of, cols_of, rows, cols, tile, group, feats, tail, scale)
    groups, wide, win, pairs, fours = rows // 8, cols + 16, tile + 16, rows // 2, rows // 4
    slots, _ = slab_table(rows_of)
    chips, share, quarter = cols_of // 2, feats // cols_of, group // rows_of
    act = pltpu.VMEM((3, pairs + 8, wide, 128), BF)
    pre = pltpu.VMEM((pairs + 6, wide, 128), F32)
    dma = pltpu.SemaphoreType.DMA
    mat = pltpu.VMEM((12 * feats, 2 * feats), BF)

    def vm(*shape, kind=BF):
        return pltpu.VMEM(shape, kind)

    scratch = [pltpu.VMEM(x.shape, x.dtype) for x in (pix, stem, first, second, entry, final, up)]
    scratch += [dma((7,)), dma(()), dma((3,))]
    scratch += [
        vm(groups, tile, 128), vm(groups + 2, cols_of, tile, 128), vm(groups + 2, wide, 128),
        vm(wide, 128, kind=F32), vm(wide, 4 * group, kind=F32), vm(4, 128, 6 * feats), vm(6, 128, 48),
        mat, mat, mat, mat, vm(2, 12 * feats, tail),
        vm(12 * tail, 2 * feats), act, act, act, pre, pre, pre,
        vm(rows + 8, cols, tail), vm(rows + 8, wide, tail, kind=F32),
        vm(rows + 4, 3 * group, cols), vm(9 * group, tail, kind=F32),
        vm(rows, group, cols, kind=F32),
        vm(fours, wide, 4 * group), vm(cols_of, fours + 2, win, 4 * group),
        vm(3, rows + 8, win, tail), vm(3, pairs + 3, 2, win, tail),
        vm(3, pairs + 4, win, 128), vm(3, pairs + 2, win, 128), vm(pairs, win, 384),
        vm(slots, rows_of, tail, tail),
        vm(rows_of, 9 * group, tail),
        vm(rows_of, cols_of, 5, quarter, 128), vm(rows_of, cols_of, 5, quarter, 128), vm(cols_of, 5, quarter, 128),
        vm(cols_of, 5, quarter, 128), vm(5, quarter, 128),
        vm(cols_of, 5, share, 128), vm(cols_of, 5, share, 128), vm(5, share, 128),
        vm(rows_of, 5, share, 128), vm(5, share, 128),
        vm(cols_of, 5, share, 128), vm(cols_of, 5, share, 128), vm(5, share, 128),
        vm(rows_of, 5, share, 128), vm(5, share, 128),
    ]
    for shape in (
        (cols_of,), (2, cols_of), (cols_of,), (2, cols_of), (2, chips), (2, rows_of, chips), (2, chips), (rows_of,),
        (rows_of,), (cols_of,), (rows_of,),
        (cols_of,), (rows_of,), (cols_of,), (cols_of,), (rows_of,), (cols_of,),
    ):
        scratch += [dma(shape), dma(shape)]
    return pl.pallas_call(
        functools.partial(step_kernel, dims),
        out_shape=(
            jax.ShapeDtypeStruct((9 * group, tail), F32),
            jax.ShapeDtypeStruct((rows_of, 5, quarter, 128), BF),
            jax.ShapeDtypeStruct((cols_of, 5, share, 128), BF),
            jax.ShapeDtypeStruct((cols_of, 5, share, 128), BF),
        ),
        in_specs=[ANY] * 7,
        out_specs=(ANY,) * 4,
        scratch_shapes=scratch,
        compiler_params=pltpu.CompilerParams(
            collective_id=0, has_side_effects=True, vmem_limit_bytes=58 * 1024 * 1024),
    )(pix, stem, first, second, entry, final, up)


def finish_kernel(fg_ref, eg_ref, sa_ref, sb_ref, stem_out, first_out, second_out, entry_out, final_out):
    group, feats = entry_out.shape[1:]
    for p in range(3):
        for q in range(3):
            at = ((2 - p) * 3 + q) * group
            final_out[3 * p + q] = fg_ref[at : at + group]
    for t in range(5):
        entry = eg_ref[:, t].astype(F32).reshape(group, 2 * feats)
        second = sa_ref[:, t].astype(F32).reshape(feats, 2 * feats)
        first = sb_ref[:, t].astype(F32).reshape(feats, 2 * feats)
        for u in range(2):
            if 2 * t + u < 9:
                half = slice(u * feats, (u + 1) * feats)
                entry_out[2 * t + u] = entry[:, half]
                second_out[2 * t + u] = second[:, half]
                first_out[2 * t + u] = first[:, half]
    stem_out[...] = first.T[feats : feats + stem_out.shape[0]]


def finish(fg, eg, sa, sb, feats):
    group, tail = fg.shape[0] // 9, fg.shape[1]
    return pl.pallas_call(
        finish_kernel,
        out_shape=(
            jax.ShapeDtypeStruct((48, feats), F32),
            jax.ShapeDtypeStruct((9, feats, feats), F32),
            jax.ShapeDtypeStruct((9, feats, feats), F32),
            jax.ShapeDtypeStruct((9, group, feats), F32),
            jax.ShapeDtypeStruct((9, group, tail), F32),
        ),
        in_specs=[VMEM] * 4,
        out_specs=(VMEM,) * 5,
    )(fg, eg, sa, sb)


def per_device(pixels, stem_weight, first_weight, second_weight, entry_weight, final_weight, upstream):
    chans, pix_rows, pix_cols = pixels.shape
    rows, tile = pix_rows // 2, pix_cols // 2
    cols = tile * lax.axis_size("col")
    scale = 1.0 / math.sqrt(rows * lax.axis_size("row") * cols)

    def flat(kernel):
        return kernel.transpose(2, 3, 0, 1).reshape(9, kernel.shape[0], kernel.shape[1])

    stem = stem_weight.transpose(1, 2, 3, 0).reshape(chans * 16, stem_weight.shape[0])
    fg, eg, sa, sb = step(
        pixels.transpose(0, 2, 1), stem, flat(first_weight), flat(second_weight), flat(entry_weight),
        flat(final_weight), upstream, tile, scale)
    stem_grad, first_grad, second_grad, entry_grad, final_grad = finish(fg, eg, sa, sb, stem_weight.shape[0])

    def taps_last(grad):
        return grad.reshape(3, 3, grad.shape[1], grad.shape[2]).transpose(2, 3, 0, 1)

    return (
        stem_grad.reshape(chans, 4, 4, -1).transpose(3, 0, 1, 2),
        taps_last(first_grad),
        taps_last(second_grad),
        taps_last(entry_grad),
        taps_last(final_grad),
    )


def solution(mesh):
    return jax.shard_map(
        per_device,
        mesh=mesh,
        in_specs=(
            P(None, "row", "col"),
            P(),
            P(),
            P(),
            P("col", None, None, None),
            P("col", None, None, None),
            P("col", "row", None),
        ),
        out_specs=(P(), P(), P(), P("col", None, None, None), P("col", None, None, None)),
        check_vma=False,
    )
```
